128 devices in a mesh: section: 8 (over y, core), expert: 16 (over x, z).
Axes of the slice: x: 4, y: 4, z: 4, core: 2. Of those that a mesh axis runs over, the one named last changes fastest.
Arguments:
- section_input: bfloat16 [8, 2048, 2880], P('section', 'expert'), may hold values from -6 to 6
- attention_gain: float32 [8, 2880], P('section'), may hold values from 0.1 to 1.9
- query_key_value_weight: bfloat16 [8, 2880, 2560], P('section', 'expert'), may hold values from -0.109375 to 0.109375
- qkv_bias: float32 [8, 2560], P('section'), may hold values from -3 to 8
- out_weight: bfloat16 [8, 2048, 2880], P('section'), may hold values from -0.125 to 0.125
- out_bias: float32 [8, 2880], P('section'), may hold values from -3 to 3
- attention_sink_logits: float32 [8, 32], P('section'), may hold values from -1 to 250
- expert_gain: float32 [8, 2880], P('section'), may hold values from 0.1 to 1.9
- gate_up_weight: bfloat16 [8, 16, 2880, 1440], P('section', 'expert'), may hold values from -0.109375 to 0.109375
- down_weight: bfloat16 [8, 16, 720, 2880], P('section', 'expert'), may hold values from -0.15625 to 0.15625
- expert_ids: int32 [8, 2048, 4], P('section', 'expert'), may hold values from 0 to 7, all different within a row; in each aligned block of 128 rows (0 to 127, 128 to 255, ..., all dimensions but the last counted through in order) at most 80 rows name the same one
- gate_logits: float32 [8, 2048, 4], P('section', 'expert'), may hold values from -8 to 204
- placement: int32 [8, 8], P('section'), may hold values from 0 to 7, each once within a row
Outputs:
- section_output: bfloat16 [8, 2048, 2880], P('section', 'expert')
The draws below stay inside these ranges and needn't reach their ends.
Inputs may be any that keep to these rules, and one draw needn't show every extreme that they name: `expert_ids`: within each section, among the 128 tokens of one device no expert is named more than 80 times, a bound that some block reaches. `placement`: each row names every expert once.
All inputs are finite; a program needn't handle non-finite values.
Results may differ from the reference program's by a relative error of at most 0.018.
Values may be sent and summed in bfloat16 or wider, within the bound.
A program may use at most 128 MiB of HBM per device.

```python
import math
import jax
import jax.numpy as jnp
import numpy as np
from jax import lax

MODEL_DIM = 2880
HEAD_DIM = 64
QUERY_HEADS = 32
KEY_VALUE_HEADS = 4
WINDOW_TOKENS = 128
HID = 1440
TOP = 4
TOK_DEV = 128
SEQUENCE_TOKENS = 2048
EXPERTS = 8
HID_DEV = 720
CAP = 80
N_SECTION = 8
N_EXPERT = 16


def draw_attention_sink_logits(key, part):
    key_portions = jax.random.split(key, 1)
    tensor_shape = (N_SECTION, QUERY_HEADS)
    gentle = jax.random.uniform(key_portions[0], tensor_shape, jnp.float32, -1.0, 4.0)
    return gentle


def draw_qkv_bias(key, part):
    key_portions = jax.random.split(key, 1)
    tensor_shape = (N_SECTION, (QUERY_HEADS + 2 * KEY_VALUE_HEADS) * HEAD_DIM)
    return 0.5 * jax.random.truncated_normal(key_portions[0], -6.0, 6.0, tensor_shape, jnp.float32)


def draw_gate_logits(key, part):
    key_portions = jax.random.split(key, 1)
    tensor_shape = (N_SECTION, SEQUENCE_TOKENS, TOP)
    return 1.5 * jax.random.truncated_normal(key_portions[0], -5.0, 5.0, tensor_shape, jnp.float32)


def level_of(rng, extent, cuts, smallest, high):
    factor_of, own = 1.0, jax.random.fold_in(rng, 6)
    for axis_at, parts in cuts:
        draws = jnp.exp(jax.random.uniform(jax.random.fold_in(own, axis_at), (parts,), jnp.float32, smallest / len(cuts), high / len(cuts)))
        factor_of = factor_of * jnp.repeat(draws, extent[axis_at] // parts).reshape([-1 if axis == axis_at else 1 for axis in range(len(extent))])
    return factor_of


def routed_block(own_key, own, number, rows, number_of, top, limit, skew):
    ranking = jax.random.permutation(own_key, number_of)
    heavy_load, ordinary = load_shares(number_of, rows * top, limit, skew, True), load_shares(number_of, rows * top, limit, skew, False)
    places = jnp.arange(number_of)

    def named(sizes, rotation):
        used = int((sizes > 0).sum())
        fixed = max(1, used // 4)
        passed = fixed + (places - fixed + rotation * (used - fixed)) % max(1, number_of - fixed)
        return jnp.zeros((number_of,), jnp.int32).at[ranking[jnp.where(places < fixed, places, passed)]].set(jnp.asarray(sizes, jnp.int32))

    sizes = jnp.where(number % 4 == 0, named(heavy_load, number // 4), named(ordinary, number - number // 4 - 1))
    mixed = jax.random.permutation(jax.random.fold_in(own, 3), number_of)
    source_of, taker = mixed[0:number_of // 2 * 2:2], mixed[1:number_of // 2 * 2:2]
    room = jnp.minimum(sizes[source_of] - 1, limit - sizes[taker]) // 2
    room = jnp.where((source_of == ranking[0]) | (taker == ranking[0]) | (sizes[taker] == 0), 0, jnp.maximum(room, 0))
    passed = jax.random.randint(jax.random.fold_in(own, 4), (number_of // 2,), 0, 1 << 20) % (room + 1)
    sizes = sizes.at[source_of].add(-passed).at[taker].add(passed)
    members = jnp.searchsorted(jnp.cumsum(sizes), jnp.arange(rows * top), side="right").astype(jnp.int32)
    table = members.reshape(top, rows).T
    table = table[jax.random.permutation(jax.random.fold_in(own, 1), rows)]
    rotation = jax.random.randint(jax.random.fold_in(own, 2), (rows, 1), 0, top)
    return jnp.take_along_axis(table, (jnp.arange(top)[None, :] + rotation) % top, axis=1)


def load_shares(number_of, total, limit, lean, full):
    loads = [(1 << 20) // math.isqrt(grade ** lean) + 1 for grade in range(1, number_of + 1)]
    largest = limit if full else min(limit, max(-(-total // number_of), total * loads[0] // sum(loads)))
    least = 1 if total - largest >= number_of - 1 else 0
    given, surplus = [largest] + [least] * (number_of - 1), total - largest - least * (number_of - 1)
    while surplus > 0:
        candidates = [i for i in range(1, number_of) if given[i] < largest] or [i for i in range(1, number_of) if given[i] < limit]
        whole, remaining = sum([loads[i] for i in candidates]), surplus
        for i in candidates:
            addition = min(limit - given[i], max(1, remaining * loads[i] // whole), surplus)
            given[i] = given[i] + addition
            surplus = surplus - addition
    return np.array(given)


def centred(stream_key, dims, deviation, reach, shards=(), held_as=jnp.bfloat16):
    gain = level_of(stream_key, dims, shards, -0.22, 0.18) if shards else 1.0
    drawn = jax.random.normal(stream_key, dims, jnp.float32) * deviation * gain
    return jnp.minimum(jnp.maximum(drawn, -reach), reach).astype(held_as)


def setup_inputs(seed: int = 0) -> dict:
    splits = jax.random.split(jax.random.key(seed), 14)
    section_input = centred(splits[0], (N_SECTION, SEQUENCE_TOKENS, MODEL_DIM), 1.0, 6.0, ((0, 8), (1, 16)))
    attention_gain = jnp.clip(1.0 + 0.18 * jax.random.normal(splits[1], (N_SECTION, MODEL_DIM), jnp.float32), 0.1, 1.9)
    query_key_value_weight = centred(splits[2], (N_SECTION, MODEL_DIM, (QUERY_HEADS + 2 * KEY_VALUE_HEADS) * HEAD_DIM), MODEL_DIM ** -0.5, 0.109375, ((0, 8), (1, 16)))
    qkv_bias = draw_qkv_bias(jax.random.fold_in(splits[13], 71), 0)
    out_weight = centred(splits[4], (N_SECTION, QUERY_HEADS * HEAD_DIM, MODEL_DIM), (QUERY_HEADS * HEAD_DIM) ** -0.5, 0.125, ((0, 8),))
    out_bias = centred(splits[5], (N_SECTION, MODEL_DIM), 0.5, 3.0, ((0, 8),), jnp.float32)
    attention_sink_logits = draw_attention_sink_logits(jax.random.fold_in(splits[13], 71), 0)
    expert_gain = jnp.clip(1.0 + 0.18 * jax.random.normal(splits[7], (N_SECTION, MODEL_DIM), jnp.float32), 0.1, 1.9)
    gate_up_weight = centred(splits[8], (N_SECTION, N_EXPERT, MODEL_DIM, 2 * HID_DEV), MODEL_DIM ** -0.5, 0.109375, ((0, 8), (1, 16)))
    down_weight = centred(splits[9], (N_SECTION, N_EXPERT, HID_DEV, MODEL_DIM), HID ** -0.5, 0.15625, ((0, 8), (1, 16)))
    expert_ids_keys = jax.random.split(jax.random.fold_in(splits[10], 1), N_SECTION * SEQUENCE_TOKENS // TOK_DEV)
    expert_ids_turns = jax.random.permutation(jax.random.fold_in(splits[10], 3), N_SECTION * SEQUENCE_TOKENS // TOK_DEV)
    expert_ids = jax.vmap(lambda own, number: routed_block(jax.random.fold_in(splits[10], 2), own, number, TOK_DEV, EXPERTS, TOP, CAP, 2))(expert_ids_keys, expert_ids_turns).reshape((N_SECTION, SEQUENCE_TOKENS, TOP))
    gate_logits = draw_gate_logits(jax.random.fold_in(splits[13], 71), 0)
    placement = jax.vmap(lambda own: jax.random.permutation(own, EXPERTS))(jax.random.split(splits[12], N_SECTION)).reshape((N_SECTION, EXPERTS)).astype(jnp.int32)
    return dict(section_input=section_input, attention_gain=attention_gain, query_key_value_weight=query_key_value_weight, qkv_bias=qkv_bias, out_weight=out_weight, out_bias=out_bias, attention_sink_logits=attention_sink_logits, expert_gain=expert_gain, gate_up_weight=gate_up_weight, down_weight=down_weight, expert_ids=expert_ids, gate_logits=gate_logits, placement=placement)


def normed(vector, gain_row):
    as_float = vector.astype(jnp.float32)
    inverse_rms = lax.rsqrt(lax.optimization_barrier(jnp.mean(as_float * as_float, axis=-1, keepdims=True)) + 1e-05)
    return (as_float * inverse_rms * gain_row).astype(jnp.bfloat16)

def attend(projected_rows, sink_logit_row):
    query_group_width = QUERY_HEADS // KEY_VALUE_HEADS
    count_of_blocks = SEQUENCE_TOKENS // WINDOW_TOKENS
    query_rows = projected_rows[:, :QUERY_HEADS * HEAD_DIM].reshape(count_of_blocks, WINDOW_TOKENS, KEY_VALUE_HEADS, query_group_width, HEAD_DIM).astype(jnp.float32)
    key_columns = projected_rows[:, QUERY_HEADS * HEAD_DIM:QUERY_HEADS * HEAD_DIM + KEY_VALUE_HEADS * HEAD_DIM].reshape(SEQUENCE_TOKENS, KEY_VALUE_HEADS, HEAD_DIM)
    value_columns = projected_rows[:, QUERY_HEADS * HEAD_DIM + KEY_VALUE_HEADS * HEAD_DIM:].reshape(SEQUENCE_TOKENS, KEY_VALUE_HEADS, HEAD_DIM)

    def banded(source_rows):
        padded_rows = jnp.concatenate([jnp.zeros((WINDOW_TOKENS, KEY_VALUE_HEADS, HEAD_DIM), source_rows.dtype), source_rows], 0)
        preceding_rows = padded_rows[:SEQUENCE_TOKENS].reshape(count_of_blocks, WINDOW_TOKENS, KEY_VALUE_HEADS, HEAD_DIM)
        return jnp.concatenate([preceding_rows, source_rows.reshape(count_of_blocks, WINDOW_TOKENS, KEY_VALUE_HEADS, HEAD_DIM)], 1).astype(jnp.float32)
    key_row_slice = banded(key_columns)
    value_row_slice = banded(value_columns)
    scores = jnp.einsum('bikgd,bjkd->bkgij', query_rows, key_row_slice) * 0.125
    query_idx = jnp.arange(WINDOW_TOKENS).astype(jnp.int32)[:, None]
    key_idx = jnp.arange(2 * WINDOW_TOKENS).astype(jnp.int32)[None, :]
    key_start = (jnp.arange(count_of_blocks).astype(jnp.int32) * WINDOW_TOKENS - WINDOW_TOKENS)[:, None, None]
    distance = query_idx - key_idx + WINDOW_TOKENS
    inside = (distance >= 0) & (distance < WINDOW_TOKENS) & (key_start + key_idx >= 0)
    inside = inside[:, None, None, :, :]
    head_sink_logit = sink_logit_row.reshape(KEY_VALUE_HEADS, query_group_width)[None, :, :, None]
    masked = jnp.where(inside, scores, -1e+30)
    peak = jnp.maximum(lax.optimization_barrier(jnp.max(masked, axis=-1)), head_sink_logit)
    numer = jnp.where(inside, jnp.exp(masked - peak[..., None]), 0.0)
    denominator = lax.optimization_barrier(jnp.sum(numer, axis=-1)) + jnp.exp(head_sink_logit - peak)
    attention = (numer / denominator[..., None]).astype(jnp.bfloat16)
    mixed = jnp.einsum('bkgij,bjkd->bikgd', attention.astype(jnp.float32), value_row_slice)
    return mixed.astype(jnp.bfloat16).reshape(SEQUENCE_TOKENS, QUERY_HEADS * HEAD_DIM)

def swiglu(hidden):
    gate_part = hidden[:, :HID_DEV]
    up_part = hidden[:, HID_DEV:]
    return ((up_part + 1.0) * gate_part * jax.nn.sigmoid(1.702 * gate_part)).astype(jnp.bfloat16)

def experts(normed_mid, chosen, logits, holders, gate_up_weight, down_weight):
    flat_ids = chosen.reshape(N_EXPERT, TOK_DEV * TOP)
    one_hot = (flat_ids[:, :, None] == jnp.arange(EXPERTS).astype(jnp.int32)[None, None, :]).astype(jnp.int32)
    slot_of = lax.optimization_barrier(jnp.sum((jnp.cumsum(one_hot, axis=1) - 1) * one_hot, axis=-1))
    block_index = jnp.arange(N_EXPERT).astype(jnp.int32)[:, None]
    where_row = (block_index * CAP + slot_of).reshape(-1).astype(jnp.int32)
    token_of = (block_index * TOK_DEV + jnp.arange(TOK_DEV * TOP).astype(jnp.int32)[None, :] // TOP).reshape(-1).astype(jnp.int32)
    source_rows = jnp.full((EXPERTS, N_EXPERT * CAP), -1, jnp.int32).at[chosen.reshape(-1), where_row].set(token_of)
    matches = (holders[:, None] == jnp.arange(EXPERTS).astype(jnp.int32)[None, :]).astype(jnp.int32)
    holder_of = lax.optimization_barrier(jnp.sum(jnp.arange(EXPERTS).astype(jnp.int32)[:, None] * matches, axis=0)).astype(jnp.int32)

    def one_expert(expert_index):
        row_ids = source_rows[expert_index]
        valid_rows = (row_ids >= 0)[:, None].astype(jnp.bfloat16)
        rows_in = jnp.take(normed_mid, jnp.maximum(row_ids, 0), axis=0) * valid_rows
        pair_slot = holder_of[expert_index]
        accumulated = jnp.zeros((N_EXPERT * CAP, MODEL_DIM), jnp.float32)
        for tile_index in range(2):
            tile_gu = gate_up_weight[2 * pair_slot + tile_index]
            tile_down = down_weight[2 * pair_slot + tile_index]
            tile_act = swiglu(jnp.dot(rows_in, tile_gu, preferred_element_type=jnp.float32))
            tile_part = jnp.dot(tile_act, tile_down, preferred_element_type=jnp.float32).astype(jnp.bfloat16)
            tile_part = lax.optimization_barrier(tile_part)
            accumulated = accumulated + tile_part.astype(jnp.float32)
        return accumulated.astype(jnp.bfloat16)
    results = lax.map(one_expert, jnp.arange(EXPERTS).astype(jnp.int32))
    picked = results[chosen.reshape(-1), where_row].reshape(SEQUENCE_TOKENS, TOP, MODEL_DIM)
    picked = lax.optimization_barrier(picked).astype(jnp.float32)
    gate_weights = jax.nn.softmax(logits, axis=-1)
    return lax.optimization_barrier(jnp.sum(picked * gate_weights[..., None], axis=1))

def reference(section_input, attention_gain, query_key_value_weight, qkv_bias, out_weight, out_bias, attention_sink_logits, expert_gain, gate_up_weight, down_weight, expert_ids, gate_logits, placement):
    collected = []
    for section_index in range(N_SECTION):
        state = section_input[section_index]
        normed_in = normed(state, attention_gain[section_index])
        projected_rows = (jnp.dot(normed_in, query_key_value_weight[section_index], preferred_element_type=jnp.float32) + qkv_bias[section_index]).astype(jnp.bfloat16)
        attended = attend(projected_rows, attention_sink_logits[section_index])
        residual = (state.astype(jnp.float32) + jnp.dot(attended, out_weight[section_index], preferred_element_type=jnp.float32) + out_bias[section_index]).astype(jnp.bfloat16)
        normed_mid = normed(residual, expert_gain[section_index])
        mixture = experts(normed_mid, expert_ids[section_index], gate_logits[section_index], placement[section_index], gate_up_weight[section_index], down_weight[section_index])
        collected.append((residual.astype(jnp.float32) + mixture).astype(jnp.bfloat16))
    return jnp.roll(jnp.stack(collected), 1, axis=0)
```

```python
import functools

import jax
import jax.numpy as jnp
from jax import lax
from jax.experimental import pallas as pl
from jax.experimental.pallas import tpu as pltpu
from jax.sharding import PartitionSpec as P

HEAD_DIM = 64
QUERY_HEADS = 32
KEY_VALUE_HEADS = 4
WINDOW_TOKENS = 128
TOP = 4
SIDE = 4
MESH = pl.DeviceIdType.MESH
F32 = jnp.float32
BF16 = jnp.bfloat16


def from_behind(x, axis, by):
    size = lax.axis_size(axis)
    pairs = [(i, i + by) for i in range(size) if 0 <= i + by < size]
    return lax.ppermute(x, axis, pairs)


def normed(vector, gain_row):
    as_float = vector.astype(jnp.float32)
    inverse_rms = lax.rsqrt(jnp.mean(as_float * as_float, axis=-1, keepdims=True) + 1e-05)
    return (as_float * inverse_rms * gain_row).astype(jnp.bfloat16)


class Links:
    def __init__(self, send, recv):
        self.send, self.recv = send, recv
        self.keys, self.started, self.done = {}, [], set()
        self.made = {}
        self.section = lax.axis_index("section")
        me = lax.axis_index("expert")
        self.x, self.z = me // SIDE, me % SIDE

    def neighbour(self, axis, step):
        if axis == 2:
            return ((self.section + step + 8) % 8, self.x * SIDE + self.z)
        if axis == 0:
            return (self.section, ((self.x + step + SIDE) % SIDE) * SIDE + self.z)
        return (self.section, self.x * SIDE + (self.z + step + SIDE) % SIDE)

    def barrier(self, partners):
        sem = pltpu.get_barrier_semaphore()
        for axis, step in partners:
            pl.semaphore_signal(
                sem, inc=1, device_id=self.neighbour(axis, step), device_id_type=MESH
            )
        pl.semaphore_wait(sem, len(partners))

    def start(self, name, src, dst, axis, step):
        key = self.keys.setdefault(name, len(self.keys))
        copy = pltpu.make_async_remote_copy(
            src_ref=src(),
            dst_ref=dst(),
            send_sem=self.send.at[key],
            recv_sem=self.recv.at[key],
            device_id=self.neighbour(axis, step),
            device_id_type=MESH,
        )
        copy.start()
        self.made[name] = (src, dst, axis, step)

    def remake(self, name):
        src, dst, axis, step = self.made[name]
        key = self.keys[name]
        return pltpu.make_async_remote_copy(
            src_ref=src(),
            dst_ref=dst(),
            send_sem=self.send.at[key],
            recv_sem=self.recv.at[key],
            device_id=self.neighbour(axis, step),
            device_id_type=MESH,
        )

    def need(self, *names):
        for name in names:
            if name not in self.done:
                self.done.add(name)
                self.remake(name).wait_recv()

    def finish(self):
        for name in self.made:
            self.need(name)
            self.remake(name).wait_send()


def add_rows(dst, *parts):
    step = 16

    def body(i, carry):
        rows = pl.ds(pl.multiple_of(i * step, step), step)
        total = parts[0][rows].astype(F32)
        for part in parts[1:]:
            total = total + part[rows].astype(F32)
        dst[rows] = total.astype(dst.dtype)
        return carry

    lax.fori_loop(0, dst.shape[0] // step, body, 0)


def view(ref, *index):
    return lambda: ref.at[index]


def chunks(total, size):
    return [(at, min(size, total - at)) for at in range(0, total, size)]


def expert_kernel(
    slots,
    normed_ref,
    residual_ref,
    meta_ref,
    chosen_ref,
    gate_up_hbm,
    down_hbm,
    out_ref,
    tokens,
    parts,
    meta,
    gate_up,
    down,
    packed,
    hidden,
    act,
    picks,
    half_in,
    full_in,
    half_last,
    full_last,
    local_sem,
    send_sem,
    recv_sem,
):
    half_rows = tokens.shape[2] // 2
    quarter = half_rows // 2
    width = tokens.shape[3]
    inner = act.shape[1]
    net = Links(send_sem, recv_sem)
    load_tokens = pltpu.make_async_copy(normed_ref, tokens.at[0, 0], local_sem.at[0])
    load_gate_up = pltpu.make_async_copy(gate_up_hbm, gate_up, local_sem.at[1])
    load_down = pltpu.make_async_copy(down_hbm, down, local_sem.at[2])
    load_tokens.start()
    meta[0, 0] = meta_ref[...]
    net.barrier([(0, 1), (0, -1), (1, 1), (1, -1), (2, 1), (2, -1)])

    net.start(("mx", 1), view(meta, 0, 0), view(meta, 0, 3), 0, 1)
    net.start(("mx", -1), view(meta, 0, 0), view(meta, 0, 1), 0, -1)
    load_tokens.wait()
    load_gate_up.start()
    load_down.start()

    def block(which, dp, dq, at, size):
        first, second = (dp, dq) if which == 0 else (dq, dp)
        rows = slice(which * half_rows + at, which * half_rows + at + size)
        return lambda: tokens.at[first, second, rows]

    def part(which, dp, dq, at, size):
        first, second = (dp, dq) if which == 0 else (dq, dp)
        rows = slice(which * half_rows + at, which * half_rows + at + size)
        return lambda: parts.at[first, second, rows]

    def own(which, axis, step):
        to = (-step) % SIDE
        place = (to, 0) if axis == which else (0, to)
        name = ("op" if axis == which else "oq", which, step)
        net.start(
            name,
            block(which, 0, 0, 0, half_rows),
            block(which, *place, 0, half_rows),
            axis,
            step,
        )

    for axis in (0, 1):
        for step in (1, -1):
            own(axis, axis, step)
    for axis in (0, 1):
        for step in (1, -1):
            own(1 - axis, axis, step)
    net.need(("mx", 1))
    net.start(("mf", 0), view(meta, 0, 3), view(meta, 0, 2), 0, 1)

    def at_of(step):
        return 0 if step == 1 else quarter

    def on_across(which, dp, dq_axis_step):
        step = dq_axis_step
        net.start(
            ("pq", which, dp, step),
            block(which, dp, 0, 0, half_rows),
            block(which, dp, (-step) % SIDE, 0, half_rows),
            1 - which,
            step,
        )

    def first_hops():
        for step in (1, -1):
            for which in (0, 1):
                dp = (-step) % SIDE
                net.need(("op", which, step))
                net.start(
                    ("fp", which, step),
                    block(which, dp, 0, at_of(step), quarter),
                    block(which, 2, 0, at_of(step), quarter),
                    which,
                    step,
                )
                on_across(which, dp, 1)
                on_across(which, dp, -1)

    def meta_across():
        net.need(("mx", -1), ("mf", 0))
        net.start(("mz", 1), view(meta, 0), view(meta, 3), 1, 1)
        net.start(("mz", -1), view(meta, 0), view(meta, 1), 1, -1)

    def meta_last():
        net.need(("mz", 1), ("mz", -1))
        net.start(("mg", 0), view(meta, 3), view(meta, 2), 1, 1)

    def far_hops():
        for half in (1, -1):
            for which in (0, 1):
                net.need(("fp", which, half))
                for step in (1, -1):
                    net.start(
                        ("pq2", which, half, step),
                        block(which, 2, 0, at_of(half), quarter),
                        block(which, 2, (-step) % SIDE, at_of(half), quarter),
                        1 - which,
                        step,
                    )

    def second_hops(dp):
        for step in (1, -1):
            for which in (0, 1):
                if dp == 0:
                    net.need(("oq", which, step))
                elif dp == 2:
                    net.need(("pq2", which, step, step))
                else:
                    net.need(("pq", which, dp, step))
                net.start(
                    ("fq", which, dp, step),
                    block(which, dp, (-step) % SIDE, at_of(step), quarter),
                    block(which, dp, 2, at_of(step), quarter),
                    1 - which,
                    step,
                )

    def arrived(dx):
        for dz in range(SIDE):
            for which in (0, 1):
                dp, dq = (dx, dz) if which == 0 else (dz, dx)
                step = {1: -1, 3: 1}
                if dq == 0:
                    if dp in step:
                        net.need(("op", which, step[dp]))
                    elif dp == 2:
                        net.need(("fp", which, 1), ("fp", which, -1))
                elif dq == 2:
                    net.need(("fq", which, dp, 1), ("fq", which, dp, -1))
                elif dp == 0:
                    net.need(("oq", which, step[dq]))
                elif dp == 2:
                    net.need(("pq2", which, 1, step[dq]), ("pq2", which, -1, step[dq]))
                else:
                    net.need(("pq", which, dp, step[dq]))

    def stage(at):
        if at == 0:
            meta_across()
            first_hops()
            meta_last()
            far_hops()
            second_hops(0)
            net.need(("mg", 0))
            load_gate_up.wait()
            load_down.wait()
            arrived(0)
        elif at == 1:
            second_hops(1)
            second_hops(3)
            arrived(1)
        elif at == 2:
            second_hops(2)
            arrived(3)
        else:
            arrived(2)

    before = lax.broadcasted_iota(jnp.int32, (128, 128), 0)
    after = lax.broadcasted_iota(jnp.int32, (128, 128), 1)
    earlier = jnp.where(before < after, 1.0, 0.0).astype(BF16)
    slot = lax.broadcasted_iota(jnp.int32, (slots, 128), 0).astype(F32)

    def group(g, carry):
        for at in range(SIDE):
            pl.when(g == at)(functools.partial(stage, at))
        dx = g + g // 2 - 2 * (g // 3)
        scales = []
        for dz in range(SIDE):
            table = meta[dz, dx]
            member = jnp.sum(table[0:8] * chosen_ref[...], axis=0, keepdims=True)
            weight = jnp.sum(table[8:16] * chosen_ref[...], axis=0, keepdims=True)
            wide = jnp.broadcast_to(member, (16, 128)).astype(BF16)
            rank = jnp.dot(wide, earlier, preferred_element_type=F32)[0:1]
            hit = (slot == rank) & (member > 0.5)
            pick = jnp.where(hit, 1.0, 0.0).astype(BF16)
            scales.append(jnp.sum(jnp.where(hit, weight, 0.0), axis=1, keepdims=True))
            picks[dz] = pick
            for at, size in chunks(width, 1024):
                packed[dz * slots : (dz + 1) * slots, at : at + size] = jnp.dot(
                    pick, tokens[dx, dz, :, at : at + size], preferred_element_type=F32
                ).astype(BF16)
        scale = jnp.concatenate(scales, axis=0)
        for at, size in chunks(2 * inner, 512):
            hidden[:, at : at + size] = jnp.dot(
                packed[...], gate_up[:, at : at + size], preferred_element_type=F32
            )
        gate = hidden[:, :inner]
        up = hidden[:, inner:]
        act[...] = ((up + 1.0) * gate * jax.nn.sigmoid(1.702 * gate)).astype(BF16)
        for at, size in chunks(width, 640):
            tile = jnp.dot(act[...], down[:, at : at + size], preferred_element_type=F32)
            tile = (tile * scale).astype(BF16)
            for dz in range(SIDE):
                parts[dx, dz, :, at : at + size] = lax.dot_general(
                    picks[dz],
                    tile[dz * slots : (dz + 1) * slots],
                    (((0,), (0,)), ((), ())),
                    preferred_element_type=F32,
                ).astype(BF16)
        return carry

    lax.fori_loop(0, SIDE, group, 0)

    for dp in (2, 1, 3, 0):
        for which in (0, 1):
            for side, step in ((0, 1), (1, -1)):
                net.start(
                    ("rh", which, dp, step),
                    part(which, dp, 2, at_of(step), quarter),
                    view(half_in, which, dp, side),
                    1 - which,
                    step,
                )

    def relay(dp):
        for which in (0, 1):
            for side, step in ((0, 1), (1, -1)):
                net.need(("rh", which, dp, step))
                there = part(which, dp, step % SIDE, at_of(step), quarter)
                add_rows(there(), there(), half_in.at[which, dp, side])
                net.start(
                    ("rf", which, dp, step),
                    part(which, dp, step % SIDE, 0, half_rows),
                    view(full_in, which, dp, side),
                    1 - which,
                    step,
                )

    def gather_in(dp):
        for which in (0, 1):
            net.need(("rf", which, dp, 1), ("rf", which, dp, -1))
            here = part(which, dp, 0, 0, half_rows)
            add_rows(here(), here(), full_in.at[which, dp, 0], full_in.at[which, dp, 1])

    def last_half(which):
        for side, step in ((0, 1), (1, -1)):
            net.start(
                ("lh", which, step),
                part(which, 2, 0, at_of(step), quarter),
                view(half_last, which, side),
                which,
                step,
            )

    def last_full(which):
        for side, step in ((0, 1), (1, -1)):
            net.need(("lh", which, step))
            there = part(which, step % SIDE, 0, at_of(step), quarter)
            add_rows(there(), there(), half_last.at[which, side])
            net.start(
                ("lf", which, step),
                part(which, step % SIDE, 0, 0, half_rows),
                view(full_last, which, side),
                which,
                step,
            )

    relay(2)
    relay(1)
    gather_in(2)
    last_half(0)
    last_half(1)
    relay(3)
    gather_in(1)
    relay(0)
    gather_in(3)
    last_full(0)
    last_full(1)
    for which in (0, 1):
        net.need(("rf", which, 0, 1), ("rf", which, 0, -1))
        net.need(("lf", which, 1), ("lf", which, -1))
        here = part(which, 0, 0, 0, half_rows)
        rows = slice(which * half_rows, (which + 1) * half_rows)
        add_rows(
            here(),
            here(),
            full_in.at[which, 0, 0],
            full_in.at[which, 0, 1],
            full_last.at[which, 0],
            full_last.at[which, 1],
            residual_ref.at[rows],
        )
        net.start(("out", which), here, view(out_ref, rows), 2, 1)
    net.finish()


def experts_and_pass(normed_mid, residual, meta, chosen, gate_up, down, slots):
    rows, width = normed_mid.shape
    inner = down.shape[0]
    anywhere = pl.BlockSpec(memory_space=pl.ANY)
    vmem = pl.BlockSpec(memory_space=pltpu.VMEM)
    half, quarter = rows // 2, rows // 4
    return pl.pallas_call(
        functools.partial(expert_kernel, slots),
        out_shape=jax.ShapeDtypeStruct((rows, width), BF16),
        in_specs=[anywhere, vmem, vmem, vmem, anywhere, anywhere],
        out_specs=anywhere,
        scratch_shapes=[
            pltpu.VMEM((SIDE, SIDE, rows, width), BF16),
            pltpu.VMEM((SIDE, SIDE, rows, width), BF16),
            pltpu.VMEM((SIDE, SIDE, 16, rows), F32),
            pltpu.VMEM(gate_up.shape, BF16),
            pltpu.VMEM(down.shape, BF16),
            pltpu.VMEM((SIDE * slots, width), BF16),
            pltpu.VMEM((SIDE * slots, 2 * inner), F32),
            pltpu.VMEM((SIDE * slots, inner), BF16),
            pltpu.VMEM((SIDE, slots, rows), BF16),
            pltpu.VMEM((2, SIDE, 2, quarter, width), BF16),
            pltpu.VMEM((2, SIDE, 2, half, width), BF16),
            pltpu.VMEM((2, 2, quarter, width), BF16),
            pltpu.VMEM((2, 2, half, width), BF16),
            pltpu.SemaphoreType.DMA((3,)),
            pltpu.SemaphoreType.DMA((96,)),
            pltpu.SemaphoreType.DMA((96,)),
        ],
        compiler_params=pltpu.CompilerParams(
            collective_id=1, has_side_effects=True, vmem_limit_bytes=62 * 1024 * 1024
        ),
        cost_estimate=pl.CostEstimate(
            flops=16_000_000_000, bytes_accessed=16_000_000, transcendentals=1_000_000
        ),
    )(normed_mid, residual, meta, chosen, gate_up, down)


def routing_tables(ids, logits, holders):
    kinds = lax.broadcasted_iota(jnp.int32, (8, ids.shape[0], TOP), 0)
    equal = (ids[None] == kinds).astype(F32)
    weights = jax.nn.softmax(logits, axis=-1)
    member = jnp.sum(equal, axis=-1)
    weight = jnp.sum(equal * weights[None], axis=-1)
    pair = lax.axis_index("expert") // 2
    mine = jnp.sum(jnp.where(jnp.arange(8) == pair, holders, 0))
    chosen = (lax.broadcasted_iota(jnp.int32, (8, ids.shape[0]), 0) == mine).astype(F32)
    return jnp.concatenate([member, weight], axis=0), chosen


def shards(
    section_input,
    attention_gain,
    query_key_value_weight,
    qkv_bias,
    out_weight,
    out_bias,
    attention_sink_logits,
    expert_gain,
    gate_up_weight,
    down_weight,
    expert_ids,
    gate_logits,
    placement,
):
    count_of_rows = section_input.shape[1]
    experts_count = placement.shape[1]
    slots = 2 * min(count_of_rows // 2, count_of_rows * TOP * 5 // (8 * experts_count))
    offset = lax.axis_index("expert") * count_of_rows
    query_group_width = QUERY_HEADS // KEY_VALUE_HEADS
    state = section_input[0]
    normed_in = normed(state, attention_gain[0])
    projected_rows = (
        jnp.dot(
            normed_in,
            lax.all_gather(query_key_value_weight[0], "expert", axis=0, tiled=True),
            preferred_element_type=jnp.float32,
        )
        + qkv_bias[0]
    ).astype(jnp.bfloat16)
    query_rows = projected_rows[:, : QUERY_HEADS * HEAD_DIM].reshape(
        count_of_rows, KEY_VALUE_HEADS, query_group_width, HEAD_DIM
    )
    key_value = projected_rows[:, QUERY_HEADS * HEAD_DIM :]
    rim_rows = from_behind(key_value, "expert", 1)
    rows_in_window = jnp.concatenate([rim_rows, key_value], 0)
    key_row_slice = rows_in_window[:, : KEY_VALUE_HEADS * HEAD_DIM].reshape(
        WINDOW_TOKENS + count_of_rows, KEY_VALUE_HEADS, HEAD_DIM
    )
    value_row_slice = rows_in_window[:, KEY_VALUE_HEADS * HEAD_DIM :].reshape(
        WINDOW_TOKENS + count_of_rows, KEY_VALUE_HEADS, HEAD_DIM
    )
    scores = (
        jnp.einsum("ikgd,jkd->kgij", query_rows, key_row_slice, preferred_element_type=jnp.float32)
        * 0.125
    )
    query_pos = offset + jnp.arange(count_of_rows, dtype=jnp.int32)
    key_pos = offset - WINDOW_TOKENS + jnp.arange(WINDOW_TOKENS + count_of_rows, dtype=jnp.int32)
    distance = query_pos[:, None] - key_pos[None, :]
    inside = (distance >= 0) & (distance < WINDOW_TOKENS) & (key_pos >= 0)[None, :]
    head_sink_logit = attention_sink_logits[0].reshape(KEY_VALUE_HEADS, query_group_width)[
        :, :, None
    ]
    masked = jnp.where(inside, scores, -1e30)
    peak = jnp.maximum(jnp.max(masked, axis=-1), head_sink_logit)
    numer = jnp.where(inside, jnp.exp(masked - peak[..., None]), 0.0)
    denominator = jnp.sum(numer, axis=-1) + jnp.exp(head_sink_logit - peak)
    attention = (numer / denominator[..., None]).astype(jnp.bfloat16)
    mixed = jnp.einsum(
        "kgij,jkd->ikgd", attention, value_row_slice, preferred_element_type=jnp.float32
    )
    attended = mixed.astype(jnp.bfloat16).reshape(count_of_rows, QUERY_HEADS * HEAD_DIM)
    residual = (
        state.astype(jnp.float32)
        + jnp.dot(attended, out_weight[0], preferred_element_type=jnp.float32)
        + out_bias[0]
    ).astype(jnp.bfloat16)
    normed_mid = normed(residual, expert_gain[0])
    meta, chosen = routing_tables(expert_ids[0], gate_logits[0], placement[0])
    moved = experts_and_pass(
        normed_mid, residual, meta, chosen, gate_up_weight[0, 0], down_weight[0, 0], slots
    )
    return moved[None]


def solution(mesh):
    return jax.shard_map(
        shards,
        mesh=mesh,
        in_specs=(
            P("section", "expert", None),
            P("section", None),
            P("section", "expert", None),
            P("section", None),
            P("section", None, None),
            P("section", None),
            P("section", None),
            P("section", None),
            P("section", "expert", None, None),
            P("section", "expert", None, None),
            P("section", "expert", None),
            P("section", "expert", None),
            P("section", None),
        ),
        out_specs=P("section", "expert", None),
        check_vma=False,
    )
```

```python
import functools

import jax
import jax.numpy as jnp
from jax import lax
from jax.experimental import pallas as pl
from jax.experimental.pallas import tpu as pltpu
from jax.sharding import PartitionSpec as P

HEAD_DIM = 64
QUERY_HEADS = 32
KEY_VALUE_HEADS = 4
WINDOW_TOKENS = 128
TOP = 4
SIDE = 4
MESH = pl.DeviceIdType.MESH
F32 = jnp.float32
BF16 = jnp.bfloat16


def normed(vector, gain_row):
    as_float = vector.astype(jnp.float32)
    inverse_rms = lax.rsqrt(jnp.mean(as_float * as_float, axis=-1, keepdims=True) + 1e-05)
    return (as_float * inverse_rms * gain_row).astype(jnp.bfloat16)


class Links:
    def __init__(self, send, recv):
        self.send, self.recv = send, recv
        self.keys, self.started, self.done = {}, [], set()
        self.made = {}
        self.section = lax.axis_index("section")
        me = lax.axis_index("expert")
        self.x, self.z = me // SIDE, me % SIDE

    def neighbour(self, axis, step):
        if axis == 3:
            return (self.section, (self.x * SIDE + self.z + step + 16) % 16)
        if axis == 2:
            return ((self.section + step + 8) % 8, self.x * SIDE + self.z)
        if axis == 0:
            return (self.section, ((self.x + step + SIDE) % SIDE) * SIDE + self.z)
        return (self.section, self.x * SIDE + (self.z + step + SIDE) % SIDE)

    def barrier(self, partners):
        sem = pltpu.get_barrier_semaphore()
        for axis, step in partners:
            pl.semaphore_signal(
                sem, inc=1, device_id=self.neighbour(axis, step), device_id_type=MESH
            )
        pl.semaphore_wait(sem, len(partners))

    def start(self, name, src, dst, axis, step):
        key = self.keys.setdefault(name, len(self.keys))
        copy = pltpu.make_async_remote_copy(
            src_ref=src(),
            dst_ref=dst(),
            send_sem=self.send.at[key],
            recv_sem=self.recv.at[key],
            device_id=self.neighbour(axis, step),
            device_id_type=MESH,
        )
        copy.start()
        self.made[name] = (src, dst, axis, step)

    def remake(self, name):
        src, dst, axis, step = self.made[name]
        key = self.keys[name]
        return pltpu.make_async_remote_copy(
            src_ref=src(),
            dst_ref=dst(),
            send_sem=self.send.at[key],
            recv_sem=self.recv.at[key],
            device_id=self.neighbour(axis, step),
            device_id_type=MESH,
        )

    def need(self, *names):
        for name in names:
            if name not in self.done:
                self.done.add(name)
                self.remake(name).wait_recv()

    def finish(self):
        for name in self.made:
            self.need(name)
            self.remake(name).wait_send()


def add_rows(dst, *parts):
    step = 16

    def body(i, carry):
        rows = pl.ds(pl.multiple_of(i * step, step), step)
        total = parts[0][rows].astype(F32)
        for part in parts[1:]:
            total = total + part[rows].astype(F32)
        dst[rows] = total.astype(dst.dtype)
        return carry

    lax.fori_loop(0, dst.shape[0] // step, body, 0)


def view(ref, *index):
    return lambda: ref.at[index]


def across(rows, other):
    return lax.dot_general(rows, other, (((1,), (1,)), ((), ())), preferred_element_type=F32)


def along(first, second):
    return lax.dot_general(first, second, (((0,), (0,)), ((), ())), preferred_element_type=F32)


def chunks(total, size):
    return [(at, min(size, total - at)) for at in range(0, total, size)]


def expert_kernel(
    slots,
    normed_ref,
    residual_ref,
    meta_ref,
    chosen_ref,
    gate_up_hbm,
    down_hbm,
    out_ref,
    tokens,
    parts,
    gate_up,
    down,
    packed,
    act,
    picks,
    half_in,
    full_in,
    half_last,
    full_last,
    local_sem,
    send_sem,
    recv_sem,
):
    half_rows = tokens.shape[2] // 2
    quarter = half_rows // 2
    width = tokens.shape[3]
    inner = act.shape[1]
    net = Links(send_sem, recv_sem)
    load_tokens = pltpu.make_async_copy(normed_ref, tokens.at[0, 0], local_sem.at[0])
    load_gate_up = pltpu.make_async_copy(gate_up_hbm, gate_up, local_sem.at[1])
    load_down = pltpu.make_async_copy(down_hbm, down, local_sem.at[2])
    load_tokens.start()
    net.barrier([(0, 1), (0, -1), (1, 1), (1, -1), (2, 1), (2, -1)])

    load_tokens.wait()
    load_gate_up.start()
    load_down.start()

    def block(which, dp, dq, at, size):
        first, second = (dp, dq) if which == 0 else (dq, dp)
        rows = slice(which * half_rows + at, which * half_rows + at + size)
        return lambda: tokens.at[first, second, rows]

    def part(which, dp, dq, at, size):
        first, second = (dp, dq) if which == 0 else (dq, dp)
        rows = slice(which * half_rows + at, which * half_rows + at + size)
        return lambda: parts.at[first, second, rows]

    def own(which, axis, step):
        to = (-step) % SIDE
        place = (to, 0) if axis == which else (0, to)
        name = ("op" if axis == which else "oq", which, step)
        net.start(
            name,
            block(which, 0, 0, 0, half_rows),
            block(which, *place, 0, half_rows),
            axis,
            step,
        )

    for axis in (0, 1):
        for step in (1, -1):
            own(axis, axis, step)
    for axis in (0, 1):
        for step in (1, -1):
            own(1 - axis, axis, step)

    def at_of(step):
        return 0 if step == 1 else quarter

    def on_across(which, dp, dq_axis_step):
        step = dq_axis_step
        net.start(
            ("pq", which, dp, step),
            block(which, dp, 0, 0, half_rows),
            block(which, dp, (-step) % SIDE, 0, half_rows),
            1 - which,
            step,
        )

    def first_hops():
        for step in (1, -1):
            for which in (0, 1):
                dp = (-step) % SIDE
                net.need(("op", which, step))
                net.start(
                    ("fp", which, step),
                    block(which, dp, 0, at_of(step), quarter),
                    block(which, 2, 0, at_of(step), quarter),
                    which,
                    step,
                )
                on_across(which, dp, 1)
                on_across(which, dp, -1)

    def far_hops():
        for half in (1, -1):
            for which in (0, 1):
                net.need(("fp", which, half))
                for step in (1, -1):
                    net.start(
                        ("pq2", which, half, step),
                        block(which, 2, 0, at_of(half), quarter),
                        block(which, 2, (-step) % SIDE, at_of(half), quarter),
                        1 - which,
                        step,
                    )

    def second_hops(dp):
        for step in (1, -1):
            for which in (0, 1):
                if dp == 0:
                    net.need(("oq", which, step))
                elif dp == 2:
                    net.need(("pq2", which, step, step))
                else:
                    net.need(("pq", which, dp, step))
                net.start(
                    ("fq", which, dp, step),
                    block(which, dp, (-step) % SIDE, at_of(step), quarter),
                    block(which, dp, 2, at_of(step), quarter),
                    1 - which,
                    step,
                )

    def arrived(dx):
        for dz in range(SIDE):
            for which in (0, 1):
                dp, dq = (dx, dz) if which == 0 else (dz, dx)
                step = {1: -1, 3: 1}
                if dq == 0:
                    if dp in step:
                        net.need(("op", which, step[dp]))
                    elif dp == 2:
                        net.need(("fp", which, 1), ("fp", which, -1))
                elif dq == 2:
                    net.need(("fq", which, dp, 1), ("fq", which, dp, -1))
                elif dp == 0:
                    net.need(("oq", which, step[dq]))
                elif dp == 2:
                    net.need(("pq2", which, 1, step[dq]), ("pq2", which, -1, step[dq]))
                else:
                    net.need(("pq", which, dp, step[dq]))

    def stage(at):
        if at == 0:
            first_hops()
            far_hops()
            second_hops(0)
            load_gate_up.wait()
            load_down.wait()
            arrived(0)
        elif at == 1:
            second_hops(1)
            second_hops(3)
            arrived(1)
        elif at == 2:
            second_hops(2)
            arrived(3)
        else:
            arrived(2)

    before = lax.broadcasted_iota(jnp.int32, (128, 128), 0)
    after = lax.broadcasted_iota(jnp.int32, (128, 128), 1)
    earlier = jnp.where(before < after, 1.0, 0.0).astype(BF16)
    slot = lax.broadcasted_iota(jnp.int32, (slots, 128), 0).astype(F32)

    def group(g, carry):
        for at in range(SIDE):
            pl.when(g == at)(functools.partial(stage, at))
        dx = g + g // 2 - 2 * (g // 3)
        scales = []
        for dz in range(SIDE):
            table = meta_ref[dz, dx]
            member = jnp.sum(table[0:8] * chosen_ref[...], axis=0, keepdims=True)
            weight = jnp.sum(table[8:16] * chosen_ref[...], axis=0, keepdims=True)
            wide = jnp.broadcast_to(member, (16, 128)).astype(BF16)
            rank = jnp.dot(wide, earlier, preferred_element_type=F32)[0:1]
            hit = (slot == rank) & (member > 0.5)
            pick = jnp.where(hit, 1.0, 0.0).astype(BF16)
            scales.append(jnp.sum(jnp.where(hit, weight, 0.0), axis=1, keepdims=True))
            picks[dz] = pick
            for at, size in chunks(width, 1024):
                packed[dz * slots : (dz + 1) * slots, at : at + size] = jnp.dot(
                    pick, tokens[dx, dz, :, at : at + size], preferred_element_type=F32
                ).astype(BF16)
        scale = jnp.concatenate(scales, axis=0)
        for at, size in chunks(inner, 256):
            gate = across(packed[...], gate_up[at : at + size])
            up = across(packed[...], gate_up[inner + at : inner + at + size])
            act[:, at : at + size] = (
                (up + 1.0) * gate * jax.nn.sigmoid(1.702 * gate)
            ).astype(BF16)
        for at, size in chunks(width, 640):
            tile = jnp.dot(act[...], down[:, at : at + size], preferred_element_type=F32)
            tile = (tile * scale).astype(BF16)
            for dz in range(SIDE):
                parts[dx, dz, :, at : at + size] = along(
                    picks[dz], tile[dz * slots : (dz + 1) * slots]
                ).astype(BF16)
        return carry

    lax.fori_loop(0, SIDE, group, 0)

    for dp in (2, 1, 3, 0):
        for which in (0, 1):
            for side, step in ((0, 1), (1, -1)):
                net.start(
                    ("rh", which, dp, step),
                    part(which, dp, 2, at_of(step), quarter),
                    view(half_in, which, dp, side),
                    1 - which,
                    step,
                )

    def relay(dp):
        for which in (0, 1):
            for side, step in ((0, 1), (1, -1)):
                net.need(("rh", which, dp, step))
                there = part(which, dp, step % SIDE, at_of(step), quarter)
                add_rows(there(), there(), half_in.at[which, dp, side])
                net.start(
                    ("rf", which, dp, step),
                    part(which, dp, step % SIDE, 0, half_rows),
                    view(full_in, which, dp, side),
                    1 - which,
                    step,
                )

    def gather_in(dp):
        for which in (0, 1):
            net.need(("rf", which, dp, 1), ("rf", which, dp, -1))
            here = part(which, dp, 0, 0, half_rows)
            add_rows(here(), here(), full_in.at[which, dp, 0], full_in.at[which, dp, 1])

    def last_half(which):
        for side, step in ((0, 1), (1, -1)):
            net.start(
                ("lh", which, step),
                part(which, 2, 0, at_of(step), quarter),
                view(half_last, which, side),
                which,
                step,
            )

    def last_full(which):
        for side, step in ((0, 1), (1, -1)):
            net.need(("lh", which, step))
            there = part(which, step % SIDE, 0, at_of(step), quarter)
            add_rows(there(), there(), half_last.at[which, side])
            net.start(
                ("lf", which, step),
                part(which, step % SIDE, 0, 0, half_rows),
                view(full_last, which, side),
                which,
                step,
            )

    relay(2)
    relay(1)
    gather_in(2)
    last_half(0)
    last_half(1)
    relay(3)
    gather_in(1)
    relay(0)
    gather_in(3)
    last_full(0)
    last_full(1)
    for which in (0, 1):
        net.need(("rf", which, 0, 1), ("rf", which, 0, -1))
        net.need(("lf", which, 1), ("lf", which, -1))
        here = part(which, 0, 0, 0, half_rows)
        rows = slice(which * half_rows, (which + 1) * half_rows)
        add_rows(
            here(),
            here(),
            full_in.at[which, 0, 0],
            full_in.at[which, 0, 1],
            full_last.at[which, 0],
            full_last.at[which, 1],
            residual_ref.at[rows],
        )
        net.start(("out", which), here, view(out_ref, rows), 2, 1)
    net.finish()


def experts_and_pass(normed_mid, residual, meta, chosen, gate_up, down, slots):
    rows, width = normed_mid.shape
    inner = down.shape[0]
    anywhere = pl.BlockSpec(memory_space=pl.ANY)
    vmem = pl.BlockSpec(memory_space=pltpu.VMEM)
    half, quarter = rows // 2, rows // 4
    return pl.pallas_call(
        functools.partial(expert_kernel, slots),
        out_shape=jax.ShapeDtypeStruct((rows, width), BF16),
        in_specs=[anywhere, vmem, vmem, vmem, anywhere, anywhere],
        out_specs=anywhere,
        scratch_shapes=[
            pltpu.VMEM((SIDE, SIDE, rows, width), BF16),
            pltpu.VMEM((SIDE, SIDE, rows, width), BF16),
            pltpu.VMEM(gate_up.shape, BF16),
            pltpu.VMEM(down.shape, BF16),
            pltpu.VMEM((SIDE * slots, width), BF16),
            pltpu.VMEM((SIDE * slots, inner), BF16),
            pltpu.VMEM((SIDE, slots, rows), BF16),
            pltpu.VMEM((2, SIDE, 2, quarter, width), BF16),
            pltpu.VMEM((2, SIDE, 2, half, width), BF16),
            pltpu.VMEM((2, 2, quarter, width), BF16),
            pltpu.VMEM((2, 2, half, width), BF16),
            pltpu.SemaphoreType.DMA((3,)),
            pltpu.SemaphoreType.DMA((96,)),
            pltpu.SemaphoreType.DMA((96,)),
        ],
        compiler_params=pltpu.CompilerParams(
            collective_id=1, has_side_effects=True, vmem_limit_bytes=62 * 1024 * 1024
        ),
        cost_estimate=pl.CostEstimate(
            flops=16_000_000_000, bytes_accessed=16_000_000, transcendentals=1_000_000
        ),
    )(normed_mid, residual, meta, chosen, gate_up, down)


def routing_tables(ids, logits, holders):
    kinds = lax.broadcasted_iota(jnp.int32, (8, ids.shape[0], TOP), 0)
    equal = (ids[None] == kinds).astype(F32)
    weights = jax.nn.softmax(logits, axis=-1)
    member = jnp.sum(equal, axis=-1)
    weight = jnp.sum(equal * weights[None], axis=-1)
    pair = lax.axis_index("expert") // 2
    mine = jnp.sum(jnp.where(jnp.arange(8) == pair, holders, 0))
    chosen = (lax.broadcasted_iota(jnp.int32, (8, ids.shape[0]), 0) == mine).astype(F32)
    return jnp.concatenate([member, weight], axis=0), chosen


def project_kernel(
    tokens_ref,
    weight_hbm,
    bias_ref,
    meta_ref,
    projected_ref,
    behind_ref,
    tables_ref,
    weight,
    slices,
    transit,
    total,
    sent,
    half_in,
    full_in,
    behind,
    tables,
    local_sem,
    send_sem,
    recv_sem,
):
    net = Links(send_sem, recv_sem)
    columns = weight.shape[3]
    middle = columns // 2
    rows = projected_ref.shape[0]
    loads = [
        pltpu.make_async_copy(
            weight_hbm.at[:, pl.ds(which * columns, columns)], weight.at[which, 0], local_sem.at[which]
        )
        for which in (0, 1)
    ]
    for load in loads:
        load.start()
    tables[0, 0] = meta_ref[...]
    place = (net.x, net.z)

    def for_device(which, step, at, size):
        to = (place[1 - which] + step + SIDE) % SIDE
        pieces = slice(at, at + size)
        if which == 0:
            return lambda: tokens_ref.at[pieces, to]
        return lambda: tokens_ref.at[to, pieces]

    def kept(which, dq, at, size):
        lanes = slice(dq * rows, (dq + 1) * rows)
        pieces = slice(at, at + size)
        return lambda: slices.at[which, pieces, :, lanes]

    stays = [
        pltpu.make_async_copy(
            for_device(which, 0, 0, SIDE)(), kept(which, 0, 0, SIDE)(), local_sem.at[2 + which]
        )
        for which in (0, 1)
    ]
    for stay in stays:
        stay.start()
    net.barrier([(0, 1), (0, -1), (1, 1), (1, -1), (3, 1), (3, -1)])
    steps = ((0, 1), (1, -1))
    net.start(("mx", 1), view(tables, 0, 0), view(tables, 0, 3), 0, 1)
    net.start(("mx", -1), view(tables, 0, 0), view(tables, 0, 1), 0, -1)
    for which in (0, 1):
        for side, step in steps:
            net.start(
                ("tt", which, step),
                for_device(which, 2, side * 2, 2),
                view(transit, which, side),
                1 - which,
                step,
            )
    for which in (0, 1):
        for side, step in steps:
            net.start(
                ("ta", which, step),
                for_device(which, step, 0, SIDE),
                kept(which, (-step) % SIDE, 0, SIDE),
                1 - which,
                step,
            )
    for which in (0, 1):
        loads[which].wait()
        for side, step in steps:
            net.start(
                ("wo", which, step),
                view(weight, which, 0),
                view(weight, which, (-step) % SIDE),
                which,
                step,
            )
    net.need(("mx", 1))
    net.start(("mf", 0), view(tables, 0, 3), view(tables, 0, 2), 0, 1)
    for which in (0, 1):
        for side, step in steps:
            net.need(("tt", which, step))
            net.start(
                ("tf", which, step),
                view(transit, which, side),
                kept(which, 2, side * 2, 2),
                1 - which,
                step,
            )
    net.need(("mx", -1), ("mf", 0))
    net.start(("mz", 1), view(tables, 0), view(tables, 3), 1, 1)
    net.start(("mz", -1), view(tables, 0), view(tables, 1), 1, -1)

    def multiply(which, dp):
        piece = (place[which] + dp) % SIDE
        lhs = slices[which, piece]
        for at, size in chunks(columns, 640):
            term = along(lhs, weight[which, dp, :, at : at + size])
            if dp == 0:
                total[which, :, at : at + size] = term
            else:
                total[which, :, at : at + size] += term

    def pass_on(which, step):
        net.need(("wo", which, step))
        part = slice(0, middle) if step == 1 else slice(middle, columns)
        net.start(
            ("wf", which, step),
            lambda: weight.at[which, (-step) % SIDE, :, part],
            lambda: weight.at[which, 2, :, part],
            which,
            step,
        )

    for which in (0, 1):
        stays[which].wait()
        net.need(("ta", which, 1), ("ta", which, -1), ("tf", which, 1), ("tf", which, -1))
    for which in (0, 1):
        multiply(which, 0)
    for step in (1, -1):
        for which in (0, 1):
            pass_on(which, step)
    net.need(("mz", 1), ("mz", -1))
    net.start(("mg", 0), view(tables, 3), view(tables, 2), 1, 1)
    for dp in (3, 1):
        for which in (0, 1):
            multiply(which, dp)
    for which in (1, 0):
        net.need(("wf", which, 1), ("wf", which, -1))
        multiply(which, 2)
        sent[which, 2] = total[which, 2 * rows : 3 * rows].astype(BF16)
        for side, step in steps:
            part = slice(side * middle, (side + 1) * middle)
            net.start(
                ("rh", which, step),
                view(sent, which, 2, slice(None), part),
                view(half_in, which, side),
                1 - which,
                step,
            )
    for which in (1, 0):
        for side, step in steps:
            dq = step % SIDE
            mine = slice(dq * rows, (dq + 1) * rows)
            part = slice(side * middle, (side + 1) * middle)
            other = slice((1 - side) * middle, (2 - side) * middle)
            sent[which, dq, :, other] = total[which, mine, other].astype(BF16)
            net.need(("rh", which, step))
            sent[which, dq, :, part] = (
                total[which, mine, part] + half_in[which, side].astype(F32)
            ).astype(BF16)
            net.start(
                ("rf", which, step),
                view(sent, which, dq),
                view(full_in, which, side),
                1 - which,
                step,
            )
    for which in (1, 0):
        net.need(("rf", which, 1), ("rf", which, -1))
        lanes = slice(which * columns, (which + 1) * columns)
        projected_ref[:, lanes] = (
            total[which, 0:rows]
            + full_in[which, 0].astype(F32)
            + full_in[which, 1].astype(F32)
            + bias_ref[:, lanes]
        ).astype(BF16)
        if which == 1:
            keys = slice(2 * columns - behind.shape[1], 2 * columns)
            net.start(
                ("kv", 0), view(projected_ref, slice(None), keys), view(behind), 3, 1
            )
    net.finish()
    behind_ref[...] = behind[...]
    tables_ref[...] = tables[...]


def project(tokens, weight, bias, meta):
    depth, rows = tokens.shape[2:]
    wide = weight.shape[1]
    columns = wide // 2
    keys = 2 * KEY_VALUE_HEADS * HEAD_DIM
    vmem = pl.BlockSpec(memory_space=pltpu.VMEM)
    return pl.pallas_call(
        project_kernel,
        out_shape=(
            jax.ShapeDtypeStruct((rows, wide), BF16),
            jax.ShapeDtypeStruct((rows, keys), BF16),
            jax.ShapeDtypeStruct((SIDE, SIDE, 16, rows), F32),
        ),
        in_specs=[vmem, pl.BlockSpec(memory_space=pl.ANY), vmem, vmem],
        out_specs=(vmem, vmem, vmem),
        scratch_shapes=[
            pltpu.VMEM((2, SIDE, depth, columns), BF16),
            pltpu.VMEM((2, SIDE, depth, SIDE * rows), BF16),
            pltpu.VMEM((2, 2, 2, depth, rows), BF16),
            pltpu.VMEM((2, SIDE * rows, columns), F32),
            pltpu.VMEM((2, SIDE, rows, columns), BF16),
            pltpu.VMEM((2, 2, rows, columns // 2), BF16),
            pltpu.VMEM((2, 2, rows, columns), BF16),
            pltpu.VMEM((rows, keys), BF16),
            pltpu.VMEM((SIDE, SIDE, 16, rows), F32),
            pltpu.SemaphoreType.DMA((4,)),
            pltpu.SemaphoreType.DMA((48,)),
            pltpu.SemaphoreType.DMA((48,)),
        ],
        compiler_params=pltpu.CompilerParams(
            collective_id=2, has_side_effects=True, vmem_limit_bytes=48 * 1024 * 1024
        ),
        cost_estimate=pl.CostEstimate(
            flops=2_000_000_000, bytes_accessed=4_000_000, transcendentals=0
        ),
    )(tokens, weight, bias, meta)


def shards(
    section_input,
    attention_gain,
    query_key_value_weight,
    qkv_bias,
    out_weight,
    out_bias,
    attention_sink_logits,
    expert_gain,
    gate_up_weight,
    down_weight,
    expert_ids,
    gate_logits,
    placement,
):
    count_of_rows = section_input.shape[1]
    experts_count = placement.shape[1]
    slots = 2 * min(count_of_rows // 2, count_of_rows * TOP * 5 // (8 * experts_count))
    offset = lax.axis_index("expert") * count_of_rows
    query_group_width = QUERY_HEADS // KEY_VALUE_HEADS
    state = section_input[0]
    normed_in = normed(state, attention_gain[0])
    meta, chosen = routing_tables(expert_ids[0], gate_logits[0], placement[0])
    depth = query_key_value_weight.shape[1]
    projected_rows, rim_rows, tables = project(
        normed_in.T.reshape(SIDE, SIDE, depth, count_of_rows), query_key_value_weight[0], qkv_bias, meta
    )
    query_rows = projected_rows[:, : QUERY_HEADS * HEAD_DIM].reshape(
        count_of_rows, KEY_VALUE_HEADS, query_group_width, HEAD_DIM
    )
    key_value = projected_rows[:, QUERY_HEADS * HEAD_DIM :]
    rows_in_window = jnp.concatenate([rim_rows, key_value], 0)
    key_row_slice = rows_in_window[:, : KEY_VALUE_HEADS * HEAD_DIM].reshape(
        WINDOW_TOKENS + count_of_rows, KEY_VALUE_HEADS, HEAD_DIM
    )
    value_row_slice = rows_in_window[:, KEY_VALUE_HEADS * HEAD_DIM :].reshape(
        WINDOW_TOKENS + count_of_rows, KEY_VALUE_HEADS, HEAD_DIM
    )
    scores = (
        jnp.einsum("ikgd,jkd->kgij", query_rows, key_row_slice, preferred_element_type=jnp.float32)
        * 0.125
    )
    query_pos = offset + jnp.arange(count_of_rows, dtype=jnp.int32)
    key_pos = offset - WINDOW_TOKENS + jnp.arange(WINDOW_TOKENS + count_of_rows, dtype=jnp.int32)
    distance = query_pos[:, None] - key_pos[None, :]
    inside = (distance >= 0) & (distance < WINDOW_TOKENS) & (key_pos >= 0)[None, :]
    head_sink_logit = attention_sink_logits[0].reshape(KEY_VALUE_HEADS, query_group_width)[
        :, :, None
    ]
    masked = jnp.where(inside, scores, -1e30)
    peak = jnp.maximum(jnp.max(masked, axis=-1), head_sink_logit)
    numer = jnp.where(inside, jnp.exp(masked - peak[..., None]), 0.0)
    denominator = jnp.sum(numer, axis=-1) + jnp.exp(head_sink_logit - peak)
    attention = (numer / denominator[..., None]).astype(jnp.bfloat16)
    mixed = jnp.einsum(
        "kgij,jkd->ikgd", attention, value_row_slice, preferred_element_type=jnp.float32
    )
    attended = mixed.astype(jnp.bfloat16).reshape(count_of_rows, QUERY_HEADS * HEAD_DIM)
    residual = (
        state.astype(jnp.float32)
        + jnp.dot(attended, out_weight[0], preferred_element_type=jnp.float32)
        + out_bias[0]
    ).astype(jnp.bfloat16)
    normed_mid = normed(residual, expert_gain[0])
    moved = experts_and_pass(
        normed_mid, residual, tables, chosen, gate_up_weight[0, 0].T, down_weight[0, 0], slots
    )
    return moved[None]


def solution(mesh):
    return jax.shard_map(
        shards,
        mesh=mesh,
        in_specs=(
            P("section", "expert", None),
            P("section", None),
            P("section", "expert", None),
            P("section", None),
            P("section", None, None),
            P("section", None),
            P("section", None),
            P("section", None),
            P("section", "expert", None, None),
            P("section", "expert", None, None),
            P("section", "expert", None),
            P("section", "expert", None),
            P("section", None),
        ),
        out_specs=P("section", "expert", None),
        check_vma=False,
    )
```

```python
import functools

import jax
import jax.numpy as jnp
from jax import lax
from jax.experimental import pallas as pl
from jax.experimental.pallas import tpu as pltpu
from jax.sharding import PartitionSpec as P

HEAD_DIM = 64
QUERY_HEADS = 32
KEY_VALUE_HEADS = 4
WINDOW_TOKENS = 128
TOP = 4
SIDE = 4
MESH = pl.DeviceIdType.MESH
F32 = jnp.float32
BF16 = jnp.bfloat16


def normed(vector, gain_row):
    as_float = vector.astype(jnp.float32)
    inverse_rms = lax.rsqrt(jnp.mean(as_float * as_float, axis=-1, keepdims=True) + 1e-05)
    return (as_float * inverse_rms * gain_row).astype(jnp.bfloat16)


class Links:
    def __init__(self, send, recv):
        self.send, self.recv = send, recv
        self.keys, self.started, self.done = {}, [], set()
        self.made = {}
        self.section = lax.axis_index("section")
        me = lax.axis_index("expert")
        self.x, self.z = me // SIDE, me % SIDE

    def neighbour(self, axis, step):
        if axis == 3:
            return (self.section, (self.x * SIDE + self.z + step + 16) % 16)
        if axis == 2:
            return ((self.section + step + 8) % 8, self.x * SIDE + self.z)
        if axis == 0:
            return (self.section, ((self.x + step + SIDE) % SIDE) * SIDE + self.z)
        return (self.section, self.x * SIDE + (self.z + step + SIDE) % SIDE)

    def barrier(self, partners):
        sem = pltpu.get_barrier_semaphore()
        for axis, step in partners:
            pl.semaphore_signal(
                sem, inc=1, device_id=self.neighbour(axis, step), device_id_type=MESH
            )
        pl.semaphore_wait(sem, len(partners))

    def start(self, name, src, dst, axis, step):
        key = self.keys.setdefault(name, len(self.keys))
        copy = pltpu.make_async_remote_copy(
            src_ref=src(),
            dst_ref=dst(),
            send_sem=self.send.at[key],
            recv_sem=self.recv.at[key],
            device_id=self.neighbour(axis, step),
            device_id_type=MESH,
        )
        copy.start()
        self.made[name] = (src, dst, axis, step)

    def remake(self, name):
        src, dst, axis, step = self.made[name]
        key = self.keys[name]
        return pltpu.make_async_remote_copy(
            src_ref=src(),
            dst_ref=dst(),
            send_sem=self.send.at[key],
            recv_sem=self.recv.at[key],
            device_id=self.neighbour(axis, step),
            device_id_type=MESH,
        )

    def need(self, *names):
        for name in names:
            if name not in self.done:
                self.done.add(name)
                self.remake(name).wait_recv()

    def finish(self):
        for name in self.made:
            self.need(name)
            self.remake(name).wait_send()


def of_four(g, values):
    a, b, c, d = values
    return (
        b * (g * (g - 2) * (g - 3)) // 2
        - c * (g * (g - 1) * (g - 3)) // 2
        + d * (g * (g - 1) * (g - 2)) // 6
        - a * ((g - 1) * (g - 2) * (g - 3)) // 6
    )


def add_rows(dst, *parts):
    step = 16

    def body(i, carry):
        rows = pl.ds(pl.multiple_of(i * step, step), step)
        total = parts[0][rows].astype(F32)
        for part in parts[1:]:
            total = total + part[rows].astype(F32)
        dst[rows] = total.astype(dst.dtype)
        return carry

    lax.fori_loop(0, dst.shape[0] // step, body, 0)


def view(ref, *index):
    return lambda: ref.at[index]


def across(rows, other):
    return lax.dot_general(rows, other, (((1,), (1,)), ((), ())), preferred_element_type=F32)


def along(first, second):
    return lax.dot_general(first, second, (((0,), (0,)), ((), ())), preferred_element_type=F32)


def chunks(total, size):
    return [(at, min(size, total - at)) for at in range(0, total, size)]


def expert_kernel(
    slots,
    normed_ref,
    residual_ref,
    meta_ref,
    chosen_ref,
    gate_up_hbm,
    down_hbm,
    out_ref,
    tokens,
    parts,
    gate_up,
    down,
    packed,
    act,
    picks,
    half_in,
    full_in,
    half_last,
    full_last,
    local_sem,
    send_sem,
    recv_sem,
):
    half_rows = tokens.shape[2] // 2
    quarter = half_rows // 2
    width = tokens.shape[3]
    inner = act.shape[1]
    net = Links(send_sem, recv_sem)
    load_tokens = pltpu.make_async_copy(normed_ref, tokens.at[0, 0], local_sem.at[0])
    load_gate_up = pltpu.make_async_copy(gate_up_hbm, gate_up, local_sem.at[1])
    load_down = pltpu.make_async_copy(down_hbm, down, local_sem.at[2])
    load_tokens.start()
    net.barrier([(0, 1), (0, -1), (1, 1), (1, -1), (2, 1), (2, -1)])

    load_tokens.wait()
    load_gate_up.start()
    load_down.start()

    def block(which, dp, dq, at, size):
        first, second = (dp, dq) if which == 0 else (dq, dp)
        rows = slice(which * half_rows + at, which * half_rows + at + size)
        return lambda: tokens.at[first, second, rows]

    def part(which, dp, dq, at, size):
        first, second = (dp, dq) if which == 0 else (dq, dp)
        rows = slice(which * half_rows + at, which * half_rows + at + size)
        return lambda: parts.at[first, second, rows]

    def own(which, axis, step):
        to = (-step) % SIDE
        place = (to, 0) if axis == which else (0, to)
        name = ("op" if axis == which else "oq", which, step)
        net.start(
            name,
            block(which, 0, 0, 0, half_rows),
            block(which, *place, 0, half_rows),
            axis,
            step,
        )

    for axis in (0, 1):
        for step in (1, -1):
            own(axis, axis, step)
    for axis in (0, 1):
        for step in (1, -1):
            own(1 - axis, axis, step)

    def at_of(step):
        return 0 if step == 1 else quarter

    def on_across(which, dp, dq_axis_step):
        step = dq_axis_step
        net.start(
            ("pq", which, dp, step),
            block(which, dp, 0, 0, half_rows),
            block(which, dp, (-step) % SIDE, 0, half_rows),
            1 - which,
            step,
        )

    def first_hops():
        for step in (1, -1):
            for which in (0, 1):
                dp = (-step) % SIDE
                net.need(("op", which, step))
                net.start(
                    ("fp", which, step),
                    block(which, dp, 0, at_of(step), quarter),
                    block(which, 2, 0, at_of(step), quarter),
                    which,
                    step,
                )
        for which in (0, 1):
            on_across(which, 3, 1)
            on_across(which, 3, -1)

    def other_hops():
        for which in (0, 1):
            on_across(which, 1, 1)
            on_across(which, 1, -1)

    def far_hops():
        for half in (1, -1):
            for which in (0, 1):
                net.need(("fp", which, half))
                for step in (1, -1):
                    net.start(
                        ("pq2", which, half, step),
                        block(which, 2, 0, at_of(half), quarter),
                        block(which, 2, (-step) % SIDE, at_of(half), quarter),
                        1 - which,
                        step,
                    )

    def second_hops(dp):
        for step in (1, -1):
            for which in (0, 1):
                if dp == 0:
                    net.need(("oq", which, step))
                elif dp == 2:
                    net.need(("pq2", which, step, step))
                else:
                    net.need(("pq", which, dp, step))
                net.start(
                    ("fq", which, dp, step),
                    block(which, dp, (-step) % SIDE, at_of(step), quarter),
                    block(which, dp, 2, at_of(step), quarter),
                    1 - which,
                    step,
                )

    def arrived(blocks):
        for dx, dz in blocks:
            for which in (0, 1):
                dp, dq = (dx, dz) if which == 0 else (dz, dx)
                step = {1: -1, 3: 1}
                if dq == 0:
                    if dp in step:
                        net.need(("op", which, step[dp]))
                    elif dp == 2:
                        net.need(("fp", which, 1), ("fp", which, -1))
                elif dq == 2:
                    net.need(("fq", which, dp, 1), ("fq", which, dp, -1))
                elif dp == 0:
                    net.need(("oq", which, step[dq]))
                elif dp == 2:
                    net.need(("pq2", which, 1, step[dq]), ("pq2", which, -1, step[dq]))
                else:
                    net.need(("pq", which, dp, step[dq]))

    groups = (
        ((0, 0), (1, 0), (3, 0), (0, 1)),
        ((0, 3), (0, 2), (2, 0), (3, 3)),
        ((1, 1), (1, 3), (3, 1), (3, 2)),
        ((2, 3), (1, 2), (2, 1), (2, 2)),
    )

    def stage(at):
        if at == 0:
            first_hops()
            second_hops(0)
            other_hops()
            load_gate_up.wait()
            load_down.wait()
        elif at == 1:
            far_hops()
            second_hops(3)
        elif at == 2:
            second_hops(1)
            second_hops(2)
            back(0)
        else:
            relay(0)
        arrived(groups[at])

    def relay(dp):
        for which in (0, 1):
            for side, step in ((0, 1), (1, -1)):
                net.need(("rh", which, dp, step))
                there = part(which, dp, step % SIDE, at_of(step), quarter)
                add_rows(there(), there(), half_in.at[which, dp, side])
                net.start(
                    ("rf", which, dp, step),
                    part(which, dp, step % SIDE, 0, half_rows),
                    view(full_in, which, dp, side),
                    1 - which,
                    step,
                )

    def back(dp):
        for which in (0, 1):
            for side, step in ((0, 1), (1, -1)):
                net.start(
                    ("rh", which, dp, step),
                    part(which, dp, 2, at_of(step), quarter),
                    view(half_in, which, dp, side),
                    1 - which,
                    step,
                )

    before = lax.broadcasted_iota(jnp.int32, (128, 128), 0)
    after = lax.broadcasted_iota(jnp.int32, (128, 128), 1)
    earlier = jnp.where(before < after, 1.0, 0.0).astype(BF16)
    slot = lax.broadcasted_iota(jnp.int32, (slots, 128), 0).astype(F32)

    def group(g, carry):
        for at in range(SIDE):
            pl.when(g == at)(functools.partial(stage, at))
        places = [[of_four(g, [group[k][axis] for group in groups]) for axis in (0, 1)] for k in range(SIDE)]
        scales = []
        for k, (dx, dz) in enumerate(places):
            table = meta_ref[dz, dx]
            member = jnp.sum(table[0:8] * chosen_ref[...], axis=0, keepdims=True)
            weight = jnp.sum(table[8:16] * chosen_ref[...], axis=0, keepdims=True)
            wide = jnp.broadcast_to(member, (16, 128)).astype(BF16)
            rank = jnp.dot(wide, earlier, preferred_element_type=F32)[0:1]
            hit = (slot == rank) & (member > 0.5)
            pick = jnp.where(hit, 1.0, 0.0).astype(BF16)
            scales.append(jnp.sum(jnp.where(hit, weight, 0.0), axis=1, keepdims=True))
            picks[k] = pick
            for at, size in chunks(width, 1024):
                packed[k * slots : (k + 1) * slots, at : at + size] = jnp.dot(
                    pick, tokens[dx, dz, :, at : at + size], preferred_element_type=F32
                ).astype(BF16)
        scale = jnp.concatenate(scales, axis=0)
        for at, size in chunks(inner, 256):
            gate = across(packed[...], gate_up[at : at + size])
            up = across(packed[...], gate_up[inner + at : inner + at + size])
            act[:, at : at + size] = (
                (up + 1.0) * gate * jax.nn.sigmoid(1.702 * gate)
            ).astype(BF16)
        for at, size in chunks(width, 640):
            tile = jnp.dot(act[...], down[:, at : at + size], preferred_element_type=F32)
            tile = (tile * scale).astype(BF16)
            for k, (dx, dz) in enumerate(places):
                parts[dx, dz, :, at : at + size] = along(
                    picks[k], tile[k * slots : (k + 1) * slots]
                ).astype(BF16)
        return carry

    lax.fori_loop(0, SIDE, group, 0)

    for dp in (2, 1, 3):
        back(dp)

    def gather_in(dp):
        for which in (0, 1):
            net.need(("rf", which, dp, 1), ("rf", which, dp, -1))
            here = part(which, dp, 0, 0, half_rows)
            add_rows(here(), here(), full_in.at[which, dp, 0], full_in.at[which, dp, 1])

    def last_half(which):
        for side, step in ((0, 1), (1, -1)):
            net.start(
                ("lh", which, step),
                part(which, 2, 0, at_of(step), quarter),
                view(half_last, which, side),
                which,
                step,
            )

    def last_full(step):
        side = (1 - step) // 2
        for which in (0, 1):
            net.need(("lh", which, step))
            there = part(which, step % SIDE, 0, at_of(step), quarter)
            add_rows(there(), there(), half_last.at[which, side])
            for piece in (0, 1):
                rows = slice(piece * quarter, (piece + 1) * quarter)
                net.start(
                    ("lf", which, step, piece),
                    part(which, step % SIDE, 0, piece * quarter, quarter),
                    view(full_last, which, side, rows),
                    which,
                    step,
                )

    relay(2)
    relay(1)
    gather_in(2)
    last_half(0)
    last_half(1)
    relay(3)
    gather_in(1)
    last_full(1)
    gather_in(3)
    last_full(-1)
    for which in (0, 1):
        net.need(("rf", which, 0, 1), ("rf", which, 0, -1))
    for piece in (0, 1):
        for which in (0, 1):
            net.need(("lf", which, 1, piece), ("lf", which, -1, piece))
            here = part(which, 0, 0, piece * quarter, quarter)
            inside = slice(piece * quarter, (piece + 1) * quarter)
            at = which * half_rows + piece * quarter
            rows = slice(at, at + quarter)
            add_rows(
                here(),
                here(),
                full_in.at[which, 0, 0, inside],
                full_in.at[which, 0, 1, inside],
                full_last.at[which, 0, inside],
                full_last.at[which, 1, inside],
                residual_ref.at[rows],
            )
            net.start(("out", which, piece), here, view(out_ref, rows), 2, 1)
    net.finish()


def experts_and_pass(normed_mid, residual, meta, chosen, gate_up, down, slots):
    rows, width = normed_mid.shape
    inner = down.shape[0]
    anywhere = pl.BlockSpec(memory_space=pl.ANY)
    vmem = pl.BlockSpec(memory_space=pltpu.VMEM)
    half, quarter = rows // 2, rows // 4
    return pl.pallas_call(
        functools.partial(expert_kernel, slots),
        out_shape=jax.ShapeDtypeStruct((rows, width), BF16),
        in_specs=[anywhere, vmem, vmem, vmem, anywhere, anywhere],
        out_specs=anywhere,
        scratch_shapes=[
            pltpu.VMEM((SIDE, SIDE, rows, width), BF16),
            pltpu.VMEM((SIDE, SIDE, rows, width), BF16),
            pltpu.VMEM(gate_up.shape, BF16),
            pltpu.VMEM(down.shape, BF16),
            pltpu.VMEM((SIDE * slots, width), BF16),
            pltpu.VMEM((SIDE * slots, inner), BF16),
            pltpu.VMEM((SIDE, slots, rows), BF16),
            pltpu.VMEM((2, SIDE, 2, quarter, width), BF16),
            pltpu.VMEM((2, SIDE, 2, half, width), BF16),
            pltpu.VMEM((2, 2, quarter, width), BF16),
            pltpu.VMEM((2, 2, half, width), BF16),
            pltpu.SemaphoreType.DMA((3,)),
            pltpu.SemaphoreType.DMA((96,)),
            pltpu.SemaphoreType.DMA((96,)),
        ],
        compiler_params=pltpu.CompilerParams(
            collective_id=1, has_side_effects=True, vmem_limit_bytes=62 * 1024 * 1024
        ),
        cost_estimate=pl.CostEstimate(
            flops=16_000_000_000, bytes_accessed=16_000_000, transcendentals=1_000_000
        ),
    )(normed_mid, residual, meta, chosen, gate_up, down)


def routing_tables(ids, logits, holders):
    kinds = lax.broadcasted_iota(jnp.int32, (8, ids.shape[0], TOP), 0)
    equal = (ids[None] == kinds).astype(F32)
    weights = jax.nn.softmax(logits, axis=-1)
    member = jnp.sum(equal, axis=-1)
    weight = jnp.sum(equal * weights[None], axis=-1)
    pair = lax.axis_index("expert") // 2
    mine = jnp.sum(jnp.where(jnp.arange(8) == pair, holders, 0))
    chosen = (lax.broadcasted_iota(jnp.int32, (8, ids.shape[0]), 0) == mine).astype(F32)
    return jnp.concatenate([member, weight], axis=0), chosen


def project_kernel(
    tokens_ref,
    weight_hbm,
    bias_ref,
    meta_ref,
    projected_ref,
    behind_ref,
    tables_ref,
    weight,
    slices,
    transit,
    total,
    sent,
    half_in,
    full_in,
    behind,
    tables,
    local_sem,
    send_sem,
    recv_sem,
):
    net = Links(send_sem, recv_sem)
    columns = weight.shape[3]
    middle = columns // 2
    rows = projected_ref.shape[0]
    loads = [
        pltpu.make_async_copy(
            weight_hbm.at[:, pl.ds(which * columns, columns)], weight.at[which, 0], local_sem.at[which]
        )
        for which in (0, 1)
    ]
    for load in loads:
        load.start()
    tables[0, 0] = meta_ref[...]
    place = (net.x, net.z)

    def for_device(which, step, at, size):
        to = (place[1 - which] + step + SIDE) % SIDE
        pieces = slice(at, at + size)
        if which == 0:
            return lambda: tokens_ref.at[pieces, to]
        return lambda: tokens_ref.at[to, pieces]

    def kept(which, dq, at, size):
        lanes = slice(dq * rows, (dq + 1) * rows)
        pieces = slice(at, at + size)
        return lambda: slices.at[which, pieces, :, lanes]

    stays = [
        pltpu.make_async_copy(
            for_device(which, 0, 0, SIDE)(), kept(which, 0, 0, SIDE)(), local_sem.at[2 + which]
        )
        for which in (0, 1)
    ]
    for stay in stays:
        stay.start()
    net.barrier([(0, 1), (0, -1), (1, 1), (1, -1), (3, 1), (3, -1)])
    steps = ((0, 1), (1, -1))
    net.start(("mx", 1), view(tables, 0, 0), view(tables, 0, 3), 0, 1)
    net.start(("mx", -1), view(tables, 0, 0), view(tables, 0, 1), 0, -1)
    for which in (0, 1):
        for side, step in steps:
            net.start(
                ("tt", which, step),
                for_device(which, 2, side * 2, 2),
                view(transit, which, side),
                1 - which,
                step,
            )
    for which in (0, 1):
        for side, step in steps:
            net.start(
                ("ta", which, step),
                for_device(which, step, 0, SIDE),
                kept(which, (-step) % SIDE, 0, SIDE),
                1 - which,
                step,
            )
    for which in (0, 1):
        loads[which].wait()
        for side, step in steps:
            net.start(
                ("wo", which, step),
                view(weight, which, 0),
                view(weight, which, (-step) % SIDE),
                which,
                step,
            )
    net.need(("mx", 1))
    net.start(("mf", 0), view(tables, 0, 3), view(tables, 0, 2), 0, 1)
    for which in (0, 1):
        for side, step in steps:
            net.need(("tt", which, step))
            net.start(
                ("tf", which, step),
                view(transit, which, side),
                kept(which, 2, side * 2, 2),
                1 - which,
                step,
            )
    net.need(("mx", -1), ("mf", 0))
    net.start(("mz", 1), view(tables, 0), view(tables, 3), 1, 1)
    net.start(("mz", -1), view(tables, 0), view(tables, 1), 1, -1)

    def multiply(which, dp):
        piece = (place[which] + dp) % SIDE
        lhs = slices[which, piece]
        for at, size in chunks(columns, 640):
            term = along(lhs, weight[which, dp, :, at : at + size])
            if dp == 0:
                total[which, :, at : at + size] = term
            else:
                total[which, :, at : at + size] += term

    def pass_on(which, step):
        net.need(("wo", which, step))
        part = slice(0, middle) if step == 1 else slice(middle, columns)
        net.start(
            ("wf", which, step),
            lambda: weight.at[which, (-step) % SIDE, :, part],
            lambda: weight.at[which, 2, :, part],
            which,
            step,
        )

    for which in (0, 1):
        stays[which].wait()
        net.need(("ta", which, 1), ("ta", which, -1), ("tf", which, 1), ("tf", which, -1))
    for which in (0, 1):
        multiply(which, 0)
    for step in (1, -1):
        for which in (0, 1):
            pass_on(which, step)
    net.need(("mz", 1), ("mz", -1))
    net.start(("mg", 0), view(tables, 3), view(tables, 2), 1, 1)
    for dp in (3, 1):
        for which in (0, 1):
            multiply(which, dp)
    for which in (1, 0):
        net.need(("wf", which, 1), ("wf", which, -1))
        multiply(which, 2)
        sent[which, 2] = total[which, 2 * rows : 3 * rows].astype(BF16)
        for side, step in steps:
            part = slice(side * middle, (side + 1) * middle)
            net.start(
                ("rh", which, step),
                view(sent, which, 2, slice(None), part),
                view(half_in, which, side),
                1 - which,
                step,
            )
    for which in (1, 0):
        for side, step in steps:
            dq = step % SIDE
            mine = slice(dq * rows, (dq + 1) * rows)
            part = slice(side * middle, (side + 1) * middle)
            other = slice((1 - side) * middle, (2 - side) * middle)
            sent[which, dq, :, other] = total[which, mine, other].astype(BF16)
            net.need(("rh", which, step))
            sent[which, dq, :, part] = (
                total[which, mine, part] + half_in[which, side].astype(F32)
            ).astype(BF16)
            net.start(
                ("rf", which, step),
                view(sent, which, dq),
                view(full_in, which, side),
                1 - which,
                step,
            )
    for which in (1, 0):
        net.need(("rf", which, 1), ("rf", which, -1))
        lanes = slice(which * columns, (which + 1) * columns)
        projected_ref[:, lanes] = (
            total[which, 0:rows]
            + full_in[which, 0].astype(F32)
            + full_in[which, 1].astype(F32)
            + bias_ref[:, lanes]
        ).astype(BF16)
        if which == 1:
            keys = slice(2 * columns - behind.shape[1], 2 * columns)
            net.start(
                ("kv", 0), view(projected_ref, slice(None), keys), view(behind), 3, 1
            )
    net.finish()
    behind_ref[...] = behind[...]
    tables_ref[...] = tables[...]


def project(tokens, weight, bias, meta):
    depth, rows = tokens.shape[2:]
    wide = weight.shape[1]
    columns = wide // 2
    keys = 2 * KEY_VALUE_HEADS * HEAD_DIM
    vmem = pl.BlockSpec(memory_space=pltpu.VMEM)
    return pl.pallas_call(
        project_kernel,
        out_shape=(
            jax.ShapeDtypeStruct((rows, wide), BF16),
            jax.ShapeDtypeStruct((rows, keys), BF16),
            jax.ShapeDtypeStruct((SIDE, SIDE, 16, rows), F32),
        ),
        in_specs=[vmem, pl.BlockSpec(memory_space=pl.ANY), vmem, vmem],
        out_specs=(vmem, vmem, vmem),
        scratch_shapes=[
            pltpu.VMEM((2, SIDE, depth, columns), BF16),
            pltpu.VMEM((2, SIDE, depth, SIDE * rows), BF16),
            pltpu.VMEM((2, 2, 2, depth, rows), BF16),
            pltpu.VMEM((2, SIDE * rows, columns), F32),
            pltpu.VMEM((2, SIDE, rows, columns), BF16),
            pltpu.VMEM((2, 2, rows, columns // 2), BF16),
            pltpu.VMEM((2, 2, rows, columns), BF16),
            pltpu.VMEM((rows, keys), BF16),
            pltpu.VMEM((SIDE, SIDE, 16, rows), F32),
            pltpu.SemaphoreType.DMA((4,)),
            pltpu.SemaphoreType.DMA((48,)),
            pltpu.SemaphoreType.DMA((48,)),
        ],
        compiler_params=pltpu.CompilerParams(
            collective_id=2, has_side_effects=True, vmem_limit_bytes=48 * 1024 * 1024
        ),
        cost_estimate=pl.CostEstimate(
            flops=2_000_000_000, bytes_accessed=4_000_000, transcendentals=0
        ),
    )(tokens, weight, bias, meta)


def shards(
    section_input,
    attention_gain,
    query_key_value_weight,
    qkv_bias,
    out_weight,
    out_bias,
    attention_sink_logits,
    expert_gain,
    gate_up_weight,
    down_weight,
    expert_ids,
    gate_logits,
    placement,
):
    count_of_rows = section_input.shape[1]
    experts_count = placement.shape[1]
    slots = 2 * min(count_of_rows // 2, count_of_rows * TOP * 5 // (8 * experts_count))
    offset = lax.axis_index("expert") * count_of_rows
    query_group_width = QUERY_HEADS // KEY_VALUE_HEADS
    state = section_input[0]
    normed_in = normed(state, attention_gain[0])
    meta, chosen = routing_tables(expert_ids[0], gate_logits[0], placement[0])
    depth = query_key_value_weight.shape[1]
    projected_rows, rim_rows, tables = project(
        normed_in.T.reshape(SIDE, SIDE, depth, count_of_rows), query_key_value_weight[0], qkv_bias, meta
    )
    query_rows = projected_rows[:, : QUERY_HEADS * HEAD_DIM].reshape(
        count_of_rows, KEY_VALUE_HEADS, query_group_width, HEAD_DIM
    )
    key_value = projected_rows[:, QUERY_HEADS * HEAD_DIM :]
    rows_in_window = jnp.concatenate([rim_rows, key_value], 0)
    key_row_slice = rows_in_window[:, : KEY_VALUE_HEADS * HEAD_DIM].reshape(
        WINDOW_TOKENS + count_of_rows, KEY_VALUE_HEADS, HEAD_DIM
    )
    value_row_slice = rows_in_window[:, KEY_VALUE_HEADS * HEAD_DIM :].reshape(
        WINDOW_TOKENS + count_of_rows, KEY_VALUE_HEADS, HEAD_DIM
    )
    scores = (
        jnp.einsum("ikgd,jkd->kgij", query_rows, key_row_slice, preferred_element_type=jnp.float32)
        * 0.125
    )
    query_pos = offset + jnp.arange(count_of_rows, dtype=jnp.int32)
    key_pos = offset - WINDOW_TOKENS + jnp.arange(WINDOW_TOKENS + count_of_rows, dtype=jnp.int32)
    distance = query_pos[:, None] - key_pos[None, :]
    inside = (distance >= 0) & (distance < WINDOW_TOKENS) & (key_pos >= 0)[None, :]
    head_sink_logit = attention_sink_logits[0].reshape(KEY_VALUE_HEADS, query_group_width)[
        :, :, None
    ]
    masked = jnp.where(inside, scores, -1e30)
    peak = jnp.maximum(jnp.max(masked, axis=-1), head_sink_logit)
    numer = jnp.where(inside, jnp.exp(masked - peak[..., None]), 0.0)
    denominator = jnp.sum(numer, axis=-1) + jnp.exp(head_sink_logit - peak)
    attention = (numer / denominator[..., None]).astype(jnp.bfloat16)
    mixed = jnp.einsum(
        "kgij,jkd->ikgd", attention, value_row_slice, preferred_element_type=jnp.float32
    )
    attended = mixed.astype(jnp.bfloat16).reshape(count_of_rows, QUERY_HEADS * HEAD_DIM)
    residual = (
        state.astype(jnp.float32)
        + jnp.dot(attended, out_weight[0], preferred_element_type=jnp.float32)
        + out_bias[0]
    ).astype(jnp.bfloat16)
    normed_mid = normed(residual, expert_gain[0])
    moved = experts_and_pass(
        normed_mid, residual, tables, chosen, gate_up_weight[0, 0].T, down_weight[0, 0], slots
    )
    return moved[None]


def solution(mesh):
    return jax.shard_map(
        shards,
        mesh=mesh,
        in_specs=(
            P("section", "expert", None),
            P("section", None),
            P("section", "expert", None),
            P("section", None),
            P("section", None, None),
            P("section", None),
            P("section", None),
            P("section", None),
            P("section", "expert", None, None),
            P("section", "expert", None, None),
            P("section", "expert", None),
            P("section", "expert", None),
            P("section", None),
        ),
        out_specs=P("section", "expert", None),
        check_vma=False,
    )
```

```python
import functools

import jax
import jax.numpy as jnp
from jax import lax
from jax.experimental import pallas as pl
from jax.experimental.pallas import tpu as pltpu
from jax.sharding import PartitionSpec as P

HEAD_DIM = 64
QUERY_HEADS = 32
KEY_VALUE_HEADS = 4
TOP = 4
SIDE = 4
MESH = pl.DeviceIdType.MESH
F32 = jnp.float32
BF16 = jnp.bfloat16


class Links:
    def __init__(self, send, recv):
        self.send, self.recv = send, recv
        self.keys, self.started, self.done = {}, [], set()
        self.made = {}
        self.section = lax.axis_index("section")
        me = lax.axis_index("expert")
        self.x, self.z = me // SIDE, me % SIDE

    def neighbour(self, axis, step):
        if axis == 3:
            return (self.section, (self.x * SIDE + self.z + step + 16) % 16)
        if axis == 2:
            return ((self.section + step + 8) % 8, self.x * SIDE + self.z)
        if axis == 0:
            return (self.section, ((self.x + step + SIDE) % SIDE) * SIDE + self.z)
        return (self.section, self.x * SIDE + (self.z + step + SIDE) % SIDE)

    def barrier(self, partners):
        sem = pltpu.get_barrier_semaphore()
        for axis, step in partners:
            pl.semaphore_signal(
                sem, inc=1, device_id=self.neighbour(axis, step), device_id_type=MESH
            )
        pl.semaphore_wait(sem, len(partners))

    def start(self, name, src, dst, axis, step):
        key = self.keys.setdefault(name, len(self.keys))
        copy = pltpu.make_async_remote_copy(
            src_ref=src(),
            dst_ref=dst(),
            send_sem=self.send.at[key],
            recv_sem=self.recv.at[key],
            device_id=self.neighbour(axis, step),
            device_id_type=MESH,
        )
        copy.start()
        self.made[name] = (src, dst, axis, step)

    def remake(self, name):
        src, dst, axis, step = self.made[name]
        key = self.keys[name]
        return pltpu.make_async_remote_copy(
            src_ref=src(),
            dst_ref=dst(),
            send_sem=self.send.at[key],
            recv_sem=self.recv.at[key],
            device_id=self.neighbour(axis, step),
            device_id_type=MESH,
        )

    def need(self, *names):
        for name in names:
            if name not in self.done:
                self.done.add(name)
                self.remake(name).wait_recv()

    def finish(self):
        for name in self.made:
            self.need(name)
            self.remake(name).wait_send()


def of_four(g, values):
    a, b, c, d = values
    return (
        b * (g * (g - 2) * (g - 3)) // 2
        - c * (g * (g - 1) * (g - 3)) // 2
        + d * (g * (g - 1) * (g - 2)) // 6
        - a * ((g - 1) * (g - 2) * (g - 3)) // 6
    )


def add_rows(dst, *parts):
    step = 16

    def body(i, carry):
        rows = pl.ds(pl.multiple_of(i * step, step), step)
        total = parts[0][rows].astype(F32)
        for part in parts[1:]:
            total = total + part[rows].astype(F32)
        dst[rows] = total.astype(dst.dtype)
        return carry

    lax.fori_loop(0, dst.shape[0] // step, body, 0)


def view(ref, *index):
    return lambda: ref.at[index]


def across(rows, other):
    return lax.dot_general(rows, other, (((1,), (1,)), ((), ())), preferred_element_type=F32)


def along(first, second):
    return lax.dot_general(first, second, (((0,), (0,)), ((), ())), preferred_element_type=F32)


def chunks(total, size):
    return [(at, min(size, total - at)) for at in range(0, total, size)]


def expert_kernel(
    slots,
    normed_ref,
    residual_ref,
    meta_ref,
    holders_ref,
    gate_up_hbm,
    down_hbm,
    out_ref,
    tokens,
    parts,
    gate_up,
    down,
    packed,
    act,
    picks,
    half_in,
    full_in,
    half_last,
    full_last,
    local_sem,
    send_sem,
    recv_sem,
):
    half_rows = tokens.shape[2] // 2
    quarter = half_rows // 2
    width = tokens.shape[3]
    inner = act.shape[1]
    net = Links(send_sem, recv_sem)
    load_tokens = pltpu.make_async_copy(normed_ref, tokens.at[0, 0], local_sem.at[0])
    load_gate_up = pltpu.make_async_copy(gate_up_hbm, gate_up, local_sem.at[1])
    load_down = pltpu.make_async_copy(down_hbm, down, local_sem.at[2])
    load_tokens.start()
    net.barrier([(0, 1), (0, -1), (1, 1), (1, -1), (2, 1), (2, -1)])

    load_tokens.wait()
    load_gate_up.start()
    load_down.start()

    def block(which, dp, dq, at, size):
        first, second = (dp, dq) if which == 0 else (dq, dp)
        rows = slice(which * half_rows + at, which * half_rows + at + size)
        return lambda: tokens.at[first, second, rows]

    def part(which, dp, dq, at, size):
        first, second = (dp, dq) if which == 0 else (dq, dp)
        rows = slice(which * half_rows + at, which * half_rows + at + size)
        return lambda: parts.at[first, second, rows]

    def own(which, axis, step):
        to = (-step) % SIDE
        place = (to, 0) if axis == which else (0, to)
        name = ("op" if axis == which else "oq", which, step)
        net.start(
            name,
            block(which, 0, 0, 0, half_rows),
            block(which, *place, 0, half_rows),
            axis,
            step,
        )

    for axis in (0, 1):
        for step in (1, -1):
            own(axis, axis, step)
    for axis in (0, 1):
        for step in (1, -1):
            own(1 - axis, axis, step)

    def at_of(step):
        return 0 if step == 1 else quarter

    def on_across(which, dp, dq_axis_step):
        step = dq_axis_step
        net.start(
            ("pq", which, dp, step),
            block(which, dp, 0, 0, half_rows),
            block(which, dp, (-step) % SIDE, 0, half_rows),
            1 - which,
            step,
        )

    def first_hops():
        for step in (1, -1):
            for which in (0, 1):
                dp = (-step) % SIDE
                net.need(("op", which, step))
                net.start(
                    ("fp", which, step),
                    block(which, dp, 0, at_of(step), quarter),
                    block(which, 2, 0, at_of(step), quarter),
                    which,
                    step,
                )
        for which in (0, 1):
            on_across(which, 3, 1)
            on_across(which, 3, -1)

    def other_hops():
        for which in (0, 1):
            on_across(which, 1, 1)
            on_across(which, 1, -1)

    def far_hops():
        for half in (1, -1):
            for which in (0, 1):
                net.need(("fp", which, half))
                for step in (1, -1):
                    net.start(
                        ("pq2", which, half, step),
                        block(which, 2, 0, at_of(half), quarter),
                        block(which, 2, (-step) % SIDE, at_of(half), quarter),
                        1 - which,
                        step,
                    )

    def second_hops(dp):
        for step in (1, -1):
            for which in (0, 1):
                if dp == 0:
                    net.need(("oq", which, step))
                elif dp == 2:
                    net.need(("pq2", which, step, step))
                else:
                    net.need(("pq", which, dp, step))
                net.start(
                    ("fq", which, dp, step),
                    block(which, dp, (-step) % SIDE, at_of(step), quarter),
                    block(which, dp, 2, at_of(step), quarter),
                    1 - which,
                    step,
                )

    def arrived(blocks):
        for dx, dz in blocks:
            for which in (0, 1):
                dp, dq = (dx, dz) if which == 0 else (dz, dx)
                step = {1: -1, 3: 1}
                if dq == 0:
                    if dp in step:
                        net.need(("op", which, step[dp]))
                    elif dp == 2:
                        net.need(("fp", which, 1), ("fp", which, -1))
                elif dq == 2:
                    net.need(("fq", which, dp, 1), ("fq", which, dp, -1))
                elif dp == 0:
                    net.need(("oq", which, step[dq]))
                elif dp == 2:
                    net.need(("pq2", which, 1, step[dq]), ("pq2", which, -1, step[dq]))
                else:
                    net.need(("pq", which, dp, step[dq]))

    groups = (
        ((0, 0), (1, 0), (3, 0), (0, 1)),
        ((0, 3), (0, 2), (2, 0), (3, 3)),
        ((1, 1), (1, 3), (3, 1), (3, 2)),
        ((2, 3), (1, 2), (2, 1), (2, 2)),
    )

    def stage(at):
        if at == 0:
            first_hops()
            second_hops(0)
            other_hops()
            load_gate_up.wait()
            load_down.wait()
        elif at == 1:
            far_hops()
            second_hops(3)
        elif at == 2:
            second_hops(1)
            second_hops(2)
            back(0)
        else:
            relay(0)
        arrived(groups[at])

    def relay(dp):
        for which in (0, 1):
            for side, step in ((0, 1), (1, -1)):
                net.need(("rh", which, dp, step))
                there = part(which, dp, step % SIDE, at_of(step), quarter)
                add_rows(there(), there(), half_in.at[which, dp, side])
                net.start(
                    ("rf", which, dp, step),
                    part(which, dp, step % SIDE, 0, half_rows),
                    view(full_in, which, dp, side),
                    1 - which,
                    step,
                )

    def back(dp):
        for which in (0, 1):
            for side, step in ((0, 1), (1, -1)):
                net.start(
                    ("rh", which, dp, step),
                    part(which, dp, 2, at_of(step), quarter),
                    view(half_in, which, dp, side),
                    1 - which,
                    step,
                )

    before = lax.broadcasted_iota(jnp.int32, (128, 128), 0)
    after = lax.broadcasted_iota(jnp.int32, (128, 128), 1)
    earlier = jnp.where(before < after, 1.0, 0.0).astype(BF16)
    slot = lax.broadcasted_iota(jnp.int32, (slots, 128), 0).astype(F32)

    pair = lax.axis_index("expert") // 2
    at_pair = lax.broadcasted_iota(jnp.int32, (1, 8), 1) == pair
    mine = jnp.sum(jnp.where(at_pair, holders_ref[...], 0), axis=1, keepdims=True)
    chosen = jnp.where(lax.broadcasted_iota(jnp.int32, (8, 128), 0) == mine, 1.0, 0.0)

    def group(g, carry):
        for at in range(SIDE):
            pl.when(g == at)(functools.partial(stage, at))
        places = [[of_four(g, [group[k][axis] for group in groups]) for axis in (0, 1)] for k in range(SIDE)]
        scales = []
        for k, (dx, dz) in enumerate(places):
            table = meta_ref[dz, dx]
            member = jnp.sum(table[0:8] * chosen, axis=0, keepdims=True)
            weight = jnp.sum(table[8:16] * chosen, axis=0, keepdims=True)
            wide = jnp.broadcast_to(member, (16, 128)).astype(BF16)
            rank = jnp.dot(wide, earlier, preferred_element_type=F32)[0:1]
            hit = (slot == rank) & (member > 0.5)
            pick = jnp.where(hit, 1.0, 0.0).astype(BF16)
            scales.append(jnp.sum(jnp.where(hit, weight, 0.0), axis=1, keepdims=True))
            picks[k] = pick
            for at, size in chunks(width, 1024):
                packed[k * slots : (k + 1) * slots, at : at + size] = jnp.dot(
                    pick, tokens[dx, dz, :, at : at + size], preferred_element_type=F32
                ).astype(BF16)
        scale = jnp.concatenate(scales, axis=0)
        for at, size in chunks(inner, 256):
            gate = across(packed[...], gate_up[at : at + size])
            up = across(packed[...], gate_up[inner + at : inner + at + size])
            act[:, at : at + size] = (
                (up + 1.0) * gate * jax.nn.sigmoid(1.702 * gate)
            ).astype(BF16)
        for at, size in chunks(width, 640):
            tile = jnp.dot(act[...], down[:, at : at + size], preferred_element_type=F32)
            tile = (tile * scale).astype(BF16)
            for k, (dx, dz) in enumerate(places):
                parts[dx, dz, :, at : at + size] = along(
                    picks[k], tile[k * slots : (k + 1) * slots]
                ).astype(BF16)
        return carry

    lax.fori_loop(0, SIDE, group, 0)

    for dp in (2, 1, 3):
        back(dp)

    def gather_in(dp):
        for which in (0, 1):
            net.need(("rf", which, dp, 1), ("rf", which, dp, -1))
            here = part(which, dp, 0, 0, half_rows)
            add_rows(here(), here(), full_in.at[which, dp, 0], full_in.at[which, dp, 1])

    def last_half(which):
        for side, step in ((0, 1), (1, -1)):
            net.start(
                ("lh", which, step),
                part(which, 2, 0, at_of(step), quarter),
                view(half_last, which, side),
                which,
                step,
            )

    def last_full(step):
        side = (1 - step) // 2
        for which in (0, 1):
            net.need(("lh", which, step))
            there = part(which, step % SIDE, 0, at_of(step), quarter)
            add_rows(there(), there(), half_last.at[which, side])
            for piece in (0, 1):
                rows = slice(piece * quarter, (piece + 1) * quarter)
                net.start(
                    ("lf", which, step, piece),
                    part(which, step % SIDE, 0, piece * quarter, quarter),
                    view(full_last, which, side, rows),
                    which,
                    step,
                )

    relay(2)
    relay(1)
    gather_in(2)
    last_half(0)
    last_half(1)
    relay(3)
    gather_in(1)
    last_full(1)
    gather_in(3)
    last_full(-1)
    for which in (0, 1):
        net.need(("rf", which, 0, 1), ("rf", which, 0, -1))
    for piece in (0, 1):
        for which in (0, 1):
            net.need(("lf", which, 1, piece), ("lf", which, -1, piece))
            here = part(which, 0, 0, piece * quarter, quarter)
            inside = slice(piece * quarter, (piece + 1) * quarter)
            at = which * half_rows + piece * quarter
            rows = slice(at, at + quarter)
            add_rows(
                here(),
                here(),
                full_in.at[which, 0, 0, inside],
                full_in.at[which, 0, 1, inside],
                full_last.at[which, 0, inside],
                full_last.at[which, 1, inside],
                residual_ref.at[rows],
            )
            net.start(("out", which, piece), here, view(out_ref, rows), 2, 1)
    net.finish()


def experts_and_pass(normed_mid, residual, meta, holders, gate_up, down, slots):
    rows, width = normed_mid.shape
    inner = down.shape[0]
    anywhere = pl.BlockSpec(memory_space=pl.ANY)
    vmem = pl.BlockSpec(memory_space=pltpu.VMEM)
    half, quarter = rows // 2, rows // 4
    return pl.pallas_call(
        functools.partial(expert_kernel, slots),
        out_shape=jax.ShapeDtypeStruct((rows, width), BF16),
        in_specs=[anywhere, vmem, vmem, vmem, anywhere, anywhere],
        out_specs=anywhere,
        scratch_shapes=[
            pltpu.VMEM((SIDE, SIDE, rows, width), BF16),
            pltpu.VMEM((SIDE, SIDE, rows, width), BF16),
            pltpu.VMEM(gate_up.shape, BF16),
            pltpu.VMEM(down.shape, BF16),
            pltpu.VMEM((SIDE * slots, width), BF16),
            pltpu.VMEM((SIDE * slots, inner), BF16),
            pltpu.VMEM((SIDE, slots, rows), BF16),
            pltpu.VMEM((2, SIDE, 2, quarter, width), BF16),
            pltpu.VMEM((2, SIDE, 2, half, width), BF16),
            pltpu.VMEM((2, 2, quarter, width), BF16),
            pltpu.VMEM((2, 2, half, width), BF16),
            pltpu.SemaphoreType.DMA((3,)),
            pltpu.SemaphoreType.DMA((96,)),
            pltpu.SemaphoreType.DMA((96,)),
        ],
        compiler_params=pltpu.CompilerParams(
            collective_id=1, has_side_effects=True, vmem_limit_bytes=62 * 1024 * 1024
        ),
        cost_estimate=pl.CostEstimate(
            flops=16_000_000_000, bytes_accessed=16_000_000, transcendentals=1_000_000
        ),
    )(normed_mid, residual, meta, holders, gate_up, down)


def routing_tables(ids, logits):
    kinds = lax.broadcasted_iota(jnp.int32, (8, ids.shape[1]), 0)
    grown = jnp.exp(logits - jnp.max(logits, axis=0, keepdims=True))
    weights = grown / jnp.sum(grown, axis=0, keepdims=True)
    member, weight = jnp.zeros(kinds.shape, F32), jnp.zeros(kinds.shape, F32)
    for k in range(TOP):
        equal = kinds == ids[k : k + 1]
        member = member + jnp.where(equal, 1.0, 0.0)
        weight = weight + jnp.where(equal, weights[k : k + 1], 0.0)
    return member, weight


def attend(projected, behind, sinks_ref, attended, first):
    rows = projected.shape[0]
    pair = 2 * HEAD_DIM
    group = QUERY_HEADS // KEY_VALUE_HEADS
    row = lax.broadcasted_iota(jnp.int32, (rows, rows), 0)
    lane = lax.broadcasted_iota(jnp.int32, (rows, rows), 1)
    low = lax.broadcasted_iota(jnp.int32, (rows, pair), 1) < HEAD_DIM
    older = row > lane
    scale = jnp.where(first, 0.0, 0.125)
    offset = jnp.where(first, -1e30, 0.0)
    keys_at = QUERY_HEADS * HEAD_DIM
    values_at = keys_at + KEY_VALUE_HEADS * HEAD_DIM
    for g in range(KEY_VALUE_HEADS):
        tile = g // 2 * pair
        stacked = []
        own = projected[:, keys_at + tile : keys_at + tile + pair].astype(F32)
        rim = behind[:, tile : tile + pair].astype(F32)
        for side in (0, 1):
            for keys in (rim, own):
                placed = keys if g % 2 == side else pltpu.roll(keys, HEAD_DIM, 1)
                stacked.append(jnp.where(low if side == 0 else ~low, placed, 0.0).astype(BF16))
        keys = jnp.concatenate(stacked, axis=0)
        at = values_at + tile
        values = jnp.concatenate(
            [
                behind[:, KEY_VALUE_HEADS * HEAD_DIM + tile : KEY_VALUE_HEADS * HEAD_DIM + tile + pair],
                projected[:, at : at + pair],
            ],
            axis=0,
        ).astype(F32)
        values = values.T[g % 2 * HEAD_DIM : (g % 2 + 1) * HEAD_DIM].astype(BF16)
        for head in range(g * group, (g + 1) * group, 2):
            scores = across(keys, projected[:, head * HEAD_DIM : head * HEAD_DIM + pair])
            for side in (0, 1):
                past = scores[2 * side * rows : (2 * side + 1) * rows]
                here = scores[(2 * side + 1) * rows : (2 * side + 2) * rows]
                merged = jnp.where(older, past * scale + offset, here * 0.125)
                sink = sinks_ref[0, head + side]
                peak = jnp.maximum(jnp.max(merged, axis=0, keepdims=True), sink)
                numer = jnp.exp(merged - peak)
                denominator = jnp.sum(numer, axis=0, keepdims=True) + jnp.exp(sink - peak)
                share = numer * (1.0 / denominator)
                both = jnp.concatenate(
                    [jnp.where(older, share, 0.0), jnp.where(older, 0.0, share)], axis=0
                ).astype(BF16)
                attended[(head + side) * HEAD_DIM : (head + side + 1) * HEAD_DIM] = jnp.dot(
                    values, both, preferred_element_type=F32
                ).astype(BF16)


def project_kernel(
    pieces_ref,
    gains_ref,
    state_ref,
    weight_hbm,
    bias_ref,
    ids_ref,
    logits_ref,
    sinks_ref,
    out_weight_hbm,
    out_bias_ref,
    mid_gain_ref,
    normed_ref,
    residual_ref,
    tables_ref,
    projected_ref,
    tokens_ref,
    out_weight,
    attended,
    weight,
    slices,
    transit,
    total,
    sent,
    half_in,
    full_in,
    behind,
    tables,
    local_sem,
    send_sem,
    recv_sem,
):
    net = Links(send_sem, recv_sem)
    columns = weight.shape[3]
    middle = columns // 2
    rows = projected_ref.shape[0]
    loads = [
        pltpu.make_async_copy(
            weight_hbm.at[:, pl.ds(which * columns, columns)], weight.at[which, 0], local_sem.at[which]
        )
        for which in (0, 1)
    ]
    for load in loads:
        load.start()
    load_out = pltpu.make_async_copy(out_weight_hbm, out_weight, local_sem.at[4])
    load_out.start()
    member, gate_weight = routing_tables(ids_ref[...], logits_ref[...])
    tables[0, 0, 0:8] = member
    tables[0, 0, 8:16] = gate_weight
    place = (net.x, net.z)
    features = state_ref.shape[0]

    def for_device(which, step, at, size):
        to = (place[1 - which] + step + SIDE) % SIDE
        pieces = slice(at, at + size)
        if which == 0:
            return lambda: tokens_ref.at[pieces, to]
        return lambda: tokens_ref.at[to, pieces]

    def kept(which, dq, at, size):
        lanes = slice(dq * rows, (dq + 1) * rows)
        pieces = slice(at, at + size)
        return lambda: slices.at[which, pieces, :, lanes]

    net.barrier([(0, 1), (0, -1), (1, 1), (1, -1), (3, 1), (3, -1)])
    steps = ((0, 1), (1, -1))
    net.start(("mx", 1), view(tables, 0, 0), view(tables, 0, 3), 0, 1)
    net.start(("mx", -1), view(tables, 0, 0), view(tables, 0, 1), 0, -1)
    for which in (0, 1):
        loads[which].wait()
        for side, step in steps:
            net.start(
                ("wo", which, step),
                view(weight, which, 0),
                view(weight, which, (-step) % SIDE),
                which,
                step,
            )
    squares = jnp.zeros(pieces_ref.shape[2:], F32)
    for a in range(SIDE):
        for b in range(SIDE):
            piece = pieces_ref[a, b].astype(F32)
            squares = squares + piece * piece
    inverse = lax.rsqrt(jnp.sum(squares, axis=0, keepdims=True) / features + 1e-05)
    for a in range(SIDE):
        for b in range(SIDE):
            piece = pieces_ref[a, b].astype(F32)
            tokens_ref[a, b] = (piece * inverse * gains_ref[a, b]).astype(BF16)
    stays = [
        pltpu.make_async_copy(
            for_device(which, 0, 0, SIDE)(), kept(which, 0, 0, SIDE)(), local_sem.at[2 + which]
        )
        for which in (0, 1)
    ]
    for stay in stays:
        stay.start()
    for which in (0, 1):
        for side, step in steps:
            net.start(
                ("tt", which, step),
                for_device(which, 2, side * 2, 2),
                view(transit, which, side),
                1 - which,
                step,
            )
    for which in (0, 1):
        for side, step in steps:
            net.start(
                ("ta", which, step),
                for_device(which, step, 0, SIDE),
                kept(which, (-step) % SIDE, 0, SIDE),
                1 - which,
                step,
            )
    net.need(("mx", 1))
    net.start(("mf", 0), view(tables, 0, 3), view(tables, 0, 2), 0, 1)
    for which in (0, 1):
        for side, step in steps:
            net.need(("tt", which, step))
            net.start(
                ("tf", which, step),
                view(transit, which, side),
                kept(which, 2, side * 2, 2),
                1 - which,
                step,
            )
    net.need(("mx", -1), ("mf", 0))
    net.start(("mz", 1), view(tables, 0), view(tables, 3), 1, 1)
    net.start(("mz", -1), view(tables, 0), view(tables, 1), 1, -1)

    def multiply(which, dp):
        piece = (place[which] + dp) % SIDE
        lhs = slices[which, piece]
        for at, size in chunks(columns, 640):
            term = along(lhs, weight[which, dp, :, at : at + size])
            if dp == 0:
                total[which, :, at : at + size] = term
            else:
                total[which, :, at : at + size] += term

    def pass_on(which, step):
        net.need(("wo", which, step))
        part = slice(0, middle) if step == 1 else slice(middle, columns)
        net.start(
            ("wf", which, step),
            lambda: weight.at[which, (-step) % SIDE, :, part],
            lambda: weight.at[which, 2, :, part],
            which,
            step,
        )

    for which in (0, 1):
        stays[which].wait()
        net.need(("ta", which, 1), ("ta", which, -1), ("tf", which, 1), ("tf", which, -1))
    for which in (0, 1):
        multiply(which, 0)
    for step in (1, -1):
        for which in (0, 1):
            pass_on(which, step)
    net.need(("mz", 1), ("mz", -1))
    net.start(("mg", 0), view(tables, 3), view(tables, 2), 1, 1)
    for dp in (3, 1):
        for which in (0, 1):
            multiply(which, dp)
    for which in (1, 0):
        net.need(("wf", which, 1), ("wf", which, -1))
        multiply(which, 2)
        sent[which, 2] = total[which, 2 * rows : 3 * rows].astype(BF16)
        for side, step in steps:
            part = slice(side * middle, (side + 1) * middle)
            net.start(
                ("rh", which, step),
                view(sent, which, 2, slice(None), part),
                view(half_in, which, side),
                1 - which,
                step,
            )
    for which in (1, 0):
        for side, step in steps:
            dq = step % SIDE
            mine = slice(dq * rows, (dq + 1) * rows)
            part = slice(side * middle, (side + 1) * middle)
            other = slice((1 - side) * middle, (2 - side) * middle)
            sent[which, dq, :, other] = total[which, mine, other].astype(BF16)
            net.need(("rh", which, step))
            sent[which, dq, :, part] = (
                total[which, mine, part] + half_in[which, side].astype(F32)
            ).astype(BF16)
            net.start(
                ("rf", which, step),
                view(sent, which, dq),
                view(full_in, which, side),
                1 - which,
                step,
            )
    for which in (1, 0):
        net.need(("rf", which, 1), ("rf", which, -1))
        lanes = slice(which * columns, (which + 1) * columns)
        projected_ref[:, lanes] = (
            total[which, 0:rows]
            + full_in[which, 0].astype(F32)
            + full_in[which, 1].astype(F32)
            + bias_ref[:, lanes]
        ).astype(BF16)
        if which == 1:
            keys = slice(2 * columns - behind.shape[1], 2 * columns)
            net.start(
                ("kv", 0), view(projected_ref, slice(None), keys), view(behind), 3, 1
            )
    net.finish()
    tables_ref[...] = tables[...]
    attend(projected_ref, behind, sinks_ref, attended, net.x * SIDE + net.z == 0)
    load_out.wait()
    squares = jnp.zeros((rows, 1), F32)
    for at, size in chunks(features, 640):
        lanes = slice(at, at + size)
        mixed = jnp.dot(out_weight[lanes], attended[...], preferred_element_type=F32)
        mixed = mixed + state_ref[lanes].astype(F32)
        kept_sum = (mixed.T + out_bias_ref[:, lanes]).astype(BF16)
        residual_ref[:, lanes] = kept_sum
        wide = kept_sum.astype(F32)
        squares = squares + jnp.sum(wide * wide, axis=1, keepdims=True)
    inverse = lax.rsqrt(squares / features + 1e-05)
    for at, size in chunks(features, 640):
        lanes = slice(at, at + size)
        wide = residual_ref[:, lanes].astype(F32)
        normed_ref[:, lanes] = (wide * inverse * mid_gain_ref[:, lanes]).astype(BF16)


def attention_part(pieces, gains, state, weight, bias, ids, logits, sinks, out_weight, out_bias, mid_gain):
    features, rows = state.shape
    depth = pieces.shape[2]
    wide = weight.shape[1]
    columns = wide // 2
    keys = 2 * KEY_VALUE_HEADS * HEAD_DIM
    anywhere = pl.BlockSpec(memory_space=pl.ANY)
    vmem = pl.BlockSpec(memory_space=pltpu.VMEM)
    return pl.pallas_call(
        project_kernel,
        out_shape=(
            jax.ShapeDtypeStruct((rows, features), BF16),
            jax.ShapeDtypeStruct((rows, features), BF16),
            jax.ShapeDtypeStruct((SIDE, SIDE, 16, rows), F32),
        ),
        in_specs=[
            vmem,
            vmem,
            vmem,
            anywhere,
            vmem,
            vmem,
            vmem,
            pl.BlockSpec(memory_space=pltpu.SMEM),
            anywhere,
            vmem,
            vmem,
        ],
        out_specs=(vmem, vmem, vmem),
        scratch_shapes=[
            pltpu.VMEM((rows, wide), BF16),
            pltpu.VMEM(pieces.shape, BF16),
            pltpu.VMEM(out_weight.shape, BF16),
            pltpu.VMEM((QUERY_HEADS * HEAD_DIM, rows), BF16),
            pltpu.VMEM((2, SIDE, depth, columns), BF16),
            pltpu.VMEM((2, SIDE, depth, SIDE * rows), BF16),
            pltpu.VMEM((2, 2, 2, depth, rows), BF16),
            pltpu.VMEM((2, SIDE * rows, columns), F32),
            pltpu.VMEM((2, SIDE, rows, columns), BF16),
            pltpu.VMEM((2, 2, rows, columns // 2), BF16),
            pltpu.VMEM((2, 2, rows, columns), BF16),
            pltpu.VMEM((rows, keys), BF16),
            pltpu.VMEM((SIDE, SIDE, 16, rows), F32),
            pltpu.SemaphoreType.DMA((5,)),
            pltpu.SemaphoreType.DMA((48,)),
            pltpu.SemaphoreType.DMA((48,)),
        ],
        compiler_params=pltpu.CompilerParams(
            collective_id=2, has_side_effects=True, vmem_limit_bytes=56 * 1024 * 1024
        ),
        cost_estimate=pl.CostEstimate(
            flops=2_000_000_000, bytes_accessed=4_000_000, transcendentals=0
        ),
    )(pieces, gains, state, weight, bias, ids, logits, sinks, out_weight, out_bias, mid_gain)


def shards(
    section_input,
    attention_gain,
    query_key_value_weight,
    qkv_bias,
    out_weight,
    out_bias,
    attention_sink_logits,
    expert_gain,
    gate_up_weight,
    down_weight,
    expert_ids,
    gate_logits,
    placement,
):
    rows, features = section_input.shape[1:]
    experts = placement.shape[1]
    slots = 2 * min(rows // 2, rows * TOP * 5 // (8 * experts))
    depth = query_key_value_weight.shape[1]
    state = section_input[0].T
    apart = (SIDE, SIDE, depth, rows)
    normed_mid, residual, tables = attention_part(
        state.reshape(apart),
        jnp.broadcast_to(attention_gain[0].reshape(apart[:3])[..., None], apart),
        state,
        query_key_value_weight[0],
        qkv_bias,
        expert_ids[0].T,
        gate_logits[0].T,
        attention_sink_logits,
        out_weight[0].T,
        out_bias,
        expert_gain,
    )
    moved = experts_and_pass(
        normed_mid, residual, tables, placement, gate_up_weight[0, 0].T, down_weight[0, 0], slots
    )
    return moved[None]


def solution(mesh):
    return jax.shard_map(
        shards,
        mesh=mesh,
        in_specs=(
            P("section", "expert", None),
            P("section", None),
            P("section", "expert", None),
            P("section", None),
            P("section", None, None),
            P("section", None),
            P("section", None),
            P("section", None),
            P("section", "expert", None, None),
            P("section", "expert", None, None),
            P("section", "expert", None),
            P("section", "expert", None),
            P("section", None),
        ),
        out_specs=P("section", "expert", None),
        check_vma=False,
    )
```

```python
import functools

import jax
import jax.numpy as jnp
from jax import lax
from jax.experimental import pallas as pl
from jax.experimental.pallas import tpu as pltpu
from jax.sharding import PartitionSpec as P

HEAD_DIM = 64
QUERY_HEADS = 32
KEY_VALUE_HEADS = 4
TOP = 4
SIDE = 4
MESH = pl.DeviceIdType.MESH
F32 = jnp.float32
BF16 = jnp.bfloat16


class Links:
    def __init__(self, send, recv):
        self.send, self.recv = send, recv
        self.keys, self.started, self.done = {}, [], set()
        self.made = {}
        self.section = lax.axis_index("section")
        me = lax.axis_index("expert")
        self.x, self.z = me // SIDE, me % SIDE

    def neighbour(self, axis, step):
        if axis == 3:
            return (self.section, (self.x * SIDE + self.z + step + 16) % 16)
        if axis == 2:
            return ((self.section + step + 8) % 8, self.x * SIDE + self.z)
        if axis == 0:
            return (self.section, ((self.x + step + SIDE) % SIDE) * SIDE + self.z)
        return (self.section, self.x * SIDE + (self.z + step + SIDE) % SIDE)

    def barrier(self, partners):
        sem = pltpu.get_barrier_semaphore()
        for axis, step in partners:
            pl.semaphore_signal(
                sem, inc=1, device_id=self.neighbour(axis, step), device_id_type=MESH
            )
        pl.semaphore_wait(sem, len(partners))

    def start(self, name, src, dst, axis, step):
        assert name not in self.made
        key = self.keys.setdefault(name, len(self.keys))
        copy = pltpu.make_async_remote_copy(
            src_ref=src(),
            dst_ref=dst(),
            send_sem=self.send.at[key],
            recv_sem=self.recv.at[key],
            device_id=self.neighbour(axis, step),
            device_id_type=MESH,
        )
        copy.start()
        self.made[name] = (src, dst, axis, step)

    def remake(self, name):
        src, dst, axis, step = self.made[name]
        key = self.keys[name]
        return pltpu.make_async_remote_copy(
            src_ref=src(),
            dst_ref=dst(),
            send_sem=self.send.at[key],
            recv_sem=self.recv.at[key],
            device_id=self.neighbour(axis, step),
            device_id_type=MESH,
        )

    def need(self, *names):
        for name in names:
            if name not in self.done:
                self.done.add(name)
                self.remake(name).wait_recv()

    def finish(self):
        for name in self.made:
            self.need(name)
            self.remake(name).wait_send()


def of_four(g, values):
    a, b, c, d = values
    return (
        b * (g * (g - 2) * (g - 3)) // 2
        - c * (g * (g - 1) * (g - 3)) // 2
        + d * (g * (g - 1) * (g - 2)) // 6
        - a * ((g - 1) * (g - 2) * (g - 3)) // 6
    )


def add_rows(dst, *parts):
    step = 16

    def body(i, carry):
        rows = pl.ds(pl.multiple_of(i * step, step), step)
        total = parts[0][rows].astype(F32)
        for part in parts[1:]:
            total = total + part[rows].astype(F32)
        dst[rows] = total.astype(dst.dtype)
        return carry

    lax.fori_loop(0, dst.shape[0] // step, body, 0)


def view(ref, *index):
    return lambda: ref.at[index]


def across(rows, other):
    return lax.dot_general(rows, other, (((1,), (1,)), ((), ())), preferred_element_type=F32)


def along(first, second):
    return lax.dot_general(first, second, (((0,), (0,)), ((), ())), preferred_element_type=F32)


def chunks(total, size):
    return [(at, min(size, total - at)) for at in range(0, total, size)]


def expert_kernel(
    slots,
    normed_ref,
    residual_ref,
    meta_ref,
    holders_ref,
    gate_up_hbm,
    down_hbm,
    out_ref,
    tokens,
    parts,
    gate_up,
    down,
    packed,
    act,
    picks,
    half_in,
    full_in,
    half_last,
    full_last,
    local_sem,
    send_sem,
    recv_sem,
):
    half_rows = tokens.shape[2] // 2
    quarter = half_rows // 2
    width = tokens.shape[3]
    inner = act.shape[1]
    net = Links(send_sem, recv_sem)
    load_tokens = pltpu.make_async_copy(normed_ref, tokens.at[0, 0], local_sem.at[0])
    load_gate_up = pltpu.make_async_copy(gate_up_hbm, gate_up, local_sem.at[1])
    load_down = pltpu.make_async_copy(down_hbm, down, local_sem.at[2])
    load_tokens.start()
    net.barrier([(0, 1), (0, -1), (1, 1), (1, -1), (2, 1), (2, -1)])

    load_tokens.wait()
    load_gate_up.start()
    load_down.start()

    def block(which, dp, dq, at, size):
        first, second = (dp, dq) if which == 0 else (dq, dp)
        rows = slice(which * half_rows + at, which * half_rows + at + size)
        return lambda: tokens.at[first, second, rows]

    def part(which, dp, dq, at, size):
        first, second = (dp, dq) if which == 0 else (dq, dp)
        rows = slice(which * half_rows + at, which * half_rows + at + size)
        return lambda: parts.at[first, second, rows]

    def own(which, axis, step):
        to = (-step) % SIDE
        place = (to, 0) if axis == which else (0, to)
        name = ("op" if axis == which else "oq", which, step)
        net.start(
            name,
            block(which, 0, 0, 0, half_rows),
            block(which, *place, 0, half_rows),
            axis,
            step,
        )

    for axis in (0, 1):
        for step in (1, -1):
            own(axis, axis, step)
    for axis in (0, 1):
        for step in (1, -1):
            own(1 - axis, axis, step)

    def at_of(step):
        return 0 if step == 1 else quarter

    def on_across(which, dp, dq_axis_step):
        step = dq_axis_step
        net.start(
            ("pq", which, dp, step),
            block(which, dp, 0, 0, half_rows),
            block(which, dp, (-step) % SIDE, 0, half_rows),
            1 - which,
            step,
        )

    def first_hops():
        for step in (1, -1):
            for which in (0, 1):
                dp = (-step) % SIDE
                net.need(("op", which, step))
                net.start(
                    ("fp", which, step),
                    block(which, dp, 0, at_of(step), quarter),
                    block(which, 2, 0, at_of(step), quarter),
                    which,
                    step,
                )
        for which in (0, 1):
            on_across(which, 3, 1)
            on_across(which, 3, -1)

    def other_hops():
        for which in (0, 1):
            on_across(which, 1, 1)
            on_across(which, 1, -1)

    def far_hops():
        for half in (1, -1):
            for which in (0, 1):
                net.need(("fp", which, half))
                for step in (1, -1):
                    net.start(
                        ("pq2", which, half, step),
                        block(which, 2, 0, at_of(half), quarter),
                        block(which, 2, (-step) % SIDE, at_of(half), quarter),
                        1 - which,
                        step,
                    )

    def second_hops(dp):
        for step in (1, -1):
            for which in (0, 1):
                if dp == 0:
                    net.need(("oq", which, step))
                elif dp == 2:
                    net.need(("pq2", which, step, step))
                else:
                    net.need(("pq", which, dp, step))
                net.start(
                    ("fq", which, dp, step),
                    block(which, dp, (-step) % SIDE, at_of(step), quarter),
                    block(which, dp, 2, at_of(step), quarter),
                    1 - which,
                    step,
                )

    def arrived(blocks):
        for dx, dz in blocks:
            for which in (0, 1):
                dp, dq = (dx, dz) if which == 0 else (dz, dx)
                step = {1: -1, 3: 1}
                if dq == 0:
                    if dp in step:
                        net.need(("op", which, step[dp]))
                    elif dp == 2:
                        net.need(("fp", which, 1), ("fp", which, -1))
                elif dq == 2:
                    net.need(("fq", which, dp, 1), ("fq", which, dp, -1))
                elif dp == 0:
                    net.need(("oq", which, step[dq]))
                elif dp == 2:
                    net.need(("pq2", which, 1, step[dq]), ("pq2", which, -1, step[dq]))
                else:
                    net.need(("pq", which, dp, step[dq]))

    groups = (
        ((0, 0), (1, 0), (3, 0), (0, 1)),
        ((0, 3), (0, 2), (2, 0), (3, 3)),
        ((1, 1), (1, 3), (3, 1), (3, 2)),
        ((2, 3), (1, 2), (2, 1), (2, 2)),
    )

    def stage(at):
        if at == 0:
            first_hops()
            second_hops(0)
            other_hops()
            load_gate_up.wait()
            load_down.wait()
        elif at == 1:
            far_hops()
            second_hops(3)
        elif at == 2:
            second_hops(1)
            second_hops(2)
            back(0)
        else:
            relay(0)
        arrived(groups[at])

    def relay(dp):
        for which in (0, 1):
            for side, step in ((0, 1), (1, -1)):
                net.need(("rh", which, dp, step))
                there = part(which, dp, step % SIDE, at_of(step), quarter)
                add_rows(there(), there(), half_in.at[which, dp, side])
                net.start(
                    ("rf", which, dp, step),
                    part(which, dp, step % SIDE, 0, half_rows),
                    view(full_in, which, dp, side),
                    1 - which,
                    step,
                )

    def back(dp):
        for which in (0, 1):
            for side, step in ((0, 1), (1, -1)):
                net.start(
                    ("rh", which, dp, step),
                    part(which, dp, 2, at_of(step), quarter),
                    view(half_in, which, dp, side),
                    1 - which,
                    step,
                )

    before = lax.broadcasted_iota(jnp.int32, (128, 128), 0)
    after = lax.broadcasted_iota(jnp.int32, (128, 128), 1)
    earlier = jnp.where(before < after, 1.0, 0.0).astype(BF16)
    slot = lax.broadcasted_iota(jnp.int32, (slots, 128), 0).astype(F32)

    pair = lax.axis_index("expert") // 2
    at_pair = lax.broadcasted_iota(jnp.int32, (1, 8), 1) == pair
    mine = jnp.sum(jnp.where(at_pair, holders_ref[...], 0), axis=1, keepdims=True)
    chosen = jnp.where(lax.broadcasted_iota(jnp.int32, (8, 128), 0) == mine, 1.0, 0.0)

    def group(g, carry):
        for at in range(SIDE):
            pl.when(g == at)(functools.partial(stage, at))
        places = [[of_four(g, [group[k][axis] for group in groups]) for axis in (0, 1)] for k in range(SIDE)]
        scales = []
        for k, (dx, dz) in enumerate(places):
            table = meta_ref[dz, dx]
            member = jnp.sum(table[0:8] * chosen, axis=0, keepdims=True)
            weight = jnp.sum(table[8:16] * chosen, axis=0, keepdims=True)
            wide = jnp.broadcast_to(member, (16, 128)).astype(BF16)
            rank = jnp.dot(wide, earlier, preferred_element_type=F32)[0:1]
            hit = (slot == rank) & (member > 0.5)
            pick = jnp.where(hit, 1.0, 0.0).astype(BF16)
            scales.append(jnp.sum(jnp.where(hit, weight, 0.0), axis=1, keepdims=True))
            picks[k] = pick
            for at, size in chunks(width, 1024):
                packed[k * slots : (k + 1) * slots, at : at + size] = jnp.dot(
                    pick, tokens[dx, dz, :, at : at + size], preferred_element_type=F32
                ).astype(BF16)
        scale = jnp.concatenate(scales, axis=0)
        for at, size in chunks(inner, 256):
            gate = across(packed[...], gate_up[at : at + size])
            up = across(packed[...], gate_up[inner + at : inner + at + size])
            act[:, at : at + size] = (
                (up + 1.0) * gate * jax.nn.sigmoid(1.702 * gate)
            ).astype(BF16)
        for at, size in chunks(width, 640):
            tile = jnp.dot(act[...], down[:, at : at + size], preferred_element_type=F32)
            tile = (tile * scale).astype(BF16)
            for k, (dx, dz) in enumerate(places):
                parts[dx, dz, :, at : at + size] = along(
                    picks[k], tile[k * slots : (k + 1) * slots]
                ).astype(BF16)
        return carry

    lax.fori_loop(0, SIDE, group, 0)

    for dp in (2, 1, 3):
        back(dp)

    def gather_in(dp):
        for which in (0, 1):
            net.need(("rf", which, dp, 1), ("rf", which, dp, -1))
            here = part(which, dp, 0, 0, half_rows)
            add_rows(here(), here(), full_in.at[which, dp, 0], full_in.at[which, dp, 1])

    def last_half(which):
        for side, step in ((0, 1), (1, -1)):
            net.start(
                ("lh", which, step),
                part(which, 2, 0, at_of(step), quarter),
                view(half_last, which, side),
                which,
                step,
            )

    def last_full(step):
        side = (1 - step) // 2
        for which in (0, 1):
            net.need(("lh", which, step))
            there = part(which, step % SIDE, 0, at_of(step), quarter)
            add_rows(there(), there(), half_last.at[which, side])
            for piece in (0, 1):
                rows = slice(piece * quarter, (piece + 1) * quarter)
                net.start(
                    ("lf", which, step, piece),
                    part(which, step % SIDE, 0, piece * quarter, quarter),
                    view(full_last, which, side, rows),
                    which,
                    step,
                )

    relay(2)
    relay(1)
    gather_in(2)
    last_half(0)
    last_half(1)
    relay(3)
    gather_in(1)
    last_full(1)
    gather_in(3)
    last_full(-1)
    for which in (0, 1):
        net.need(("rf", which, 0, 1), ("rf", which, 0, -1))
    for piece in (0, 1):
        for which in (0, 1):
            net.need(("lf", which, 1, piece), ("lf", which, -1, piece))
            here = part(which, 0, 0, piece * quarter, quarter)
            inside = slice(piece * quarter, (piece + 1) * quarter)
            at = which * half_rows + piece * quarter
            rows = slice(at, at + quarter)
            add_rows(
                here(),
                here(),
                full_in.at[which, 0, 0, inside],
                full_in.at[which, 0, 1, inside],
                full_last.at[which, 0, inside],
                full_last.at[which, 1, inside],
                residual_ref.at[rows],
            )
            net.start(("out", which, piece), here, view(out_ref, rows), 2, 1)
    net.finish()


def experts_and_pass(normed_mid, residual, meta, holders, gate_up, down, slots):
    rows, width = normed_mid.shape
    inner = down.shape[0]
    anywhere = pl.BlockSpec(memory_space=pl.ANY)
    vmem = pl.BlockSpec(memory_space=pltpu.VMEM)
    half, quarter = rows // 2, rows // 4
    return pl.pallas_call(
        functools.partial(expert_kernel, slots),
        out_shape=jax.ShapeDtypeStruct((rows, width), BF16),
        in_specs=[anywhere, vmem, vmem, vmem, anywhere, anywhere],
        out_specs=anywhere,
        scratch_shapes=[
            pltpu.VMEM((SIDE, SIDE, rows, width), BF16),
            pltpu.VMEM((SIDE, SIDE, rows, width), BF16),
            pltpu.VMEM(gate_up.shape, BF16),
            pltpu.VMEM(down.shape, BF16),
            pltpu.VMEM((SIDE * slots, width), BF16),
            pltpu.VMEM((SIDE * slots, inner), BF16),
            pltpu.VMEM((SIDE, slots, rows), BF16),
            pltpu.VMEM((2, SIDE, 2, quarter, width), BF16),
            pltpu.VMEM((2, SIDE, 2, half, width), BF16),
            pltpu.VMEM((2, 2, quarter, width), BF16),
            pltpu.VMEM((2, 2, half, width), BF16),
            pltpu.SemaphoreType.DMA((3,)),
            pltpu.SemaphoreType.DMA((96,)),
            pltpu.SemaphoreType.DMA((96,)),
        ],
        compiler_params=pltpu.CompilerParams(
            collective_id=1, has_side_effects=True, vmem_limit_bytes=62 * 1024 * 1024
        ),
        cost_estimate=pl.CostEstimate(
            flops=16_000_000_000, bytes_accessed=16_000_000, transcendentals=1_000_000
        ),
    )(normed_mid, residual, meta, holders, gate_up, down)


def routing_tables(ids, logits):
    kinds = lax.broadcasted_iota(jnp.int32, (8, ids.shape[1]), 0)
    grown = jnp.exp(logits - jnp.max(logits, axis=0, keepdims=True))
    weights = grown / jnp.sum(grown, axis=0, keepdims=True)
    member, weight = jnp.zeros(kinds.shape, F32), jnp.zeros(kinds.shape, F32)
    for k in range(TOP):
        equal = kinds == ids[k : k + 1]
        member = member + jnp.where(equal, 1.0, 0.0)
        weight = weight + jnp.where(equal, weights[k : k + 1], 0.0)
    return member, weight


def attend(projected, behind, sinks_ref, attended, first):
    rows = projected.shape[0]
    pair = 2 * HEAD_DIM
    group = QUERY_HEADS // KEY_VALUE_HEADS
    row = lax.broadcasted_iota(jnp.int32, (rows, rows), 0)
    lane = lax.broadcasted_iota(jnp.int32, (rows, rows), 1)
    low = lax.broadcasted_iota(jnp.int32, (rows, pair), 1) < HEAD_DIM
    older = row > lane
    scale = jnp.where(first, 0.0, 0.125)
    offset = jnp.where(first, -1e30, 0.0)
    keys_at = QUERY_HEADS * HEAD_DIM
    values_at = keys_at + KEY_VALUE_HEADS * HEAD_DIM
    for g in range(KEY_VALUE_HEADS):
        tile = g // 2 * pair
        stacked = []
        own = projected[:, keys_at + tile : keys_at + tile + pair].astype(F32)
        rim = behind[:, tile : tile + pair].astype(F32)
        for side in (0, 1):
            for keys in (rim, own):
                placed = keys if g % 2 == side else pltpu.roll(keys, HEAD_DIM, 1)
                stacked.append(jnp.where(low if side == 0 else ~low, placed, 0.0).astype(BF16))
        keys = jnp.concatenate(stacked, axis=0)
        at = values_at + tile
        values = jnp.concatenate(
            [
                behind[:, KEY_VALUE_HEADS * HEAD_DIM + tile : KEY_VALUE_HEADS * HEAD_DIM + tile + pair],
                projected[:, at : at + pair],
            ],
            axis=0,
        ).astype(F32)
        values = values.T[g % 2 * HEAD_DIM : (g % 2 + 1) * HEAD_DIM].astype(BF16)
        for head in range(g * group, (g + 1) * group, 2):
            scores = across(keys, projected[:, head * HEAD_DIM : head * HEAD_DIM + pair])
            for side in (0, 1):
                past = scores[2 * side * rows : (2 * side + 1) * rows]
                here = scores[(2 * side + 1) * rows : (2 * side + 2) * rows]
                merged = jnp.where(older, past * scale + offset, here * 0.125)
                sink = sinks_ref[0, head + side]
                peak = jnp.maximum(jnp.max(merged, axis=0, keepdims=True), sink)
                numer = jnp.exp(merged - peak)
                denominator = jnp.sum(numer, axis=0, keepdims=True) + jnp.exp(sink - peak)
                share = numer * (1.0 / denominator)
                both = jnp.concatenate(
                    [jnp.where(older, share, 0.0), jnp.where(older, 0.0, share)], axis=0
                ).astype(BF16)
                attended[(head + side) * HEAD_DIM : (head + side + 1) * HEAD_DIM] = jnp.dot(
                    values, both, preferred_element_type=F32
                ).astype(BF16)


def project_kernel(
    state_ref,
    gain_ref,
    weight_hbm,
    bias_ref,
    ids_ref,
    logits_ref,
    sinks_ref,
    out_weight_hbm,
    out_bias_ref,
    mid_gain_ref,
    normed_ref,
    residual_ref,
    tables_ref,
    projected_ref,
    scaled,
    tokens_ref,
    out_weight,
    attended,
    weight,
    slices,
    transit,
    total,
    sent,
    half_in,
    full_in,
    behind,
    tables,
    local_sem,
    send_sem,
    recv_sem,
):
    net = Links(send_sem, recv_sem)
    columns = weight.shape[4]
    rows = normed_ref.shape[0]
    cuts = (384, 256)

    def column_at(which, chunk):
        return columns * (chunk if which == 0 else 3 - chunk)

    loads = {
        (which, chunk): pltpu.make_async_copy(
            weight_hbm.at[:, pl.ds(column_at(which, chunk), columns)],
            weight.at[which, chunk, 0],
            local_sem.at[5 + 2 * which + chunk],
        )
        for chunk in (0, 1)
        for which in (0, 1)
    }
    for load in loads.values():
        load.start()
    load_out = pltpu.make_async_copy(out_weight_hbm, out_weight, local_sem.at[4])
    load_out.start()
    member, gate_weight = routing_tables(ids_ref[...], logits_ref[...])
    tables[0, 0, 0:8] = member
    tables[0, 0, 8:16] = gate_weight
    place = (net.x, net.z)
    features = state_ref.shape[0]

    def for_device(which, step, at, size):
        to = (place[1 - which] + step + SIDE) % SIDE
        pieces = slice(at, at + size)
        if which == 0:
            return lambda: tokens_ref.at[pieces, to]
        return lambda: tokens_ref.at[to, pieces]

    def kept(which, dq, at, size):
        lanes = slice(dq * rows, (dq + 1) * rows)
        pieces = slice(at, at + size)
        return lambda: slices.at[which, pieces, :, lanes]

    net.barrier([(0, 1), (0, -1), (1, 1), (1, -1), (3, 1), (3, -1)])
    steps = ((0, 1), (1, -1))
    net.start(("mx", 1), view(tables, 0, 0), view(tables, 0, 3), 0, 1)
    net.start(("mx", -1), view(tables, 0, 0), view(tables, 0, 1), 0, -1)

    def offer(which, chunk):
        loads[which, chunk].wait()
        for side, step in steps:
            net.start(
                ("wo", which, chunk, step),
                view(weight, which, chunk, 0),
                view(weight, which, chunk, (-step) % SIDE),
                which,
                step,
            )

    for which in (0, 1):
        offer(which, 0)
    squares = jnp.zeros((1, rows), F32)
    for at, size in chunks(features, 640):
        part = state_ref[at : at + size].astype(F32)
        squares = squares + jnp.sum(part * part, axis=0, keepdims=True)
    inverse = lax.rsqrt(squares / features + 1e-05)
    for at, size in chunks(features, 640):
        gain = jnp.broadcast_to(gain_ref[:, at : at + size], (rows, size)).T
        scaled[at : at + size] = state_ref[at : at + size].astype(F32) * inverse * gain
    depth = tokens_ref.shape[2]
    for a in range(SIDE):
        for b in range(SIDE):
            at = (a * SIDE + b) * depth
            tokens_ref[a, b] = scaled[at : at + depth].astype(BF16)
    stays = [
        pltpu.make_async_copy(
            for_device(which, 0, 0, SIDE)(), kept(which, 0, 0, SIDE)(), local_sem.at[2 + which]
        )
        for which in (0, 1)
    ]
    for stay in stays:
        stay.start()
    for which in (0, 1):
        for side, step in steps:
            net.start(
                ("tt", which, step),
                for_device(which, 2, side * 2, 2),
                view(transit, which, side),
                1 - which,
                step,
            )
    for which in (0, 1):
        for side, step in steps:
            net.start(
                ("ta", which, step),
                for_device(which, step, 0, SIDE),
                kept(which, (-step) % SIDE, 0, SIDE),
                1 - which,
                step,
            )
    def pass_on(which, chunk, step):
        net.need(("wo", which, chunk, step))
        part = slice(0, cuts[chunk]) if step == 1 else slice(cuts[chunk], columns)
        every = slice(None)
        net.start(
            ("wf", which, chunk, step),
            view(weight, which, chunk, (-step) % SIDE, every, part),
            view(weight, which, chunk, 2, every, part),
            which,
            step,
        )

    def multiply(which, chunk, dp):
        piece = (place[which] + dp) % SIDE
        term = along(slices[which, piece], weight[which, chunk, dp])
        if dp == 0:
            total[which, chunk] = term
        else:
            total[which, chunk] += term

    def half_of(side):
        return slice(side * rows // 2, (side + 1) * rows // 2)

    def sums_out(which, chunk):
        net.need(("wf", which, chunk, 1), ("wf", which, chunk, -1))
        multiply(which, chunk, 2)
        sent[which, chunk, 2] = total[which, chunk, 2 * rows : 3 * rows].astype(BF16)
        for side, step in steps:
            net.start(
                ("rh", which, chunk, step),
                view(sent, which, chunk, 2, half_of(side)),
                view(half_in, which, chunk, side),
                1 - which,
                step,
            )

    def sums_on(which, chunk):
        for side, step in steps:
            dq = step % SIDE
            other = half_of(1 - side)
            sent[which, chunk, dq, other] = total[
                which, chunk, dq * rows + other.start : dq * rows + other.stop
            ].astype(BF16)
            net.need(("rh", which, chunk, step))
            part = half_of(side)
            sent[which, chunk, dq, part] = (
                total[which, chunk, dq * rows + part.start : dq * rows + part.stop]
                + half_in[which, chunk, side].astype(F32)
            ).astype(BF16)
            net.start(
                ("rf", which, chunk, step),
                view(sent, which, chunk, dq),
                view(full_in, which, chunk, side),
                1 - which,
                step,
            )

    def sums_in(which, chunk):
        net.need(("rf", which, chunk, 1), ("rf", which, chunk, -1))
        lanes = slice(column_at(which, chunk), column_at(which, chunk) + columns)
        projected_ref[:, lanes] = (
            total[which, chunk, 0:rows]
            + full_in[which, chunk, 0].astype(F32)
            + full_in[which, chunk, 1].astype(F32)
            + bias_ref[:, lanes]
        ).astype(BF16)

    for step in (1, -1):
        for which in (0, 1):
            pass_on(which, 0, step)
    for which in (0, 1):
        for side, step in steps:
            net.need(("tt", which, step))
            net.start(
                ("tf", which, step),
                view(transit, which, side),
                kept(which, 2, side * 2, 2),
                1 - which,
                step,
            )
    for which in (0, 1):
        offer(which, 1)
    net.need(("mx", 1))
    net.start(("mf", 0), view(tables, 0, 3), view(tables, 0, 2), 0, 1)
    for which in (0, 1):
        stays[which].wait()
        net.need(("ta", which, 1), ("ta", which, -1), ("tf", which, 1), ("tf", which, -1))
    for which in (1, 0):
        for dp in (0, 3, 1):
            multiply(which, 0, dp)
    for which in (1, 0):
        sums_out(which, 0)
    for step in (1, -1):
        for which in (0, 1):
            pass_on(which, 1, step)
    net.need(("mx", -1), ("mf", 0))
    net.start(("mz", 1), view(tables, 0), view(tables, 3), 1, 1)
    net.start(("mz", -1), view(tables, 0), view(tables, 1), 1, -1)
    for which in (1, 0):
        sums_on(which, 0)
    for which in (1, 0):
        for dp in (0, 3, 1):
            multiply(which, 1, dp)
    for which in (1, 0):
        sums_out(which, 1)
    net.need(("mz", 1), ("mz", -1))
    net.start(("mg", 0), view(tables, 3), view(tables, 2), 1, 1)
    sums_in(1, 0)
    keys = slice(4 * columns - behind.shape[1], 4 * columns)
    net.start(("kv", 0), view(projected_ref, slice(None), keys), view(behind), 3, 1)
    for which in (1, 0):
        sums_on(which, 1)
    sums_in(0, 0)
    for which in (1, 0):
        sums_in(which, 1)
    net.finish()
    tables_ref[...] = tables[...]
    attend(projected_ref, behind, sinks_ref, attended, net.x * SIDE + net.z == 0)
    load_out.wait()
    squares = jnp.zeros((rows, 1), F32)
    for at, size in chunks(features, 640):
        lanes = slice(at, at + size)
        mixed = jnp.dot(out_weight[lanes], attended[...], preferred_element_type=F32)
        mixed = mixed + state_ref[lanes].astype(F32)
        kept_sum = (mixed.T + out_bias_ref[:, lanes]).astype(BF16)
        residual_ref[:, lanes] = kept_sum
        wide = kept_sum.astype(F32)
        squares = squares + jnp.sum(wide * wide, axis=1, keepdims=True)
    inverse = lax.rsqrt(squares / features + 1e-05)
    for at, size in chunks(features, 640):
        lanes = slice(at, at + size)
        wide = residual_ref[:, lanes].astype(F32)
        normed_ref[:, lanes] = (wide * inverse * mid_gain_ref[:, lanes]).astype(BF16)


def attention_part(state, gain, weight, bias, ids, logits, sinks, out_weight, out_bias, mid_gain):
    features, rows = state.shape
    depth = weight.shape[0]
    wide = weight.shape[1]
    columns = wide // 4
    keys = 2 * KEY_VALUE_HEADS * HEAD_DIM
    anywhere = pl.BlockSpec(memory_space=pl.ANY)
    vmem = pl.BlockSpec(memory_space=pltpu.VMEM)
    return pl.pallas_call(
        project_kernel,
        out_shape=(
            jax.ShapeDtypeStruct((rows, features), BF16),
            jax.ShapeDtypeStruct((rows, features), BF16),
            jax.ShapeDtypeStruct((SIDE, SIDE, 16, rows), F32),
        ),
        in_specs=[
            vmem,
            vmem,
            anywhere,
            vmem,
            vmem,
            vmem,
            pl.BlockSpec(memory_space=pltpu.SMEM),
            anywhere,
            vmem,
            vmem,
        ],
        out_specs=(vmem, vmem, vmem),
        scratch_shapes=[
            pltpu.VMEM((rows, wide), BF16),
            pltpu.VMEM((features, rows), F32),
            pltpu.VMEM((SIDE, SIDE, depth, rows), BF16),
            pltpu.VMEM(out_weight.shape, BF16),
            pltpu.VMEM((QUERY_HEADS * HEAD_DIM, rows), BF16),
            pltpu.VMEM((2, 2, SIDE, depth, columns), BF16),
            pltpu.VMEM((2, SIDE, depth, SIDE * rows), BF16),
            pltpu.VMEM((2, 2, 2, depth, rows), BF16),
            pltpu.VMEM((2, 2, SIDE * rows, columns), F32),
            pltpu.VMEM((2, 2, SIDE, rows, columns), BF16),
            pltpu.VMEM((2, 2, 2, rows // 2, columns), BF16),
            pltpu.VMEM((2, 2, 2, rows, columns), BF16),
            pltpu.VMEM((rows, keys), BF16),
            pltpu.VMEM((SIDE, SIDE, 16, rows), F32),
            pltpu.SemaphoreType.DMA((9,)),
            pltpu.SemaphoreType.DMA((64,)),
            pltpu.SemaphoreType.DMA((64,)),
        ],
        compiler_params=pltpu.CompilerParams(
            collective_id=2, has_side_effects=True, vmem_limit_bytes=56 * 1024 * 1024
        ),
        cost_estimate=pl.CostEstimate(
            flops=2_000_000_000, bytes_accessed=4_000_000, transcendentals=0
        ),
    )(state, gain, weight, bias, ids, logits, sinks, out_weight, out_bias, mid_gain)


def shards(
    section_input,
    attention_gain,
    query_key_value_weight,
    qkv_bias,
    out_weight,
    out_bias,
    attention_sink_logits,
    expert_gain,
    gate_up_weight,
    down_weight,
    expert_ids,
    gate_logits,
    placement,
):
    rows = section_input.shape[1]
    experts = placement.shape[1]
    slots = 2 * min(rows // 2, rows * TOP * 5 // (8 * experts))
    normed_mid, residual, tables = attention_part(
        section_input[0].T,
        attention_gain,
        query_key_value_weight[0],
        qkv_bias,
        expert_ids[0].T,
        gate_logits[0].T,
        attention_sink_logits,
        out_weight[0].T,
        out_bias,
        expert_gain,
    )
    moved = experts_and_pass(
        normed_mid, residual, tables, placement, gate_up_weight[0, 0].T, down_weight[0, 0], slots
    )
    return moved[None]


def solution(mesh):
    return jax.shard_map(
        shards,
        mesh=mesh,
        in_specs=(
            P("section", "expert", None),
            P("section", None),
            P("section", "expert", None),
            P("section", None),
            P("section", None, None),
            P("section", None),
            P("section", None),
            P("section", None),
            P("section", "expert", None, None),
            P("section", "expert", None, None),
            P("section", "expert", None),
            P("section", "expert", None),
            P("section", None),
        ),
        out_specs=P("section", "expert", None),
        check_vma=False,
    )
```

```python
import functools

import jax
import jax.numpy as jnp
from jax import lax
from jax.experimental import pallas as pl
from jax.experimental.pallas import tpu as pltpu
from jax.sharding import PartitionSpec as P

HEAD_DIM = 64
QUERY_HEADS = 32
KEY_VALUE_HEADS = 4
TOP = 4
SIDE = 4
MESH = pl.DeviceIdType.MESH
F32 = jnp.float32
BF16 = jnp.bfloat16


class Links:
    def __init__(self, send, recv):
        self.send, self.recv = send, recv
        self.keys, self.started, self.done = {}, [], set()
        self.made = {}
        self.section = lax.axis_index("section")
        me = lax.axis_index("expert")
        self.x, self.z = me // SIDE, me % SIDE

    def neighbour(self, axis, step):
        if axis == 3:
            return (self.section, (self.x * SIDE + self.z + step + 16) % 16)
        if axis == 2:
            return ((self.section + step + 8) % 8, self.x * SIDE + self.z)
        if axis == 0:
            return (self.section, ((self.x + step + SIDE) % SIDE) * SIDE + self.z)
        return (self.section, self.x * SIDE + (self.z + step + SIDE) % SIDE)

    def barrier(self, partners):
        sem = pltpu.get_barrier_semaphore()
        for axis, step in partners:
            pl.semaphore_signal(
                sem, inc=1, device_id=self.neighbour(axis, step), device_id_type=MESH
            )
        pl.semaphore_wait(sem, len(partners))

    def start(self, name, src, dst, axis, step):
        assert name not in self.made
        key = self.keys.setdefault(name, len(self.keys))
        copy = pltpu.make_async_remote_copy(
            src_ref=src(),
            dst_ref=dst(),
            send_sem=self.send.at[key],
            recv_sem=self.recv.at[key],
            device_id=self.neighbour(axis, step),
            device_id_type=MESH,
        )
        copy.start()
        self.made[name] = (src, dst, axis, step)

    def remake(self, name):
        src, dst, axis, step = self.made[name]
        key = self.keys[name]
        return pltpu.make_async_remote_copy(
            src_ref=src(),
            dst_ref=dst(),
            send_sem=self.send.at[key],
            recv_sem=self.recv.at[key],
            device_id=self.neighbour(axis, step),
            device_id_type=MESH,
        )

    def need(self, *names):
        for name in names:
            if name not in self.done:
                self.done.add(name)
                self.remake(name).wait_recv()

    def finish(self):
        for name in self.made:
            self.need(name)
            self.remake(name).wait_send()


def of_four(g, values):
    a, b, c, d = values
    return (
        b * (g * (g - 2) * (g - 3)) // 2
        - c * (g * (g - 1) * (g - 3)) // 2
        + d * (g * (g - 1) * (g - 2)) // 6
        - a * ((g - 1) * (g - 2) * (g - 3)) // 6
    )


def add_rows(dst, *parts):
    step = 16

    def body(i, carry):
        rows = pl.ds(pl.multiple_of(i * step, step), step)
        total = parts[0][rows].astype(F32)
        for part in parts[1:]:
            total = total + part[rows].astype(F32)
        dst[rows] = total.astype(dst.dtype)
        return carry

    lax.fori_loop(0, dst.shape[0] // step, body, 0)


def view(ref, *index):
    return lambda: ref.at[index]


def across(rows, other):
    return lax.dot_general(rows, other, (((1,), (1,)), ((), ())), preferred_element_type=F32)


def along(first, second):
    return lax.dot_general(first, second, (((0,), (0,)), ((), ())), preferred_element_type=F32)


def chunks(total, size):
    return [(at, min(size, total - at)) for at in range(0, total, size)]


def expert_kernel(
    slots,
    normed_ref,
    residual_ref,
    meta_ref,
    holders_ref,
    gate_up_hbm,
    down_hbm,
    out_ref,
    tokens,
    parts,
    gate_up,
    down,
    packed,
    act,
    picks,
    half_in,
    full_in,
    half_last,
    full_last,
    local_sem,
    send_sem,
    recv_sem,
):
    half_rows = tokens.shape[2] // 2
    quarter = half_rows // 2
    width = tokens.shape[3]
    inner = act.shape[1]
    net = Links(send_sem, recv_sem)
    load_tokens = pltpu.make_async_copy(normed_ref, tokens.at[0, 0], local_sem.at[0])
    load_gate_up = pltpu.make_async_copy(gate_up_hbm, gate_up, local_sem.at[1])
    load_down = pltpu.make_async_copy(down_hbm, down, local_sem.at[2])
    load_tokens.start()
    net.barrier([(0, 1), (0, -1), (1, 1), (1, -1), (2, 1), (2, -1)])

    load_tokens.wait()
    load_gate_up.start()
    load_down.start()

    def block(which, dp, dq, at, size):
        first, second = (dp, dq) if which == 0 else (dq, dp)
        rows = slice(which * half_rows + at, which * half_rows + at + size)
        return lambda: tokens.at[first, second, rows]

    def part(which, dp, dq, at, size):
        first, second = (dp, dq) if which == 0 else (dq, dp)
        rows = slice(which * half_rows + at, which * half_rows + at + size)
        return lambda: parts.at[first, second, rows]

    def own(which, axis, step):
        to = (-step) % SIDE
        place = (to, 0) if axis == which else (0, to)
        name = ("op" if axis == which else "oq", which, step)
        net.start(
            name,
            block(which, 0, 0, 0, half_rows),
            block(which, *place, 0, half_rows),
            axis,
            step,
        )

    for axis in (0, 1):
        for step in (1, -1):
            own(axis, axis, step)
    for axis in (0, 1):
        for step in (1, -1):
            own(1 - axis, axis, step)

    def at_of(step):
        return 0 if step == 1 else quarter

    def on_across(which, dp, dq_axis_step):
        step = dq_axis_step
        net.start(
            ("pq", which, dp, step),
            block(which, dp, 0, 0, half_rows),
            block(which, dp, (-step) % SIDE, 0, half_rows),
            1 - which,
            step,
        )

    def first_hops():
        for step in (1, -1):
            for which in (0, 1):
                dp = (-step) % SIDE
                net.need(("op", which, step))
                net.start(
                    ("fp", which, step),
                    block(which, dp, 0, at_of(step), quarter),
                    block(which, 2, 0, at_of(step), quarter),
                    which,
                    step,
                )
        for which in (0, 1):
            on_across(which, 3, 1)
            on_across(which, 3, -1)

    def other_hops():
        for which in (0, 1):
            on_across(which, 1, 1)
            on_across(which, 1, -1)

    def far_hops():
        for half in (1, -1):
            for which in (0, 1):
                net.need(("fp", which, half))
                for step in (1, -1):
                    net.start(
                        ("pq2", which, half, step),
                        block(which, 2, 0, at_of(half), quarter),
                        block(which, 2, (-step) % SIDE, at_of(half), quarter),
                        1 - which,
                        step,
                    )

    def second_hops(dp):
        for step in (1, -1):
            for which in (0, 1):
                if dp == 0:
                    net.need(("oq", which, step))
                elif dp == 2:
                    net.need(("pq2", which, step, step))
                else:
                    net.need(("pq", which, dp, step))
                net.start(
                    ("fq", which, dp, step),
                    block(which, dp, (-step) % SIDE, at_of(step), quarter),
                    block(which, dp, 2, at_of(step), quarter),
                    1 - which,
                    step,
                )

    def arrived(blocks):
        for dx, dz in blocks:
            for which in (0, 1):
                dp, dq = (dx, dz) if which == 0 else (dz, dx)
                step = {1: -1, 3: 1}
                if dq == 0:
                    if dp in step:
                        net.need(("op", which, step[dp]))
                    elif dp == 2:
                        net.need(("fp", which, 1), ("fp", which, -1))
                elif dq == 2:
                    net.need(("fq", which, dp, 1), ("fq", which, dp, -1))
                elif dp == 0:
                    net.need(("oq", which, step[dq]))
                elif dp == 2:
                    net.need(("pq2", which, 1, step[dq]), ("pq2", which, -1, step[dq]))
                else:
                    net.need(("pq", which, dp, step[dq]))

    groups = (
        ((0, 0), (1, 0), (3, 0), (0, 1)),
        ((0, 3), (0, 2), (2, 0), (3, 3)),
        ((1, 1), (1, 3), (3, 1), (3, 2)),
        ((2, 3), (1, 2), (2, 1), (2, 2)),
    )

    def stage(at):
        if at == 0:
            first_hops()
            second_hops(0)
            other_hops()
            load_gate_up.wait()
            load_down.wait()
        elif at == 1:
            far_hops()
            second_hops(3)
        elif at == 2:
            second_hops(1)
            second_hops(2)
            back(0)
        else:
            relay(0)
        arrived(groups[at])

    def relay(dp, pieces=1):
        size = half_rows // pieces
        for which in (0, 1):
            for side, step in ((0, 1), (1, -1)):
                net.need(("rh", which, dp, step))
                there = part(which, dp, step % SIDE, at_of(step), quarter)
                add_rows(there(), there(), half_in.at[which, dp, side])
                for piece in range(pieces):
                    rows = slice(piece * size, (piece + 1) * size)
                    net.start(
                        ("rf", which, dp, step, piece),
                        part(which, dp, step % SIDE, piece * size, size),
                        view(full_in, which, dp, side, rows),
                        1 - which,
                        step,
                    )

    def back(dp):
        for which in (0, 1):
            for side, step in ((0, 1), (1, -1)):
                net.start(
                    ("rh", which, dp, step),
                    part(which, dp, 2, at_of(step), quarter),
                    view(half_in, which, dp, side),
                    1 - which,
                    step,
                )

    before = lax.broadcasted_iota(jnp.int32, (128, 128), 0)
    after = lax.broadcasted_iota(jnp.int32, (128, 128), 1)
    earlier = jnp.where(before < after, 1.0, 0.0).astype(BF16)
    slot = lax.broadcasted_iota(jnp.int32, (slots, 128), 0).astype(F32)

    pair = lax.axis_index("expert") // 2
    at_pair = lax.broadcasted_iota(jnp.int32, (1, 8), 1) == pair
    mine = jnp.sum(jnp.where(at_pair, holders_ref[...], 0), axis=1, keepdims=True)
    chosen = jnp.where(lax.broadcasted_iota(jnp.int32, (8, 128), 0) == mine, 1.0, 0.0)

    def group(g, carry):
        for at in range(SIDE):
            pl.when(g == at)(functools.partial(stage, at))
        places = [[of_four(g, [group[k][axis] for group in groups]) for axis in (0, 1)] for k in range(SIDE)]
        scales = []
        for k, (dx, dz) in enumerate(places):
            table = meta_ref[dz, dx]
            member = jnp.sum(table[0:8] * chosen, axis=0, keepdims=True)
            weight = jnp.sum(table[8:16] * chosen, axis=0, keepdims=True)
            wide = jnp.broadcast_to(member, (16, 128)).astype(BF16)
            rank = jnp.dot(wide, earlier, preferred_element_type=F32)[0:1]
            hit = (slot == rank) & (member > 0.5)
            pick = jnp.where(hit, 1.0, 0.0).astype(BF16)
            scales.append(jnp.sum(jnp.where(hit, weight, 0.0), axis=1, keepdims=True))
            picks[k] = pick
            for at, size in chunks(width, 1024):
                packed[k * slots : (k + 1) * slots, at : at + size] = jnp.dot(
                    pick, tokens[dx, dz, :, at : at + size], preferred_element_type=F32
                ).astype(BF16)
        scale = jnp.concatenate(scales, axis=0)
        for at, size in chunks(inner, 256):
            gate = across(packed[...], gate_up[at : at + size])
            up = across(packed[...], gate_up[inner + at : inner + at + size])
            act[:, at : at + size] = (
                (up + 1.0) * gate * jax.nn.sigmoid(1.702 * gate)
            ).astype(BF16)
        for at, size in chunks(width, 640):
            tile = jnp.dot(act[...], down[:, at : at + size], preferred_element_type=F32)
            tile = (tile * scale).astype(BF16)
            for k, (dx, dz) in enumerate(places):
                parts[dx, dz, :, at : at + size] = along(
                    picks[k], tile[k * slots : (k + 1) * slots]
                ).astype(BF16)
        return carry

    lax.fori_loop(0, SIDE, group, 0)

    for dp in (2, 1, 3):
        back(dp)

    def gather_in(which, dp, piece=0, pieces=1):
        size = half_rows // pieces
        rows = slice(piece * size, (piece + 1) * size)
        net.need(("rf", which, dp, 1, piece), ("rf", which, dp, -1, piece))
        here = part(which, dp, 0, piece * size, size)
        add_rows(here(), here(), full_in.at[which, dp, 0, rows], full_in.at[which, dp, 1, rows])

    def last_half(which):
        for side, step in ((0, 1), (1, -1)):
            net.start(
                ("lh", which, step),
                part(which, 2, 0, at_of(step), quarter),
                view(half_last, which, side),
                which,
                step,
            )

    ends = ((0, quarter), (quarter, quarter // 2), (quarter * 3 // 2, quarter // 2))

    def last_full(which, step, at, size):
        side = (1 - step) // 2
        if at == at_of(step):
            there = part(which, step % SIDE, 0, at, quarter)
            net.need(("lh", which, step))
            add_rows(there(), there(), half_last.at[which, side])
        net.start(
            ("lf", which, step, at),
            part(which, step % SIDE, 0, at, size),
            view(full_last, which, side, slice(at, at + size)),
            which,
            step,
        )

    relay(2)
    relay(1)
    for which in (0, 1):
        gather_in(which, 2)
        last_half(which)
    relay(3, 2)
    for which in (0, 1):
        gather_in(which, 1)
        for at, size in ends:
            last_full(which, 1, at, size)
    for piece in (0, 1):
        for which in (0, 1):
            gather_in(which, 3, piece, 2)
            for at, size in ends:
                if at // quarter == piece:
                    last_full(which, -1, at, size)
    for which in (0, 1):
        net.need(("rf", which, 0, 1, 0), ("rf", which, 0, -1, 0))
    for at, size in ends:
        for which in (0, 1):
            net.need(("lf", which, 1, at), ("lf", which, -1, at))
            here = part(which, 0, 0, at, size)
            inside = slice(at, at + size)
            rows = slice(which * half_rows + at, which * half_rows + at + size)
            add_rows(
                here(),
                here(),
                full_in.at[which, 0, 0, inside],
                full_in.at[which, 0, 1, inside],
                full_last.at[which, 0, inside],
                full_last.at[which, 1, inside],
                residual_ref.at[rows],
            )
            net.start(("out", which, at), here, view(out_ref, rows), 2, 1)
    net.finish()


def experts_and_pass(normed_mid, residual, meta, holders, gate_up, down, slots):
    rows, width = normed_mid.shape
    inner = down.shape[0]
    anywhere = pl.BlockSpec(memory_space=pl.ANY)
    vmem = pl.BlockSpec(memory_space=pltpu.VMEM)
    half, quarter = rows // 2, rows // 4
    return pl.pallas_call(
        functools.partial(expert_kernel, slots),
        out_shape=jax.ShapeDtypeStruct((rows, width), BF16),
        in_specs=[anywhere, vmem, vmem, vmem, anywhere, anywhere],
        out_specs=anywhere,
        scratch_shapes=[
            pltpu.VMEM((SIDE, SIDE, rows, width), BF16),
            pltpu.VMEM((SIDE, SIDE, rows, width), BF16),
            pltpu.VMEM(gate_up.shape, BF16),
            pltpu.VMEM(down.shape, BF16),
            pltpu.VMEM((SIDE * slots, width), BF16),
            pltpu.VMEM((SIDE * slots, inner), BF16),
            pltpu.VMEM((SIDE, slots, rows), BF16),
            pltpu.VMEM((2, SIDE, 2, quarter, width), BF16),
            pltpu.VMEM((2, SIDE, 2, half, width), BF16),
            pltpu.VMEM((2, 2, quarter, width), BF16),
            pltpu.VMEM((2, 2, half, width), BF16),
            pltpu.SemaphoreType.DMA((3,)),
            pltpu.SemaphoreType.DMA((112,)),
            pltpu.SemaphoreType.DMA((112,)),
        ],
        compiler_params=pltpu.CompilerParams(
            collective_id=1, has_side_effects=True, vmem_limit_bytes=62 * 1024 * 1024
        ),
        cost_estimate=pl.CostEstimate(
            flops=16_000_000_000, bytes_accessed=16_000_000, transcendentals=1_000_000
        ),
    )(normed_mid, residual, meta, holders, gate_up, down)


def routing_tables(ids, logits):
    kinds = lax.broadcasted_iota(jnp.int32, (8, ids.shape[1]), 0)
    grown = jnp.exp(logits - jnp.max(logits, axis=0, keepdims=True))
    weights = grown / jnp.sum(grown, axis=0, keepdims=True)
    member, weight = jnp.zeros(kinds.shape, F32), jnp.zeros(kinds.shape, F32)
    for k in range(TOP):
        equal = kinds == ids[k : k + 1]
        member = member + jnp.where(equal, 1.0, 0.0)
        weight = weight + jnp.where(equal, weights[k : k + 1], 0.0)
    return member, weight


def attend(groups, projected, behind, sinks_ref, attended, first):
    rows = projected.shape[0]
    pair = 2 * HEAD_DIM
    group = QUERY_HEADS // KEY_VALUE_HEADS
    row = lax.broadcasted_iota(jnp.int32, (rows, rows), 0)
    lane = lax.broadcasted_iota(jnp.int32, (rows, rows), 1)
    low = lax.broadcasted_iota(jnp.int32, (rows, pair), 1) < HEAD_DIM
    older = row > lane
    scale = jnp.where(first, 0.0, 0.125)
    offset = jnp.where(first, -1e30, 0.0)
    keys_at = QUERY_HEADS * HEAD_DIM
    values_at = keys_at + KEY_VALUE_HEADS * HEAD_DIM
    for g in groups:
        tile = g // 2 * pair
        stacked = []
        own = projected[:, keys_at + tile : keys_at + tile + pair].astype(F32)
        rim = behind[:, tile : tile + pair].astype(F32)
        for side in (0, 1):
            for keys in (rim, own):
                placed = keys if g % 2 == side else pltpu.roll(keys, HEAD_DIM, 1)
                stacked.append(jnp.where(low if side == 0 else ~low, placed, 0.0).astype(BF16))
        keys = jnp.concatenate(stacked, axis=0)
        at = values_at + tile
        values = jnp.concatenate(
            [
                behind[:, KEY_VALUE_HEADS * HEAD_DIM + tile : KEY_VALUE_HEADS * HEAD_DIM + tile + pair],
                projected[:, at : at + pair],
            ],
            axis=0,
        ).astype(F32)
        values = values.T[g % 2 * HEAD_DIM : (g % 2 + 1) * HEAD_DIM].astype(BF16)
        for head in range(g * group, (g + 1) * group, 2):
            scores = across(keys, projected[:, head * HEAD_DIM : head * HEAD_DIM + pair])
            for side in (0, 1):
                past = scores[2 * side * rows : (2 * side + 1) * rows]
                here = scores[(2 * side + 1) * rows : (2 * side + 2) * rows]
                merged = jnp.where(older, past * scale + offset, here * 0.125)
                sink = sinks_ref[0, head + side]
                peak = jnp.maximum(jnp.max(merged, axis=0, keepdims=True), sink)
                numer = jnp.exp(merged - peak)
                denominator = jnp.sum(numer, axis=0, keepdims=True) + jnp.exp(sink - peak)
                share = numer * (1.0 / denominator)
                both = jnp.concatenate(
                    [jnp.where(older, share, 0.0), jnp.where(older, 0.0, share)], axis=0
                ).astype(BF16)
                attended[(head + side) * HEAD_DIM : (head + side + 1) * HEAD_DIM] = jnp.dot(
                    values, both, preferred_element_type=F32
                ).astype(BF16)


def project_kernel(
    state_ref,
    gain_ref,
    weight_hbm,
    bias_ref,
    ids_ref,
    logits_ref,
    sinks_ref,
    out_weight_hbm,
    out_bias_ref,
    mid_gain_ref,
    normed_ref,
    residual_ref,
    tables_ref,
    projected_ref,
    scaled,
    tokens_ref,
    out_weight,
    attended,
    weight,
    slices,
    transit,
    total,
    sent,
    half_in,
    full_in,
    behind,
    tables,
    local_sem,
    send_sem,
    recv_sem,
):
    net = Links(send_sem, recv_sem)
    columns = weight.shape[4]
    rows = normed_ref.shape[0]
    cuts = (384, 256)

    def column_at(which, chunk):
        return columns * (chunk if which == 0 else 3 - chunk)

    loads = {
        (which, chunk): pltpu.make_async_copy(
            weight_hbm.at[:, pl.ds(column_at(which, chunk), columns)],
            weight.at[which, chunk, 0],
            local_sem.at[5 + 2 * which + chunk],
        )
        for chunk in (0, 1)
        for which in (0, 1)
    }
    for load in loads.values():
        load.start()
    load_out = pltpu.make_async_copy(out_weight_hbm, out_weight, local_sem.at[4])
    load_out.start()
    member, gate_weight = routing_tables(ids_ref[...], logits_ref[...])
    tables[0, 0, 0:8] = member
    tables[0, 0, 8:16] = gate_weight
    place = (net.x, net.z)
    features = state_ref.shape[0]

    def for_device(which, step, at, size):
        to = (place[1 - which] + step + SIDE) % SIDE
        pieces = slice(at, at + size)
        if which == 0:
            return lambda: tokens_ref.at[pieces, to]
        return lambda: tokens_ref.at[to, pieces]

    def kept(which, dq, at, size):
        lanes = slice(dq * rows, (dq + 1) * rows)
        pieces = slice(at, at + size)
        return lambda: slices.at[which, pieces, :, lanes]

    net.barrier([(0, 1), (0, -1), (1, 1), (1, -1), (3, 1), (3, -1)])
    steps = ((0, 1), (1, -1))
    net.start(("mx", 1), view(tables, 0, 0), view(tables, 0, 3), 0, 1)
    net.start(("mx", -1), view(tables, 0, 0), view(tables, 0, 1), 0, -1)

    def offer(which, chunk):
        loads[which, chunk].wait()
        for side, step in steps:
            net.start(
                ("wo", which, chunk, step),
                view(weight, which, chunk, 0),
                view(weight, which, chunk, (-step) % SIDE),
                which,
                step,
            )

    for which in (0, 1):
        offer(which, 0)
    squares = jnp.zeros((1, rows), F32)
    for at, size in chunks(features, 640):
        part = state_ref[at : at + size].astype(F32)
        squares = squares + jnp.sum(part * part, axis=0, keepdims=True)
    inverse = lax.rsqrt(squares / features + 1e-05)
    for at, size in chunks(features, 640):
        gain = jnp.broadcast_to(gain_ref[:, at : at + size], (rows, size)).T
        scaled[at : at + size] = state_ref[at : at + size].astype(F32) * inverse * gain
    depth = tokens_ref.shape[2]
    for a in range(SIDE):
        for b in range(SIDE):
            at = (a * SIDE + b) * depth
            tokens_ref[a, b] = scaled[at : at + depth].astype(BF16)
    stays = [
        pltpu.make_async_copy(
            for_device(which, 0, 0, SIDE)(), kept(which, 0, 0, SIDE)(), local_sem.at[2 + which]
        )
        for which in (0, 1)
    ]
    for stay in stays:
        stay.start()
    for which in (0, 1):
        for side, step in steps:
            net.start(
                ("tt", which, step),
                for_device(which, 2, side * 2, 2),
                view(transit, which, side),
                1 - which,
                step,
            )
    for which in (0, 1):
        for side, step in steps:
            net.start(
                ("ta", which, step),
                for_device(which, step, 0, SIDE),
                kept(which, (-step) % SIDE, 0, SIDE),
                1 - which,
                step,
            )
    def pass_on(which, chunk, step):
        net.need(("wo", which, chunk, step))
        part = slice(0, cuts[chunk]) if step == 1 else slice(cuts[chunk], columns)
        every = slice(None)
        net.start(
            ("wf", which, chunk, step),
            view(weight, which, chunk, (-step) % SIDE, every, part),
            view(weight, which, chunk, 2, every, part),
            which,
            step,
        )

    def multiply(which, chunk, dp):
        piece = (place[which] + dp) % SIDE
        term = along(slices[which, piece], weight[which, chunk, dp])
        if dp == 0:
            total[which, chunk] = term
        else:
            total[which, chunk] += term

    def half_of(side):
        return slice(side * rows // 2, (side + 1) * rows // 2)

    def sums_out(which, chunk):
        net.need(("wf", which, chunk, 1), ("wf", which, chunk, -1))
        multiply(which, chunk, 2)
        sent[which, chunk, 2] = total[which, chunk, 2 * rows : 3 * rows].astype(BF16)
        for side, step in steps:
            net.start(
                ("rh", which, chunk, step),
                view(sent, which, chunk, 2, half_of(side)),
                view(half_in, which, chunk, side),
                1 - which,
                step,
            )

    def sums_on(which, chunk):
        for side, step in steps:
            dq = step % SIDE
            other = half_of(1 - side)
            sent[which, chunk, dq, other] = total[
                which, chunk, dq * rows + other.start : dq * rows + other.stop
            ].astype(BF16)
            net.need(("rh", which, chunk, step))
            part = half_of(side)
            sent[which, chunk, dq, part] = (
                total[which, chunk, dq * rows + part.start : dq * rows + part.stop]
                + half_in[which, chunk, side].astype(F32)
            ).astype(BF16)
            net.start(
                ("rf", which, chunk, step),
                view(sent, which, chunk, dq),
                view(full_in, which, chunk, side),
                1 - which,
                step,
            )

    def sums_in(which, chunk):
        net.need(("rf", which, chunk, 1), ("rf", which, chunk, -1))
        lanes = slice(column_at(which, chunk), column_at(which, chunk) + columns)
        projected_ref[:, lanes] = (
            total[which, chunk, 0:rows]
            + full_in[which, chunk, 0].astype(F32)
            + full_in[which, chunk, 1].astype(F32)
            + bias_ref[:, lanes]
        ).astype(BF16)

    for step in (1, -1):
        for which in (0, 1):
            pass_on(which, 0, step)
    for which in (0, 1):
        for side, step in steps:
            net.need(("tt", which, step))
            net.start(
                ("tf", which, step),
                view(transit, which, side),
                kept(which, 2, side * 2, 2),
                1 - which,
                step,
            )
    for which in (0, 1):
        offer(which, 1)
    net.need(("mx", 1))
    net.start(("mf", 0), view(tables, 0, 3), view(tables, 0, 2), 0, 1)
    for which in (0, 1):
        stays[which].wait()
        net.need(("ta", which, 1), ("ta", which, -1), ("tf", which, 1), ("tf", which, -1))
    for which in (1, 0):
        for dp in (0, 3, 1):
            multiply(which, 0, dp)
    for which in (1, 0):
        sums_out(which, 0)
    for step in (1, -1):
        for which in (0, 1):
            pass_on(which, 1, step)
    net.need(("mx", -1), ("mf", 0))
    net.start(("mz", 1), view(tables, 0), view(tables, 3), 1, 1)
    net.start(("mz", -1), view(tables, 0), view(tables, 1), 1, -1)
    for which in (1, 0):
        sums_on(which, 0)
    for which in (1, 0):
        for dp in (0, 3, 1):
            multiply(which, 1, dp)
    for which in (1, 0):
        sums_out(which, 1)
    net.need(("mz", 1), ("mz", -1))
    net.start(("mg", 0), view(tables, 3), view(tables, 2), 1, 1)
    sums_in(1, 0)
    keys = slice(4 * columns - behind.shape[1], 4 * columns)
    net.start(("kv", 0), view(projected_ref, slice(None), keys), view(behind), 3, 1)
    for which in (1, 0):
        sums_on(which, 1)
    sums_in(0, 0)
    first = net.x * SIDE + net.z == 0
    net.need(("kv", 0))
    attend((0,), projected_ref, behind, sinks_ref, attended, first)
    for which in (1, 0):
        sums_in(which, 1)
    net.finish()
    tables_ref[...] = tables[...]
    attend((1, 2, 3), projected_ref, behind, sinks_ref, attended, first)
    load_out.wait()
    squares = jnp.zeros((rows, 1), F32)
    for at, size in chunks(features, 640):
        lanes = slice(at, at + size)
        mixed = jnp.dot(out_weight[lanes], attended[...], preferred_element_type=F32)
        mixed = mixed + state_ref[lanes].astype(F32)
        kept_sum = (mixed.T + out_bias_ref[:, lanes]).astype(BF16)
        residual_ref[:, lanes] = kept_sum
        wide = kept_sum.astype(F32)
        squares = squares + jnp.sum(wide * wide, axis=1, keepdims=True)
    inverse = lax.rsqrt(squares / features + 1e-05)
    for at, size in chunks(features, 640):
        lanes = slice(at, at + size)
        wide = residual_ref[:, lanes].astype(F32)
        normed_ref[:, lanes] = (wide * inverse * mid_gain_ref[:, lanes]).astype(BF16)


def attention_part(state, gain, weight, bias, ids, logits, sinks, out_weight, out_bias, mid_gain):
    features, rows = state.shape
    depth = weight.shape[0]
    wide = weight.shape[1]
    columns = wide // 4
    keys = 2 * KEY_VALUE_HEADS * HEAD_DIM
    anywhere = pl.BlockSpec(memory_space=pl.ANY)
    vmem = pl.BlockSpec(memory_space=pltpu.VMEM)
    return pl.pallas_call(
        project_kernel,
        out_shape=(
            jax.ShapeDtypeStruct((rows, features), BF16),
            jax.ShapeDtypeStruct((rows, features), BF16),
            jax.ShapeDtypeStruct((SIDE, SIDE, 16, rows), F32),
        ),
        in_specs=[
            vmem,
            vmem,
            anywhere,
            vmem,
            vmem,
            vmem,
            pl.BlockSpec(memory_space=pltpu.SMEM),
            anywhere,
            vmem,
            vmem,
        ],
        out_specs=(vmem, vmem, vmem),
        scratch_shapes=[
            pltpu.VMEM((rows, wide), BF16),
            pltpu.VMEM((features, rows), F32),
            pltpu.VMEM((SIDE, SIDE, depth, rows), BF16),
            pltpu.VMEM(out_weight.shape, BF16),
            pltpu.VMEM((QUERY_HEADS * HEAD_DIM, rows), BF16),
            pltpu.VMEM((2, 2, SIDE, depth, columns), BF16),
            pltpu.VMEM((2, SIDE, depth, SIDE * rows), BF16),
            pltpu.VMEM((2, 2, 2, depth, rows), BF16),
            pltpu.VMEM((2, 2, SIDE * rows, columns), F32),
            pltpu.VMEM((2, 2, SIDE, rows, columns), BF16),
            pltpu.VMEM((2, 2, 2, rows // 2, columns), BF16),
            pltpu.VMEM((2, 2, 2, rows, columns), BF16),
            pltpu.VMEM((rows, keys), BF16),
            pltpu.VMEM((SIDE, SIDE, 16, rows), F32),
            pltpu.SemaphoreType.DMA((9,)),
            pltpu.SemaphoreType.DMA((64,)),
            pltpu.SemaphoreType.DMA((64,)),
        ],
        compiler_params=pltpu.CompilerParams(
            collective_id=2, has_side_effects=True, vmem_limit_bytes=56 * 1024 * 1024
        ),
        cost_estimate=pl.CostEstimate(
            flops=2_000_000_000, bytes_accessed=4_000_000, transcendentals=0
        ),
    )(state, gain, weight, bias, ids, logits, sinks, out_weight, out_bias, mid_gain)


def shards(
    section_input,
    attention_gain,
    query_key_value_weight,
    qkv_bias,
    out_weight,
    out_bias,
    attention_sink_logits,
    expert_gain,
    gate_up_weight,
    down_weight,
    expert_ids,
    gate_logits,
    placement,
):
    rows = section_input.shape[1]
    experts = placement.shape[1]
    slots = 2 * min(rows // 2, rows * TOP * 5 // (8 * experts))
    normed_mid, residual, tables = attention_part(
        section_input[0].T,
        attention_gain,
        query_key_value_weight[0],
        qkv_bias,
        expert_ids[0].T,
        gate_logits[0].T,
        attention_sink_logits,
        out_weight[0].T,
        out_bias,
        expert_gain,
    )
    moved = experts_and_pass(
        normed_mid, residual, tables, placement, gate_up_weight[0, 0].T, down_weight[0, 0], slots
    )
    return moved[None]


def solution(mesh):
    return jax.shard_map(
        shards,
        mesh=mesh,
        in_specs=(
            P("section", "expert", None),
            P("section", None),
            P("section", "expert", None),
            P("section", None),
            P("section", None, None),
            P("section", None),
            P("section", None),
            P("section", None),
            P("section", "expert", None, None),
            P("section", "expert", None, None),
            P("section", "expert", None),
            P("section", "expert", None),
            P("section", None),
        ),
        out_specs=P("section", "expert", None),
        check_vma=False,
    )
```

```python
import functools

import jax
import jax.numpy as jnp
from jax import lax
from jax.experimental import pallas as pl
from jax.experimental.pallas import tpu as pltpu
from jax.sharding import PartitionSpec as P

HEAD_DIM = 64
QUERY_HEADS = 32
KEY_VALUE_HEADS = 4
TOP = 4
SIDE = 4
MESH = pl.DeviceIdType.MESH
F32 = jnp.float32
BF16 = jnp.bfloat16


class Links:
    def __init__(self, send, recv):
        self.send, self.recv = send, recv
        self.keys, self.started, self.done = {}, [], set()
        self.made = {}
        self.section = lax.axis_index("section")
        me = lax.axis_index("expert")
        self.x, self.z = me // SIDE, me % SIDE

    def neighbour(self, axis, step):
        if axis == 3:
            return (self.section, (self.x * SIDE + self.z + step + 16) % 16)
        if axis == 2:
            return ((self.section + step + 8) % 8, self.x * SIDE + self.z)
        if axis == 0:
            return (self.section, ((self.x + step + SIDE) % SIDE) * SIDE + self.z)
        return (self.section, self.x * SIDE + (self.z + step + SIDE) % SIDE)

    def barrier(self, partners):
        sem = pltpu.get_barrier_semaphore()
        for axis, step in partners:
            pl.semaphore_signal(
                sem, inc=1, device_id=self.neighbour(axis, step), device_id_type=MESH
            )
        pl.semaphore_wait(sem, len(partners))

    def start(self, name, src, dst, axis, step):
        assert name not in self.made
        key = self.keys.setdefault(name, len(self.keys))
        copy = pltpu.make_async_remote_copy(
            src_ref=src(),
            dst_ref=dst(),
            send_sem=self.send.at[key],
            recv_sem=self.recv.at[key],
            device_id=self.neighbour(axis, step),
            device_id_type=MESH,
        )
        copy.start()
        self.made[name] = (src, dst, axis, step)

    def remake(self, name):
        src, dst, axis, step = self.made[name]
        key = self.keys[name]
        return pltpu.make_async_remote_copy(
            src_ref=src(),
            dst_ref=dst(),
            send_sem=self.send.at[key],
            recv_sem=self.recv.at[key],
            device_id=self.neighbour(axis, step),
            device_id_type=MESH,
        )

    def need(self, *names):
        for name in names:
            if name not in self.done:
                self.done.add(name)
                self.remake(name).wait_recv()

    def finish(self):
        for name in self.made:
            self.need(name)
            self.remake(name).wait_send()


def of_four(g, values):
    a, b, c, d = values
    return (
        b * (g * (g - 2) * (g - 3)) // 2
        - c * (g * (g - 1) * (g - 3)) // 2
        + d * (g * (g - 1) * (g - 2)) // 6
        - a * ((g - 1) * (g - 2) * (g - 3)) // 6
    )


def add_rows(dst, *parts):
    step = 16

    def body(i, carry):
        rows = pl.ds(pl.multiple_of(i * step, step), step)
        total = parts[0][rows].astype(F32)
        for part in parts[1:]:
            total = total + part[rows].astype(F32)
        dst[rows] = total.astype(dst.dtype)
        return carry

    lax.fori_loop(0, dst.shape[0] // step, body, 0)


def view(ref, *index):
    return lambda: ref.at[index]


def across(rows, other):
    return lax.dot_general(rows, other, (((1,), (1,)), ((), ())), preferred_element_type=F32)


def along(first, second):
    return lax.dot_general(first, second, (((0,), (0,)), ((), ())), preferred_element_type=F32)


def chunks(total, size):
    return [(at, min(size, total - at)) for at in range(0, total, size)]


def expert_kernel(
    slots,
    normed_ref,
    residual_ref,
    meta_ref,
    holders_ref,
    gate_up_hbm,
    down_hbm,
    out_ref,
    tokens,
    parts,
    gate_up,
    down,
    packed,
    act,
    picks,
    half_in,
    full_in,
    half_last,
    full_last,
    local_sem,
    send_sem,
    recv_sem,
):
    half_rows = tokens.shape[2] // 2
    quarter = half_rows // 2
    width = tokens.shape[3]
    inner = act.shape[1]
    net = Links(send_sem, recv_sem)
    load_tokens = pltpu.make_async_copy(normed_ref, tokens.at[0, 0], local_sem.at[0])
    load_gate_up = pltpu.make_async_copy(gate_up_hbm, gate_up, local_sem.at[1])
    load_down = pltpu.make_async_copy(down_hbm, down, local_sem.at[2])
    load_tokens.start()
    net.barrier([(0, 1), (0, -1), (1, 1), (1, -1), (2, 1), (2, -1)])

    load_tokens.wait()
    load_gate_up.start()
    load_down.start()

    def block(which, dp, dq, at, size):
        first, second = (dp, dq) if which == 0 else (dq, dp)
        rows = slice(which * half_rows + at, which * half_rows + at + size)
        return lambda: tokens.at[first, second, rows]

    def part(which, dp, dq, at, size):
        first, second = (dp, dq) if which == 0 else (dq, dp)
        rows = slice(which * half_rows + at, which * half_rows + at + size)
        return lambda: parts.at[first, second, rows]

    def own(which, axis, step):
        to = (-step) % SIDE
        place = (to, 0) if axis == which else (0, to)
        name = ("op" if axis == which else "oq", which, step)
        net.start(
            name,
            block(which, 0, 0, 0, half_rows),
            block(which, *place, 0, half_rows),
            axis,
            step,
        )

    for axis in (0, 1):
        for step in (1, -1):
            own(axis, axis, step)
    for axis in (0, 1):
        for step in (1, -1):
            own(1 - axis, axis, step)

    def at_of(step):
        return 0 if step == 1 else quarter

    def on_across(which, dp, dq_axis_step):
        step = dq_axis_step
        net.start(
            ("pq", which, dp, step),
            block(which, dp, 0, 0, half_rows),
            block(which, dp, (-step) % SIDE, 0, half_rows),
            1 - which,
            step,
        )

    def first_hops():
        for step in (1, -1):
            for which in (0, 1):
                dp = (-step) % SIDE
                net.need(("op", which, step))
                net.start(
                    ("fp", which, step),
                    block(which, dp, 0, at_of(step), quarter),
                    block(which, 2, 0, at_of(step), quarter),
                    which,
                    step,
                )
        for which in (0, 1):
            on_across(which, 3, 1)
            on_across(which, 3, -1)

    def other_hops():
        for which in (0, 1):
            on_across(which, 1, 1)
            on_across(which, 1, -1)

    def far_hops():
        for half in (1, -1):
            for which in (0, 1):
                net.need(("fp", which, half))
                for step in (1, -1):
                    net.start(
                        ("pq2", which, half, step),
                        block(which, 2, 0, at_of(half), quarter),
                        block(which, 2, (-step) % SIDE, at_of(half), quarter),
                        1 - which,
                        step,
                    )

    def second_hops(dp):
        for step in (1, -1):
            for which in (0, 1):
                if dp == 0:
                    net.need(("oq", which, step))
                elif dp == 2:
                    net.need(("pq2", which, step, step))
                else:
                    net.need(("pq", which, dp, step))
                net.start(
                    ("fq", which, dp, step),
                    block(which, dp, (-step) % SIDE, at_of(step), quarter),
                    block(which, dp, 2, at_of(step), quarter),
                    1 - which,
                    step,
                )

    def arrived(blocks):
        for dx, dz in blocks:
            for which in (0, 1):
                dp, dq = (dx, dz) if which == 0 else (dz, dx)
                step = {1: -1, 3: 1}
                if dq == 0:
                    if dp in step:
                        net.need(("op", which, step[dp]))
                    elif dp == 2:
                        net.need(("fp", which, 1), ("fp", which, -1))
                elif dq == 2:
                    net.need(("fq", which, dp, 1), ("fq", which, dp, -1))
                elif dp == 0:
                    net.need(("oq", which, step[dq]))
                elif dp == 2:
                    net.need(("pq2", which, 1, step[dq]), ("pq2", which, -1, step[dq]))
                else:
                    net.need(("pq", which, dp, step[dq]))

    groups = (
        ((0, 0), (1, 0), (3, 0), (0, 1)),
        ((0, 3), (0, 2), (2, 0), (3, 3)),
        ((1, 1), (1, 3), (3, 1), (3, 2)),
        ((2, 3), (1, 2), (2, 1), (2, 2)),
    )

    def stage(at):
        if at == 0:
            first_hops()
            second_hops(0)
            other_hops()
            load_gate_up.wait()
            load_down.wait()
        elif at == 1:
            far_hops()
            second_hops(3)
        elif at == 2:
            second_hops(1)
            second_hops(2)
            back(0)
        else:
            relay(0)
        arrived(groups[at])

    def relay(dp, pieces=1):
        size = half_rows // pieces
        for which in (0, 1):
            for side, step in ((0, 1), (1, -1)):
                net.need(("rh", which, dp, step))
                there = part(which, dp, step % SIDE, at_of(step), quarter)
                add_rows(there(), there(), half_in.at[which, dp, side])
                for piece in range(pieces):
                    rows = slice(piece * size, (piece + 1) * size)
                    net.start(
                        ("rf", which, dp, step, piece),
                        part(which, dp, step % SIDE, piece * size, size),
                        view(full_in, which, dp, side, rows),
                        1 - which,
                        step,
                    )

    def back(dp):
        for which in (0, 1):
            for side, step in ((0, 1), (1, -1)):
                net.start(
                    ("rh", which, dp, step),
                    part(which, dp, 2, at_of(step), quarter),
                    view(half_in, which, dp, side),
                    1 - which,
                    step,
                )

    before = lax.broadcasted_iota(jnp.int32, (128, 128), 0)
    after = lax.broadcasted_iota(jnp.int32, (128, 128), 1)
    earlier = jnp.where(before < after, 1.0, 0.0).astype(BF16)
    slot = lax.broadcasted_iota(jnp.int32, (slots, 128), 0).astype(F32)

    pair = lax.axis_index("expert") // 2
    at_pair = lax.broadcasted_iota(jnp.int32, (1, 8), 1) == pair
    mine = jnp.sum(jnp.where(at_pair, holders_ref[...], 0), axis=1, keepdims=True)
    chosen = jnp.where(lax.broadcasted_iota(jnp.int32, (8, 128), 0) == mine, 1.0, 0.0)

    def group(g, carry):
        for at in range(SIDE):
            pl.when(g == at)(functools.partial(stage, at))
        places = [[of_four(g, [group[k][axis] for group in groups]) for axis in (0, 1)] for k in range(SIDE)]
        scales = []
        for k, (dx, dz) in enumerate(places):
            table = meta_ref[dz, dx]
            member = jnp.sum(table[0:8] * chosen, axis=0, keepdims=True)
            weight = jnp.sum(table[8:16] * chosen, axis=0, keepdims=True)
            wide = jnp.broadcast_to(member, (16, 128)).astype(BF16)
            rank = jnp.dot(wide, earlier, preferred_element_type=F32)[0:1]
            hit = (slot == rank) & (member > 0.5)
            pick = jnp.where(hit, 1.0, 0.0).astype(BF16)
            scales.append(jnp.sum(jnp.where(hit, weight, 0.0), axis=1, keepdims=True))
            picks[k] = pick
            for at, size in chunks(width, 1024):
                packed[k * slots : (k + 1) * slots, at : at + size] = jnp.dot(
                    pick, tokens[dx, dz, :, at : at + size], preferred_element_type=F32
                ).astype(BF16)
        scale = jnp.concatenate(scales, axis=0)
        for at, size in chunks(inner, 256):
            gate = across(packed[...], gate_up[at : at + size])
            up = across(packed[...], gate_up[inner + at : inner + at + size])
            act[:, at : at + size] = (
                (up + 1.0) * gate * jax.nn.sigmoid(1.702 * gate)
            ).astype(BF16)
        for at, size in chunks(width, 640):
            tile = jnp.dot(act[...], down[:, at : at + size], preferred_element_type=F32)
            tile = (tile * scale).astype(BF16)
            for k, (dx, dz) in enumerate(places):
                parts[dx, dz, :, at : at + size] = along(
                    picks[k], tile[k * slots : (k + 1) * slots]
                ).astype(BF16)
        return carry

    lax.fori_loop(0, SIDE, group, 0)

    for dp in (2, 1, 3):
        back(dp)

    def gather_in(which, dp, piece=0, pieces=1):
        size = half_rows // pieces
        rows = slice(piece * size, (piece + 1) * size)
        net.need(("rf", which, dp, 1, piece), ("rf", which, dp, -1, piece))
        here = part(which, dp, 0, piece * size, size)
        add_rows(here(), here(), full_in.at[which, dp, 0, rows], full_in.at[which, dp, 1, rows])

    def last_half(which):
        for side, step in ((0, 1), (1, -1)):
            net.start(
                ("lh", which, step),
                part(which, 2, 0, at_of(step), quarter),
                view(half_last, which, side),
                which,
                step,
            )

    ends = ((0, quarter), (quarter, quarter // 2), (quarter * 3 // 2, quarter // 2))

    def last_full(which, step, at, size):
        side = (1 - step) // 2
        if at == at_of(step):
            there = part(which, step % SIDE, 0, at, quarter)
            net.need(("lh", which, step))
            add_rows(there(), there(), half_last.at[which, side])
        net.start(
            ("lf", which, step, at),
            part(which, step % SIDE, 0, at, size),
            view(full_last, which, side, slice(at, at + size)),
            which,
            step,
        )

    relay(2)
    relay(1)
    for which in (0, 1):
        gather_in(which, 2)
        last_half(which)
    relay(3, 2)
    for which in (0, 1):
        gather_in(which, 1)
        for at, size in ends:
            last_full(which, 1, at, size)
    for piece in (0, 1):
        for which in (0, 1):
            gather_in(which, 3, piece, 2)
            for at, size in ends:
                if at // quarter == piece:
                    last_full(which, -1, at, size)
    for which in (0, 1):
        net.need(("rf", which, 0, 1, 0), ("rf", which, 0, -1, 0))
    for at, size in ends:
        for which in (0, 1):
            net.need(("lf", which, 1, at), ("lf", which, -1, at))
            here = part(which, 0, 0, at, size)
            inside = slice(at, at + size)
            rows = slice(which * half_rows + at, which * half_rows + at + size)
            add_rows(
                here(),
                here(),
                full_in.at[which, 0, 0, inside],
                full_in.at[which, 0, 1, inside],
                full_last.at[which, 0, inside],
                full_last.at[which, 1, inside],
                residual_ref.at[rows],
            )
            net.start(("out", which, at), here, view(out_ref, rows), 2, 1)
    net.finish()


def experts_and_pass(normed_mid, residual, meta, holders, gate_up, down, slots):
    rows, width = normed_mid.shape
    inner = down.shape[0]
    anywhere = pl.BlockSpec(memory_space=pl.ANY)
    vmem = pl.BlockSpec(memory_space=pltpu.VMEM)
    half, quarter = rows // 2, rows // 4
    return pl.pallas_call(
        functools.partial(expert_kernel, slots),
        out_shape=jax.ShapeDtypeStruct((rows, width), BF16),
        in_specs=[anywhere, vmem, vmem, vmem, anywhere, anywhere],
        out_specs=anywhere,
        scratch_shapes=[
            pltpu.VMEM((SIDE, SIDE, rows, width), BF16),
            pltpu.VMEM((SIDE, SIDE, rows, width), BF16),
            pltpu.VMEM(gate_up.shape, BF16),
            pltpu.VMEM(down.shape, BF16),
            pltpu.VMEM((SIDE * slots, width), BF16),
            pltpu.VMEM((SIDE * slots, inner), BF16),
            pltpu.VMEM((SIDE, slots, rows), BF16),
            pltpu.VMEM((2, SIDE, 2, quarter, width), BF16),
            pltpu.VMEM((2, SIDE, 2, half, width), BF16),
            pltpu.VMEM((2, 2, quarter, width), BF16),
            pltpu.VMEM((2, 2, half, width), BF16),
            pltpu.SemaphoreType.DMA((3,)),
            pltpu.SemaphoreType.DMA((112,)),
            pltpu.SemaphoreType.DMA((112,)),
        ],
        compiler_params=pltpu.CompilerParams(
            collective_id=1, has_side_effects=True, vmem_limit_bytes=62 * 1024 * 1024
        ),
        cost_estimate=pl.CostEstimate(
            flops=16_000_000_000, bytes_accessed=16_000_000, transcendentals=1_000_000
        ),
    )(normed_mid, residual, meta, holders, gate_up, down)


def routing_tables(ids, logits):
    kinds = lax.broadcasted_iota(jnp.int32, (8, ids.shape[1]), 0)
    grown = jnp.exp(logits - jnp.max(logits, axis=0, keepdims=True))
    weights = grown / jnp.sum(grown, axis=0, keepdims=True)
    member, weight = jnp.zeros(kinds.shape, F32), jnp.zeros(kinds.shape, F32)
    for k in range(TOP):
        equal = kinds == ids[k : k + 1]
        member = member + jnp.where(equal, 1.0, 0.0)
        weight = weight + jnp.where(equal, weights[k : k + 1], 0.0)
    return member, weight


def attend(pairs, projected, behind, sinks_ref, attended, first):
    rows = projected.shape[0]
    pair = 2 * HEAD_DIM
    group = QUERY_HEADS // KEY_VALUE_HEADS
    row = lax.broadcasted_iota(jnp.int32, (rows, rows), 0)
    lane = lax.broadcasted_iota(jnp.int32, (rows, rows), 1)
    low = lax.broadcasted_iota(jnp.int32, (rows, pair), 1) < HEAD_DIM
    older = row > lane
    scale = jnp.where(first, 0.0, 0.125)
    offset = jnp.where(first, -1e30, 0.0)
    keys_at = QUERY_HEADS * HEAD_DIM
    values_at = keys_at + KEY_VALUE_HEADS * HEAD_DIM
    for g in sorted({head // group for head in pairs}):
        tile = g // 2 * pair
        stacked = []
        own = projected[:, keys_at + tile : keys_at + tile + pair].astype(F32)
        rim = behind[:, tile : tile + pair].astype(F32)
        for side in (0, 1):
            for keys in (rim, own):
                placed = keys if g % 2 == side else pltpu.roll(keys, HEAD_DIM, 1)
                stacked.append(jnp.where(low if side == 0 else ~low, placed, 0.0).astype(BF16))
        keys = jnp.concatenate(stacked, axis=0)
        at = values_at + tile
        values = jnp.concatenate(
            [
                behind[:, KEY_VALUE_HEADS * HEAD_DIM + tile : KEY_VALUE_HEADS * HEAD_DIM + tile + pair],
                projected[:, at : at + pair],
            ],
            axis=0,
        ).astype(F32)
        values = values.T[g % 2 * HEAD_DIM : (g % 2 + 1) * HEAD_DIM].astype(BF16)
        for head in [head for head in pairs if head // group == g]:
            scores = across(keys, projected[:, head * HEAD_DIM : head * HEAD_DIM + pair])
            for side in (0, 1):
                past = scores[2 * side * rows : (2 * side + 1) * rows]
                here = scores[(2 * side + 1) * rows : (2 * side + 2) * rows]
                merged = jnp.where(older, past * scale + offset, here * 0.125)
                sink = sinks_ref[0, head + side]
                peak = jnp.maximum(jnp.max(merged, axis=0, keepdims=True), sink)
                numer = jnp.exp(merged - peak)
                denominator = jnp.sum(numer, axis=0, keepdims=True) + jnp.exp(sink - peak)
                share = numer * (1.0 / denominator)
                both = jnp.concatenate(
                    [jnp.where(older, share, 0.0), jnp.where(older, 0.0, share)], axis=0
                ).astype(BF16)
                attended[(head + side) * HEAD_DIM : (head + side + 1) * HEAD_DIM] = jnp.dot(
                    values, both, preferred_element_type=F32
                ).astype(BF16)


def project_kernel(
    state_ref,
    gain_ref,
    weight_hbm,
    bias_ref,
    ids_ref,
    logits_ref,
    sinks_ref,
    out_weight_hbm,
    out_bias_ref,
    mid_gain_ref,
    normed_ref,
    residual_ref,
    tables_ref,
    projected_ref,
    scaled,
    tokens_ref,
    out_weight,
    attended,
    weight,
    slices,
    transit,
    total,
    sent,
    half_in,
    full_in,
    behind,
    tables,
    local_sem,
    send_sem,
    recv_sem,
):
    net = Links(send_sem, recv_sem)
    columns = weight.shape[4]
    rows = normed_ref.shape[0]
    cuts = (384, 256)

    def column_at(which, chunk):
        return columns * (chunk if which == 0 else 3 - chunk)

    loads = {
        (which, chunk): pltpu.make_async_copy(
            weight_hbm.at[:, pl.ds(column_at(which, chunk), columns)],
            weight.at[which, chunk, 0],
            local_sem.at[5 + 2 * which + chunk],
        )
        for chunk in (0, 1)
        for which in (0, 1)
    }
    for load in loads.values():
        load.start()
    load_out = pltpu.make_async_copy(out_weight_hbm, out_weight, local_sem.at[4])
    load_out.start()
    member, gate_weight = routing_tables(ids_ref[...], logits_ref[...])
    tables[0, 0, 0:8] = member
    tables[0, 0, 8:16] = gate_weight
    place = (net.x, net.z)
    features = state_ref.shape[0]

    def for_device(which, step, at, size):
        to = (place[1 - which] + step + SIDE) % SIDE
        pieces = slice(at, at + size)
        if which == 0:
            return lambda: tokens_ref.at[pieces, to]
        return lambda: tokens_ref.at[to, pieces]

    def kept(which, dq, at, size):
        lanes = slice(dq * rows, (dq + 1) * rows)
        pieces = slice(at, at + size)
        return lambda: slices.at[which, pieces, :, lanes]

    net.barrier([(0, 1), (0, -1), (1, 1), (1, -1), (3, 1), (3, -1)])
    steps = ((0, 1), (1, -1))
    net.start(("mx", 1), view(tables, 0, 0), view(tables, 0, 3), 0, 1)
    net.start(("mx", -1), view(tables, 0, 0), view(tables, 0, 1), 0, -1)

    def offer(which, chunk):
        loads[which, chunk].wait()
        for side, step in steps:
            net.start(
                ("wo", which, chunk, step),
                view(weight, which, chunk, 0),
                view(weight, which, chunk, (-step) % SIDE),
                which,
                step,
            )

    for which in (0, 1):
        offer(which, 0)
    squares = jnp.zeros((1, rows), F32)
    for at, size in chunks(features, 640):
        part = state_ref[at : at + size].astype(F32)
        squares = squares + jnp.sum(part * part, axis=0, keepdims=True)
    inverse = lax.rsqrt(squares / features + 1e-05)
    for at, size in chunks(features, 640):
        gain = jnp.broadcast_to(gain_ref[:, at : at + size], (rows, size)).T
        scaled[at : at + size] = state_ref[at : at + size].astype(F32) * inverse * gain
    depth = tokens_ref.shape[2]
    for a in range(SIDE):
        for b in range(SIDE):
            at = (a * SIDE + b) * depth
            tokens_ref[a, b] = scaled[at : at + depth].astype(BF16)
    stays = [
        pltpu.make_async_copy(
            for_device(which, 0, 0, SIDE)(), kept(which, 0, 0, SIDE)(), local_sem.at[2 + which]
        )
        for which in (0, 1)
    ]
    for stay in stays:
        stay.start()
    for which in (0, 1):
        for side, step in steps:
            net.start(
                ("tt", which, step),
                for_device(which, 2, side * 2, 2),
                view(transit, which, side),
                1 - which,
                step,
            )
    for which in (0, 1):
        for side, step in steps:
            net.start(
                ("ta", which, step),
                for_device(which, step, 0, SIDE),
                kept(which, (-step) % SIDE, 0, SIDE),
                1 - which,
                step,
            )
    def pass_on(which, chunk, step):
        net.need(("wo", which, chunk, step))
        part = slice(0, cuts[chunk]) if step == 1 else slice(cuts[chunk], columns)
        every = slice(None)
        net.start(
            ("wf", which, chunk, step),
            view(weight, which, chunk, (-step) % SIDE, every, part),
            view(weight, which, chunk, 2, every, part),
            which,
            step,
        )

    def multiply(which, chunk, dp):
        piece = (place[which] + dp) % SIDE
        term = along(slices[which, piece], weight[which, chunk, dp])
        if dp == 0:
            total[which, chunk] = term
        else:
            total[which, chunk] += term

    def half_of(side):
        return slice(side * rows // 2, (side + 1) * rows // 2)

    def sums_out(which, chunk):
        net.need(("wf", which, chunk, 1), ("wf", which, chunk, -1))
        multiply(which, chunk, 2)
        sent[which, chunk, 2] = total[which, chunk, 2 * rows : 3 * rows].astype(BF16)
        for side, step in steps:
            net.start(
                ("rh", which, chunk, step),
                view(sent, which, chunk, 2, half_of(side)),
                view(half_in, which, chunk, side),
                1 - which,
                step,
            )

    def sums_on(which, chunk):
        for side, step in steps:
            dq = step % SIDE
            other = half_of(1 - side)
            sent[which, chunk, dq, other] = total[
                which, chunk, dq * rows + other.start : dq * rows + other.stop
            ].astype(BF16)
            net.need(("rh", which, chunk, step))
            part = half_of(side)
            sent[which, chunk, dq, part] = (
                total[which, chunk, dq * rows + part.start : dq * rows + part.stop]
                + half_in[which, chunk, side].astype(F32)
            ).astype(BF16)
            net.start(
                ("rf", which, chunk, step),
                view(sent, which, chunk, dq),
                view(full_in, which, chunk, side),
                1 - which,
                step,
            )

    def sums_in(which, chunk):
        net.need(("rf", which, chunk, 1), ("rf", which, chunk, -1))
        lanes = slice(column_at(which, chunk), column_at(which, chunk) + columns)
        projected_ref[:, lanes] = (
            total[which, chunk, 0:rows]
            + full_in[which, chunk, 0].astype(F32)
            + full_in[which, chunk, 1].astype(F32)
            + bias_ref[:, lanes]
        ).astype(BF16)

    for step in (1, -1):
        for which in (0, 1):
            pass_on(which, 0, step)
    for which in (0, 1):
        for side, step in steps:
            net.need(("tt", which, step))
            net.start(
                ("tf", which, step),
                view(transit, which, side),
                kept(which, 2, side * 2, 2),
                1 - which,
                step,
            )
    for which in (0, 1):
        offer(which, 1)
    net.need(("mx", 1))
    net.start(("mf", 0), view(tables, 0, 3), view(tables, 0, 2), 0, 1)
    for which in (0, 1):
        stays[which].wait()
        net.need(("ta", which, 1), ("ta", which, -1), ("tf", which, 1), ("tf", which, -1))
    for which in (1, 0):
        for dp in (0, 3, 1):
            multiply(which, 0, dp)
    for which in (1, 0):
        sums_out(which, 0)
    for step in (1, -1):
        for which in (0, 1):
            pass_on(which, 1, step)
    net.need(("mx", -1), ("mf", 0))
    net.start(("mz", 1), view(tables, 0), view(tables, 3), 1, 1)
    net.start(("mz", -1), view(tables, 0), view(tables, 1), 1, -1)
    for which in (1, 0):
        sums_on(which, 0)
    for which in (1, 0):
        for dp in (0, 3, 1):
            multiply(which, 1, dp)
    for which in (1, 0):
        sums_out(which, 1)
    net.need(("mz", 1), ("mz", -1))
    net.start(("mg", 0), view(tables, 3), view(tables, 2), 1, 1)
    sums_in(1, 0)
    keys = slice(4 * columns - behind.shape[1], 4 * columns)
    net.start(("kv", 0), view(projected_ref, slice(None), keys), view(behind), 3, 1)
    for which in (1, 0):
        sums_on(which, 1)
    sums_in(0, 0)
    first = net.x * SIDE + net.z == 0
    net.need(("kv", 0))
    early = (0, 2, 4, 6, 8, 30)
    attend(early, projected_ref, behind, sinks_ref, attended, first)
    known = 8 * HEAD_DIM
    load_out.wait()
    for at, size in chunks(features, 640):
        lanes = slice(at, at + size)
        scaled[lanes] = state_ref[lanes].astype(F32) + jnp.dot(
            out_weight[lanes, :known], attended[:known], preferred_element_type=F32
        )
    for which in (1, 0):
        sums_in(which, 1)
    net.finish()
    tables_ref[...] = tables[...]
    late = [head for head in range(0, QUERY_HEADS, 2) if head not in early]
    attend(late, projected_ref, behind, sinks_ref, attended, first)
    squares = jnp.zeros((rows, 1), F32)
    for at, size in chunks(features, 640):
        lanes = slice(at, at + size)
        mixed = scaled[lanes] + jnp.dot(
            out_weight[lanes, known:], attended[known:], preferred_element_type=F32
        )
        kept_sum = (mixed.T + out_bias_ref[:, lanes]).astype(BF16)
        residual_ref[:, lanes] = kept_sum
        wide = kept_sum.astype(F32)
        squares = squares + jnp.sum(wide * wide, axis=1, keepdims=True)
    inverse = lax.rsqrt(squares / features + 1e-05)
    for at, size in chunks(features, 640):
        lanes = slice(at, at + size)
        wide = residual_ref[:, lanes].astype(F32)
        normed_ref[:, lanes] = (wide * inverse * mid_gain_ref[:, lanes]).astype(BF16)


def attention_part(state, gain, weight, bias, ids, logits, sinks, out_weight, out_bias, mid_gain):
    features, rows = state.shape
    depth = weight.shape[0]
    wide = weight.shape[1]
    columns = wide // 4
    keys = 2 * KEY_VALUE_HEADS * HEAD_DIM
    anywhere = pl.BlockSpec(memory_space=pl.ANY)
    vmem = pl.BlockSpec(memory_space=pltpu.VMEM)
    return pl.pallas_call(
        project_kernel,
        out_shape=(
            jax.ShapeDtypeStruct((rows, features), BF16),
            jax.ShapeDtypeStruct((rows, features), BF16),
            jax.ShapeDtypeStruct((SIDE, SIDE, 16, rows), F32),
        ),
        in_specs=[
            vmem,
            vmem,
            anywhere,
            vmem,
            vmem,
            vmem,
            pl.BlockSpec(memory_space=pltpu.SMEM),
            anywhere,
            vmem,
            vmem,
        ],
        out_specs=(vmem, vmem, vmem),
        scratch_shapes=[
            pltpu.VMEM((rows, wide), BF16),
            pltpu.VMEM((features, rows), F32),
            pltpu.VMEM((SIDE, SIDE, depth, rows), BF16),
            pltpu.VMEM(out_weight.shape, BF16),
            pltpu.VMEM((QUERY_HEADS * HEAD_DIM, rows), BF16),
            pltpu.VMEM((2, 2, SIDE, depth, columns), BF16),
            pltpu.VMEM((2, SIDE, depth, SIDE * rows), BF16),
            pltpu.VMEM((2, 2, 2, depth, rows), BF16),
            pltpu.VMEM((2, 2, SIDE * rows, columns), F32),
            pltpu.VMEM((2, 2, SIDE, rows, columns), BF16),
            pltpu.VMEM((2, 2, 2, rows // 2, columns), BF16),
            pltpu.VMEM((2, 2, 2, rows, columns), BF16),
            pltpu.VMEM((rows, keys), BF16),
            pltpu.VMEM((SIDE, SIDE, 16, rows), F32),
            pltpu.SemaphoreType.DMA((9,)),
            pltpu.SemaphoreType.DMA((64,)),
            pltpu.SemaphoreType.DMA((64,)),
        ],
        compiler_params=pltpu.CompilerParams(
            collective_id=2, has_side_effects=True, vmem_limit_bytes=56 * 1024 * 1024
        ),
        cost_estimate=pl.CostEstimate(
            flops=2_000_000_000, bytes_accessed=4_000_000, transcendentals=0
        ),
    )(state, gain, weight, bias, ids, logits, sinks, out_weight, out_bias, mid_gain)


def shards(
    section_input,
    attention_gain,
    query_key_value_weight,
    qkv_bias,
    out_weight,
    out_bias,
    attention_sink_logits,
    expert_gain,
    gate_up_weight,
    down_weight,
    expert_ids,
    gate_logits,
    placement,
):
    rows = section_input.shape[1]
    experts = placement.shape[1]
    slots = 2 * min(rows // 2, rows * TOP * 5 // (8 * experts))
    normed_mid, residual, tables = attention_part(
        section_input[0].T,
        attention_gain,
        query_key_value_weight[0],
        qkv_bias,
        expert_ids[0].T,
        gate_logits[0].T,
        attention_sink_logits,
        out_weight[0].T,
        out_bias,
        expert_gain,
    )
    moved = experts_and_pass(
        normed_mid, residual, tables, placement, gate_up_weight[0, 0].T, down_weight[0, 0], slots
    )
    return moved[None]


def solution(mesh):
    return jax.shard_map(
        shards,
        mesh=mesh,
        in_specs=(
            P("section", "expert", None),
            P("section", None),
            P("section", "expert", None),
            P("section", None),
            P("section", None, None),
            P("section", None),
            P("section", None),
            P("section", None),
            P("section", "expert", None, None),
            P("section", "expert", None, None),
            P("section", "expert", None),
            P("section", "expert", None),
            P("section", None),
        ),
        out_specs=P("section", "expert", None),
        check_vma=False,
    )
```
